32 devices in a mesh: gz: 8 (over y, x, core), xy: 4 (over z).
Axes of the slice: x: 2, y: 2, z: 4, core: 2. Of those that a mesh axis runs over, the one named last changes fastest.
Arguments:
- east_velocity: float32 [512, 64, 512], P('xy', 'gz'), may hold values from -6 to 6
- north_velocity: float32 [512, 64, 512], P('xy', 'gz'), may hold values from -6 to 6
- upward_velocity: float32 [512, 64, 512], P('xy', 'gz'), may hold values from -5 to 5
- obstacle: int32 [512, 64, 512], P('xy', 'gz'), may hold values 0 or 1
Outputs:
- east_corrected: float32 [512, 64, 512], P('xy', 'gz')
- north_corrected: float32 [512, 64, 512], P('xy', 'gz')
- upward_corrected: float32 [512, 64, 512], P('xy', 'gz')
- pressure: float32 [512, 64, 512], P('xy', 'gz')
- residual: float32 [512, 64, 512], P('xy', 'gz')
The draws below stay inside these ranges and needn't reach their ends.
All inputs are finite; a program needn't handle non-finite values. No bound on the sum of `obstacle` on one device may be relied on, other than what follows from the above.
Results may differ from the reference program's by a relative error of at most 0.0003.
Values sent between devices are 32-bit elements; how exact they have to be, the bound alone decides.
No kernel may reach another device: no remote copies, remote signals or barrier semaphores. Data moves between devices by JAX's collectives and lax.ppermute only.
A program may use at most 128 MiB of HBM per device.

```python
import jax
import jax.numpy as jnp
from jax import lax

NX = 512
NY = 512
NZ = 64


def draw_upward_velocity(key, part):
    base = jnp.clip(jax.random.normal(jax.random.fold_in(key, 17), (NX, NZ, NY), jnp.float32), -5.0, 5.0)
    return base


def plant(drawn, own_key, smallest, top_value):
    dims = drawn.shape
    spot = [jax.random.randint(jax.random.fold_in(own_key, axis), (), 0, dims[axis]) for axis in range(len(dims))]
    drawn = drawn.at[tuple(spot)].set(smallest)
    longest = dims.index(max(dims))
    spot[longest] = (spot[longest] + 1) % dims[longest]
    return drawn.at[tuple(spot)].set(top_value)


def block_scale(rng, shape, split, least, high):
    def one(dim, blocks):
        draws = jax.random.uniform(jax.random.fold_in(jax.random.fold_in(rng, 6), dim), (blocks,), jnp.float32, least / len(split), high / len(split))
        return jnp.repeat(jnp.exp(draws), shape[dim] // blocks).reshape((-1,) + (1,) * (len(shape) - dim - 1))

    level = one(*split[0])
    for cut in split[1:]:
        level = level * one(*cut)
    return level


def noise(key, dims, width, reach, pieces=(), kind=jnp.bfloat16):
    values = width * jax.random.normal(key, dims, jnp.float32)
    if pieces:
        values = values * block_scale(key, dims, pieces, -0.22, 0.18)
    return jnp.clip(values, -reach, reach).astype(kind)


def setup_inputs(seed: int = 0) -> dict:
    key_list = jax.random.split(jax.random.key(seed), 5)
    return {
        "east_velocity": noise(key_list[0], (NX, NZ, NY), 1.0, 6.0, ((0, 4), (1, 8)), jnp.float32),
        "north_velocity": noise(key_list[1], (NX, NZ, NY), 1.0, 6.0, ((0, 4), (1, 8)), jnp.float32),
        "upward_velocity": draw_upward_velocity(jax.random.fold_in(key_list[4], 71), 0),
        "obstacle": plant((jax.random.randint(key_list[3], (NX, NZ, NY), 0, 6) < 1).astype(jnp.int32), jax.random.fold_in(key_list[3], 1), 0, 1),
    }


HIGH = lax.Precision.HIGHEST


def hartley(length):
    index = jnp.arange(length, dtype=jnp.int32)
    product = (index[:, None] * index[None, :]) % length
    angle = (2.0 * jnp.pi / length) * product.astype(jnp.float32)
    return jnp.cos(angle) + jnp.sin(angle)


def eigenvalues(length):
    index = jnp.arange(length, dtype=jnp.int32).astype(jnp.float32)
    return 2.0 - 2.0 * jnp.cos((2.0 * jnp.pi / length) * index)


def tridiagonal(diagonal, right):
    start = jnp.zeros_like(right[0])

    def forward(carry, plane):
        ratio, value = carry
        divisor = diagonal + ratio
        ratio_new = -1.0 / divisor
        value_new = (plane + value) / divisor
        return (ratio_new, value_new), (ratio_new, value_new)

    _, (ratios, values) = lax.scan(forward, (start, start), right)

    def backward(after, pair):
        ratio, value = pair
        solution = value - ratio * after
        return solution, solution

    _, solved = lax.scan(backward, start, (ratios, values), reverse=True)
    return solved


def reference(east_velocity, north_velocity, upward_velocity, obstacle):
    fluid = (1 - obstacle).astype(jnp.float32)
    ones_plane = jnp.ones((NX, 1, NY), jnp.float32)
    zero_plane = jnp.zeros((NX, 1, NY), jnp.float32)
    open_east = fluid * jnp.roll(fluid, 1, 0)
    open_north = fluid * jnp.roll(fluid, 1, 2)
    open_up = fluid * jnp.concatenate([ones_plane, fluid[:, :-1]], 1)
    east_masked = open_east * east_velocity
    north_masked = open_north * north_velocity
    upward_masked = open_up * upward_velocity
    east_after = jnp.roll(east_masked, -1, 0)
    upward_after = jnp.concatenate([upward_masked[:, 1:], zero_plane], 1)
    source = (east_masked - east_after) + (north_masked - jnp.roll(north_masked, -1, 2)) + (upward_masked - upward_after)
    table_east = hartley(NX)
    table_north = hartley(NY)
    partial_modes = jnp.einsum("xzy,ky->xzk", source, table_north, precision=HIGH)
    spectrum = jnp.einsum("xzk,xa->zka", partial_modes, table_east, precision=HIGH)
    diagonal = 2.0 + eigenvalues(NY)[:, None] + eigenvalues(NX)[None, :]
    modes = tridiagonal(diagonal, spectrum)
    half_back = jnp.einsum("zka,xa->xzk", modes, table_east, precision=HIGH)
    pressure = jnp.einsum("xzk,yk->xzy", half_back, table_north, precision=HIGH) * (1.0 / (NX * NY))
    west_full = jnp.roll(pressure, 1, 0)
    east_full = jnp.roll(pressure, -1, 0)
    below_full = jnp.concatenate([zero_plane, pressure[:, :-1]], 1)
    above_full = jnp.concatenate([pressure[:, 1:], zero_plane], 1)
    open_east_after = jnp.roll(open_east, -1, 0)
    open_north_after = jnp.roll(open_north, -1, 2)
    open_up_after = jnp.concatenate([open_up[:, 1:], zero_plane], 1)
    applied = (open_east * (pressure - west_full) + open_east_after * (pressure - east_full)
               + open_north * (pressure - jnp.roll(pressure, 1, 2)) + open_north_after * (pressure - jnp.roll(pressure, -1, 2))
               + open_up * (pressure - below_full) + open_up_after * (pressure - above_full))
    residual = source - applied
    east_corrected = open_east * (east_velocity - (pressure - west_full))
    north_corrected = open_north * (north_velocity - (pressure - jnp.roll(pressure, 1, 2)))
    upward_corrected = open_up * (upward_velocity - (pressure - below_full))
    return east_corrected, north_corrected, upward_corrected, pressure, residual
```

```python
import functools

import jax
import jax.numpy as jnp
import ml_dtypes
import numpy as np
from jax import lax
from jax.experimental import pallas as pl
from jax.experimental.pallas import tpu as pltpu
from jax.sharding import PartitionSpec as P

F32 = jnp.float32
BF16 = jnp.bfloat16
VMEM_LIMIT = 60 * 1024 * 1024


def pair_np(table):
    high = table.astype(np.float32).astype(ml_dtypes.bfloat16)
    low = (table - high.astype(np.float64)).astype(np.float32).astype(ml_dtypes.bfloat16)
    return high, low


def north_tables(length):
    half = length // 2
    cell = np.arange(half)[:, None]
    mode = np.arange(half)[None, :]

    def cas(number):
        angle = 2.0 * np.pi * ((cell * number) % length) / length
        return (np.cos(angle) + np.sin(angle)) / np.sqrt(length)

    numbers = np.concatenate([2 * np.arange(half), 2 * np.arange(half) + 1])
    eigen = 4.0 * np.sin(np.pi * numbers / length) ** 2
    return cas(2 * mode), cas(2 * mode + 1), eigen


def east_tables(length):
    modes = np.concatenate([np.arange(0, length, 2), np.arange(1, length, 2)])
    cell = np.arange(length)
    table = np.cos(np.pi * modes[:, None] * (2 * cell[None, :] + 1) / (2 * length)) * np.sqrt(2.0 / length)
    table[0] = np.sqrt(1.0 / length)
    eigen = 4.0 * np.sin(np.pi * modes / (2 * length)) ** 2
    return table, eigen


def sine_table(length):
    index = np.arange(1, length + 1)
    table = np.sqrt(2.0 / (length + 1)) * np.sin(np.pi * np.outer(index, index) / (length + 1))
    eigen = 4.0 * np.sin(np.pi * index / (2 * (length + 1))) ** 2
    return table, eigen


def split(value):
    high = value.astype(BF16)
    return high, (value - high.astype(F32)).astype(BF16)


def dot3(left, right):
    (lh, ll), (rh, rl) = left, right
    dot = functools.partial(jnp.dot, preferred_element_type=F32)
    return dot(lh, rh) + (dot(ll, rh) + dot(lh, rl))


def chebyshev(shift, count):
    values = [jnp.ones_like(shift)]
    step = values[0]
    for n in range(count):
        step = step + shift * values[n]
        values.append(values[n] + step)
    return values


def slab_solve(shift, right):
    count = len(right)
    u = chebyshev(shift, count)
    inverse = 1.0 / u[count]
    lower = [right[0]]
    for k in range(1, count):
        lower.append(lower[-1] + u[k] * right[k])
    upper = [None] * count
    for k in range(count - 2, -1, -1):
        term = u[count - 2 - k] * right[k + 1] if k < count - 2 else right[k + 1]
        upper[k] = term if upper[k + 1] is None else upper[k + 1] + term
    out = []
    for k in range(count):
        value = u[count - 1 - k] * lower[k]
        if upper[k] is not None:
            value = value + u[k] * upper[k]
        out.append(value * inverse)
    return out


def spike_of(shift, count):
    u = chebyshev(shift, count)
    inverse = 1.0 / u[count]
    return [u[count - 1 - k] * inverse for k in range(count)]


def interface_chain(couple, spread, bottoms, tops):
    count = len(bottoms)
    slope = jnp.zeros_like(couple)
    offset = jnp.zeros_like(couple)
    slopes, offsets, inverses, bases = [], [], [], []
    for s in range(count):
        inverse = 1.0 / (1.0 - couple * slope)
        base = (bottoms[s] + couple * offset) * inverse
        slopes.append(slope)
        offsets.append(offset)
        inverses.append(inverse * spread)
        bases.append(base)
        if s < count - 1:
            weight = spread * slope
            slope, offset = (
                couple + weight * spread * inverse,
                tops[s] + spread * offset + weight * base,
            )
    above = jnp.zeros_like(couple)
    lowers, uppers = [None] * count, [None] * count
    for s in range(count - 1, -1, -1):
        lower = bases[s] + inverses[s] * above
        uppers[s] = tops[s] + spread * (slopes[s] * lower + offsets[s]) + couple * above
        lowers[s] = lower
        above = lower
    below = [jnp.zeros_like(couple)] + uppers[:-1]
    above = lowers[1:] + [jnp.zeros_like(couple)]
    return below, above


def get_lanes(ref, rows):
    return jnp.concatenate([ref[n, rows, :] for n in range(ref.shape[0])], 1)


def put_lanes(ref, rows, value, start):
    for n in range(value.shape[1] // 128):
        ref[start + n, rows, :] = value[:, n * 128 : (n + 1) * 128]


def first_rows(nz, obs, up, ftop, fbot, gbot):
    rows = ftop.shape[0]
    ftop[...] = (1 - obs[pl.ds(nz - 1, rows, stride=nz), :]).astype(F32)
    low = (1 - obs[pl.ds(0, rows, stride=nz), :]).astype(F32)
    fbot[...] = low
    gbot[...] = low * up[pl.ds(0, rows, stride=nz), :]


def north_roll(value, shift):
    return pltpu.roll(value, shift % value.shape[1], 1)


def put_row(value, row, index):
    where = lax.broadcasted_iota(jnp.int32, value.shape, 0) == index
    return jnp.where(where, jnp.broadcast_to(row, value.shape), value)


def below_of(value, row):
    return put_row(pltpu.roll(value, 1, 0), row, 0)


def above_of(value, row):
    return put_row(pltpu.roll(value, value.shape[0] - 1, 0), row, value.shape[0] - 1)


def fluid_of(block):
    return (1 - block).astype(F32)


def forward_kernel(
    nz, slabs,
    obs, obs_prev, obs_next, east, east_next, north, up,
    f_west, f_east, g_east, f_below, g_above,
    te_h, te_l, to_h, to_l, c_h, c_l, lam_a, lam_b, c0,
    modes, out,
    src, half, bottom, top, acc,
):
    step = pl.program_id(0)
    steps = pl.num_programs(0)
    chunk = src.shape[0] // nz
    ny = src.shape[1]
    nx = chunk * steps
    first_slab = lax.axis_index("gz") == 0
    lift = jnp.where(first_slab, 1.0, 0.0).astype(F32)

    fluid_prev = jnp.where(step == 0, f_west[...], fluid_of(obs_prev[...]))
    last = step == steps - 1
    after_fluid = fluid_of(obs_next[...])
    flux_after = jnp.where(last, g_east[...], after_fluid * east_next[...])

    def row(i, carry):
        fluid, masked = carry
        at = pl.multiple_of(i * nz, nz)
        nxt = pl.multiple_of(jnp.minimum(i + 1, chunk - 1) * nz, nz)
        end = i == chunk - 1
        fluid_next = fluid_of(obs[pl.ds(nxt, nz), :])
        flux = jnp.where(end, flux_after, fluid_next * east[pl.ds(nxt, nz), :])
        masked_next = fluid * flux
        north_masked = fluid * north_roll(fluid, 1) * north[pl.ds(at, nz), :]
        below = below_of(fluid, f_below[pl.ds(i, 1), :] + lift)
        up_masked = fluid * below * up[pl.ds(at, nz), :]
        up_after = above_of(up_masked, fluid[nz - 1 : nz, :] * g_above[pl.ds(i, 1), :])
        src[pl.ds(at, nz), :] = (
            (masked - masked_next) + (north_masked - north_roll(north_masked, -1)) + (up_masked - up_after)
        )
        return fluid_next, masked_next

    start = fluid_of(obs[0:nz, :])
    lax.fori_loop(0, chunk, row, (start, start * fluid_prev * east[0:nz, :]), unroll=2)

    hy = ny // 2
    low, high = src[:, :hy], src[:, hy:]
    rows = pl.ds(pl.multiple_of(step * chunk * nz, chunk * nz), chunk * nz)
    put_lanes(half, rows, dot3(split(low + high), (te_h[...], te_l[...])), 0)
    put_lanes(half, rows, dot3(split(low - high), (to_h[...], to_l[...])), hy // 128)

    @pl.when(last)
    def _():
        left = (c_h[...], c_l[...])
        for k in range(nz):
            modes[k] = dot3(left, split(get_lanes(half, pl.ds(k, nx, stride=nz))))
        acc[...] = jnp.zeros_like(acc)
        blocks = nx // 8

        def solve(n, carry):
            at = pl.ds(pl.multiple_of(n * 8, 8), 8)
            parity = n // (blocks // 2)
            for lane in range(0, ny, 128):
                lanes = slice(lane, lane + 128)
                shift = lam_a[at, :] + lam_b[:, lanes]
                local = slab_solve(shift, [modes[k, at, lanes] for k in range(nz)])
                bottom[at, lanes] = local[0]
                top[at, lanes] = local[nz - 1]
                weight = c0[at, :]
                for k in range(nz):
                    acc[parity, k, :, lanes] += weight * local[k]
            return carry

        lax.fori_loop(0, blocks, solve, 0)
        even = [jnp.sum(acc[0, k], axis=0, keepdims=True) for k in range(nz)]
        odd = [jnp.sum(acc[1, k], axis=0, keepdims=True) for k in range(nz)]
        west = jnp.concatenate([e + o for e, o in zip(even, odd)], 0)
        east_end = jnp.concatenate([e - o for e, o in zip(even, odd)], 0)
        width = ny // slabs
        for j in range(slabs):
            lanes = slice(j * width, (j + 1) * width)
            out[j, 0:nx, :] = jnp.concatenate([bottom[:, lanes], top[:, lanes]], 1)
            out[j, nx : nx + nz, :] = jnp.concatenate([west[:, lanes], east_end[:, lanes]], 1)


def ends_kernel(nz, ends, lam_a, lam_b, c0, sum_h, sum_l, sine_h, sine_l, out, acc):
    slabs, width = ends.shape[0], ends.shape[2] // 2
    nx = ends.shape[1] - nz
    blocks = nx // 8
    row_b = lam_b[lax.axis_index("gz")]
    acc[...] = jnp.zeros_like(acc)

    def block(n, carry):
        at = pl.ds(pl.multiple_of(n * 8, 8), 8)
        parity = n // (blocks // 2)
        shift = lam_a[at, :width] + row_b
        spike = spike_of(shift, nz)
        pairs = [ends[s, at, :] for s in range(slabs)]
        below, above = interface_chain(
            spike[0], spike[nz - 1], [p[:, :width] for p in pairs], [p[:, width:] for p in pairs]
        )
        weight = c0[at, :width]
        spike = [weight * g for g in spike]
        for s in range(slabs):
            for k in range(nz):
                rows = pl.ds((s * nz + k) * 8, 8)
                acc[parity, rows, :] += spike[k] * below[s] + spike[nz - 1 - k] * above[s]
        return carry

    lax.fori_loop(0, blocks, block, 0)
    even, odd = acc[0], acc[1]
    sums = jnp.concatenate([even + odd, even - odd], 1)
    rows = jnp.concatenate([ends[s, nx : nx + nz, :] for s in range(slabs)], 0)
    out[...] = dot3((sum_h[...], sum_l[...]), split(sums)) + dot3((sine_h[...], sine_l[...]), split(rows))


def power(value, count):
    result = None
    while count:
        if count & 1:
            result = value if result is None else result * value
        count >>= 1
        if count:
            value = value * value
    return result


def correct_kernel(nz, groups, ends, found, lam_a, lam_b, mu, c0, sine_h, sine_l, out, jump):
    slabs, width = ends.shape[0], ends.shape[2] // 2
    nx = ends.shape[1] - nz
    total = slabs * nz
    blocks = nx // 8
    row_b = lam_b[lax.axis_index("gz")]
    shift = mu[:, :width] + row_b[0:1, :]
    cosh = 1.0 + 0.5 * shift
    sinh = jnp.sqrt(shift + 0.25 * shift * shift)
    grow = cosh + sinh
    decay = 1.0 / grow
    far = power(decay, nx)
    far2 = far * far
    scale = 1.0 / (sinh * (1.0 - far2))
    self2 = ((1.0 + far2) + (decay + far2 * grow)) * scale
    cross2 = 2.0 * (1.0 + cosh) * far * scale
    inverse = {}
    for f in range(groups):
        key = min(f, groups - f)
        if key not in inverse:
            inverse[key] = 1.0 / (1.0 + self2 - float(np.cos(2 * np.pi * f / groups)) * cross2)
    kernel = {}
    for n in range(groups // 2 + 1):
        value = None
        for f in range(groups):
            factor = float(np.cos(2 * np.pi * f * n / groups)) / groups
            term = factor * inverse[min(f, groups - f)]
            value = term if value is None else value + term
        kernel[n] = value
    jumps_east, jumps_west = None, None
    for n in range(groups):
        nxt = (n + 1) % groups
        t = found[n * total : (n + 1) * total, width:] - found[nxt * total : (nxt + 1) * total, :width]
        east_term = kernel[min(n, groups - n)] * t
        west_term = kernel[min(nxt, groups - nxt)] * t
        jumps_east = east_term if jumps_east is None else jumps_east + east_term
        jumps_west = west_term if jumps_west is None else jumps_west + west_term
    both = dot3((sine_h[...], sine_l[...]), split(jnp.concatenate([jumps_west, jumps_east], 1)))
    west, east = both[:, :width], both[:, width:]
    jump[0] = west - east
    jump[1] = west + east
    for s in range(slabs):
        out[s, nx : nx + nz, :] = both[s * nz : (s + 1) * nz, :]

    def block(n, carry):
        at = pl.ds(pl.multiple_of(n * 8, 8), 8)
        parity = n // (blocks // 2)
        shift = lam_a[at, :width] + row_b
        spike = spike_of(shift, nz)
        weight = c0[at, :width]
        loads = [weight * g for g in spike]
        bottoms, tops = [], []
        for s in range(slabs):
            pair = ends[s, at, :]
            low, high = pair[:, :width], pair[:, width:]
            for k in range(nz):
                q = jnp.broadcast_to(jump[parity, pl.ds(s * nz + k, 1), :], low.shape)
                low = low + loads[k] * q
                high = high + loads[nz - 1 - k] * q
            bottoms.append(low)
            tops.append(high)
        below, above = interface_chain(spike[0], spike[nz - 1], bottoms, tops)
        for s in range(slabs):
            out[s, at, :] = jnp.concatenate([below[s], above[s]], 1)
        return carry

    lax.fori_loop(0, blocks, block, 0)


def backward_kernel(
    nz, slabs,
    modes, solved,
    obs, obs_prev, obs_next, east, east_next, north, up,
    f_west, f_east, g_east, f_below, g_above, f_above,
    te_h, te_l, ti_h, ti_l, ct_h, ct_l, lam_a, lam_b, c0,
    out_east, out_north, out_up, out_p, out_r,
    below, above, found, half, press, p_below, p_above,
):
    step = pl.program_id(0)
    steps = pl.num_programs(0)
    chunk = obs.shape[0] // nz
    ny = obs.shape[1]
    hy = ny // 2
    nx = chunk * steps
    first_slab = lax.axis_index("gz") == 0
    lift = jnp.where(first_slab, 1.0, 0.0).astype(F32)
    last = step == steps - 1

    @pl.when(step == 0)
    def _():
        width = ny // slabs
        west, east_end = [], []
        for j in range(slabs):
            lanes = slice(j * width, (j + 1) * width)
            below[:, lanes] = solved[j, 0:nx, :width]
            above[:, lanes] = solved[j, 0:nx, width:]
            west.append(solved[j, nx : nx + nz, :width])
            east_end.append(solved[j, nx : nx + nz, width:])
        west = jnp.concatenate(west, 1)
        east_end = jnp.concatenate(east_end, 1)
        found[2] = west
        found[3] = east_end
        found[0] = west - east_end
        found[1] = west + east_end
        blocks = nx // 8

        def solve(n, carry):
            at = pl.ds(pl.multiple_of(n * 8, 8), 8)
            parity = n // (blocks // 2)
            for lane in range(0, ny, 128):
                lanes = slice(lane, lane + 128)
                shift = lam_a[at, :] + lam_b[:, lanes]
                weight = c0[at, :]
                right = []
                for k in range(nz):
                    q = jnp.broadcast_to(found[parity, pl.ds(k, 1), lanes], weight.shape)
                    right.append(modes[k, at, lanes] + weight * q)
                right[0] = right[0] + below[at, lanes]
                right[nz - 1] = right[nz - 1] + above[at, lanes]
                local = slab_solve(shift, right)
                for k in range(nz):
                    modes[k, at, lanes] = local[k]
            return carry

        lax.fori_loop(0, blocks, solve, 0)
        left = (ct_h[...], ct_l[...])
        for k in range(nz):
            put_lanes(half, pl.ds(nz + k, nx, stride=nz), dot3(left, split(modes[k])), 0)
        first, final = slice(nz, 2 * nz), slice(nx * nz, (nx + 1) * nz)
        put_lanes(half, slice(0, nz), get_lanes(half, first) + found[2], 0)
        put_lanes(half, slice((nx + 1) * nz, (nx + 2) * nz), get_lanes(half, final) - found[3], 0)

        def north_back(value):
            even = dot3(split(value[:, :hy]), (te_h[...], te_l[...]))
            odd = dot3(split(value[:, hy:]), (ti_h[...], ti_l[...]))
            return even + odd, even - odd

        p_below[:, :hy], p_below[:, hy:] = north_back(dot3(left, split(below[...])))
        p_above[:, :hy], p_above[:, hy:] = north_back(dot3(left, split(above[...])))
        size = 16 * nz

        def back(n, carry):
            at = pl.ds(pl.multiple_of(n * size, size), size)
            press[at, :hy], press[at, hy:] = north_back(get_lanes(half, at))
            return carry

        lax.fori_loop(0, nx * nz // size, back, 0)
        at = slice(nx * nz, (nx + 2) * nz)
        press[at, :hy], press[at, hy:] = north_back(get_lanes(half, at))

    fluid_prev = jnp.where(step == 0, f_west[...], fluid_of(obs_prev[...]))
    after_fluid = jnp.where(last, f_east[...], fluid_of(obs_next[...]))
    flux_after = jnp.where(last, g_east[...], fluid_of(obs_next[...]) * east_next[...])
    base = step * chunk

    def rows_of(i):
        return pl.ds(pl.multiple_of((base + i + 1) * nz, nz), nz)

    def row(i, carry):
        fluid, p, east_done = carry
        at = pl.ds(pl.multiple_of(i * nz, nz), nz)
        nxt = pl.ds(pl.multiple_of(jnp.minimum(i + 1, chunk - 1) * nz, nz), nz)
        end = i == chunk - 1
        fluid_next = jnp.where(end, after_fluid, fluid_of(obs[nxt, :]))
        flux = jnp.where(end, flux_after, fluid_next * east[nxt, :])
        p_next = press[rows_of(i + 1), :]
        east_next_done = fluid * (flux - fluid_next * (p_next - p))
        north_done = fluid * north_roll(fluid, 1) * (north[at, :] - (p - north_roll(p, 1)))
        line = pl.ds(base + i, 1)
        chunk_line = pl.ds(i, 1)
        fluid_below = below_of(fluid, f_below[chunk_line, :] + lift)
        up_done = fluid * fluid_below * (up[at, :] - (p - below_of(p, p_below[line, :])))
        edge = fluid[nz - 1 : nz, :] * (
            g_above[chunk_line, :] - f_above[chunk_line, :] * (p_above[line, :] - p[nz - 1 : nz, :])
        )
        out_east[at, :] = east_done
        out_north[at, :] = north_done
        out_up[at, :] = up_done
        out_p[at, :] = p
        out_r[at, :] = (
            (east_done - east_next_done)
            + (north_done - north_roll(north_done, -1))
            + (up_done - above_of(up_done, edge))
        )
        return fluid_next, p_next, east_next_done

    start = fluid_of(obs[0:nz, :])
    p_first = press[rows_of(0), :]
    done = start * fluid_prev * (east[0:nz, :] - (p_first - press[rows_of(-1), :]))
    lax.fori_loop(0, chunk, row, (start, p_first, done), unroll=2)


def local(groups, slabs, east_velocity, north_velocity, upward_velocity, obstacle):
    nx, nz, ny = east_velocity.shape
    total = slabs * nz
    width = ny // slabs
    flat = [a.reshape(nx * nz, ny) for a in (obstacle, east_velocity, north_velocity, upward_velocity)]
    obs, east, north, up = flat

    even_np, odd_np, lam_b_np = north_tables(ny)
    block_np, lam_a_np = east_tables(nx)
    sine_np, mu_np = sine_table(total)
    te_h, te_l = pair_np(even_np)
    to_h, to_l = pair_np(odd_np)
    ti_h, ti_l = pair_np(odd_np.T.copy())
    c_h, c_l = pair_np(block_np)
    ct_h, ct_l = pair_np(block_np.T.copy())
    sine_h, sine_l = pair_np(sine_np)
    sum_h, sum_l = (np.repeat(t, 8, axis=1) for t in (sine_h, sine_l))
    lam_a = np.repeat(lam_a_np[:, None], 128, 1).astype(np.float32)
    c0 = np.repeat(block_np[:, :1], 128, 1).astype(np.float32)
    lam_b = np.repeat(lam_b_np[None], 8, 0).astype(np.float32)
    lam_b_part = np.repeat(lam_b_np.reshape(slabs, 1, width), 8, 1).astype(np.float32)
    mu = np.repeat(mu_np[:, None], 128, 1).astype(np.float32)

    chunk = 16
    steps = nx // chunk
    params = pltpu.CompilerParams(vmem_limit_bytes=VMEM_LIMIT, dimension_semantics=("arbitrary",))
    single = pltpu.CompilerParams(vmem_limit_bytes=VMEM_LIMIT)
    big = pl.BlockSpec((chunk * nz, ny), lambda i: (i, 0))
    line = pl.BlockSpec((chunk, ny), lambda i: (i, 0))
    before = pl.BlockSpec((nz, ny), lambda i: (jnp.maximum(i * chunk - 1, 0), 0))
    after = pl.BlockSpec((nz, ny), lambda i: (jnp.minimum(i * chunk + chunk, nx - 1), 0))

    def whole(a):
        return pl.BlockSpec(a.shape, lambda *_: (0,) * len(a.shape))

    plane = jax.ShapeDtypeStruct((nx, ny), F32)
    f_top, f_bot, g_bot = pl.pallas_call(
        functools.partial(first_rows, nz),
        grid=(ny // 128,),
        in_specs=[pl.BlockSpec((nx * nz, 128), lambda i: (0, i))] * 2,
        out_specs=[pl.BlockSpec((nx, 128), lambda i: (0, i))] * 3,
        out_shape=[plane] * 3,
        compiler_params=params,
        name="planes",
    )(obs, up)

    rising = [(i, i + 1) for i in range(slabs - 1)]
    falling = [(i + 1, i) for i in range(slabs - 1)]
    to_east = [(i, (i + 1) % groups) for i in range(groups)]
    to_west = [((i + 1) % groups, i) for i in range(groups)]
    f_below = lax.ppermute(f_top, "gz", rising)
    g_above = lax.ppermute(g_bot, "gz", falling)
    f_first = (1 - obs[:nz]).astype(F32)
    f_west = lax.ppermute((1 - obs[(nx - 1) * nz :]).astype(F32), "xy", to_east)
    side = lax.ppermute(jnp.concatenate([f_first, f_first * east[:nz]], 0), "xy", to_west)
    f_east, g_east = side[:nz], side[nz:]
    f_above = lax.ppermute(f_bot, "gz", falling)

    tables = (te_h, te_l, to_h, to_l, c_h, c_l, lam_a, lam_b, c0)
    ends_shape = jax.ShapeDtypeStruct((slabs, nx + nz, 2 * width), F32)
    modes, ends = pl.pallas_call(
        functools.partial(forward_kernel, nz, slabs),
        grid=(steps,),
        in_specs=[big, before, after, big, after, big, big]
        + [whole(f_west)] * 3 + [line, line]
        + [whole(t) for t in tables],
        out_specs=[
            pl.BlockSpec((nz, nx, ny), lambda i: (0, 0, 0)),
            pl.BlockSpec(ends_shape.shape, lambda i: (0, 0, 0)),
        ],
        out_shape=[jax.ShapeDtypeStruct((nz, nx, ny), F32), ends_shape],
        scratch_shapes=[
            pltpu.VMEM((chunk * nz, ny), F32),
            pltpu.VMEM((ny // 128, nx * nz, 128), F32),
            pltpu.VMEM((nx, ny), F32),
            pltpu.VMEM((nx, ny), F32),
            pltpu.VMEM((2, nz, 8, ny), F32),
        ],
        compiler_params=params,
        name="forward",
    )(obs, obs, obs, east, east, north, up, f_west, f_east, g_east, f_below, g_above, *tables)

    ends = lax.all_to_all(ends, "gz", split_axis=0, concat_axis=0, tiled=True)
    own = pl.pallas_call(
        functools.partial(ends_kernel, nz),
        out_shape=jax.ShapeDtypeStruct((total, 2 * width), F32),
        scratch_shapes=[pltpu.VMEM((2, total * 8, width), F32)],
        compiler_params=single,
        name="ends",
    )(ends, lam_a, lam_b_part, c0, sum_h, sum_l, sine_h, sine_l)
    found = [own]
    for shift in range(1, groups):
        found.append(lax.ppermute(own, "xy", [((i + shift) % groups, i) for i in range(groups)]))
    solved = pl.pallas_call(
        functools.partial(correct_kernel, nz, groups),
        out_shape=ends_shape,
        scratch_shapes=[pltpu.VMEM((2, total, width), F32)],
        compiler_params=single,
        name="correct",
    )(ends, jnp.concatenate(found, 0), lam_a, lam_b_part, mu, c0, sine_h, sine_l)
    solved = lax.all_to_all(solved, "gz", split_axis=0, concat_axis=0, tiled=True)

    tables = (te_h, te_l, ti_h, ti_l, ct_h, ct_l, lam_a, lam_b, c0)
    field = jax.ShapeDtypeStruct((nx * nz, ny), F32)
    outs = pl.pallas_call(
        functools.partial(backward_kernel, nz, slabs),
        grid=(steps,),
        in_specs=[
            pl.BlockSpec((nz, nx, ny), lambda i: (0, 0, 0)),
            pl.BlockSpec(ends_shape.shape, lambda i: (0, 0, 0)),
        ]
        + [big, before, after, big, after, big, big]
        + [whole(f_west)] * 3 + [line, line, line]
        + [whole(t) for t in tables],
        out_specs=[big] * 5,
        out_shape=[field] * 5,
        scratch_shapes=[
            pltpu.VMEM((nx, ny), F32),
            pltpu.VMEM((nx, ny), F32),
            pltpu.VMEM((4, nz, ny), F32),
            pltpu.VMEM((ny // 128, (nx + 2) * nz, 128), F32),
            pltpu.VMEM(((nx + 2) * nz, ny), F32),
            pltpu.VMEM((nx, ny), F32),
            pltpu.VMEM((nx, ny), F32),
        ],
        compiler_params=params,
        name="backward",
    )(modes, solved, obs, obs, obs, east, east, north, up,
      f_west, f_east, g_east, f_below, g_above, f_above, *tables)
    return tuple(o.reshape(nx, nz, ny) for o in outs)


def solution(mesh):
    placed = P("xy", "gz", None)
    return jax.shard_map(
        functools.partial(local, mesh.shape["xy"], mesh.shape["gz"]),
        mesh=mesh,
        in_specs=(placed,) * 4,
        out_specs=(placed,) * 5,
        check_vma=False,
    )
```

```python
import functools

import jax
import jax.numpy as jnp
import ml_dtypes
import numpy as np
from jax import lax
from jax.experimental import pallas as pl
from jax.experimental.pallas import tpu as pltpu
from jax.sharding import PartitionSpec as P

F32 = jnp.float32
BF16 = jnp.bfloat16
VMEM_LIMIT = 60 * 1024 * 1024


def pair_np(table):
    high = table.astype(np.float32).astype(ml_dtypes.bfloat16)
    low = (table - high.astype(np.float64)).astype(np.float32).astype(ml_dtypes.bfloat16)
    return high, low


def north_tables(length):
    half = length // 2
    cell = np.arange(half)[:, None]
    mode = np.arange(half)[None, :]

    def cas(number):
        angle = 2.0 * np.pi * ((cell * number) % length) / length
        return (np.cos(angle) + np.sin(angle)) / np.sqrt(length)

    numbers = np.concatenate([2 * np.arange(half), 2 * np.arange(half) + 1])
    eigen = 4.0 * np.sin(np.pi * numbers / length) ** 2
    return cas(2 * mode), cas(2 * mode + 1), eigen


def east_tables(length):
    modes = np.concatenate([np.arange(0, length, 2), np.arange(1, length, 2)])
    cell = np.arange(length)
    table = np.cos(np.pi * modes[:, None] * (2 * cell[None, :] + 1) / (2 * length)) * np.sqrt(2.0 / length)
    table[0] = np.sqrt(1.0 / length)
    eigen = 4.0 * np.sin(np.pi * modes / (2 * length)) ** 2
    return table, eigen


def sine_table(length):
    index = np.arange(1, length + 1)
    table = np.sqrt(2.0 / (length + 1)) * np.sin(np.pi * np.outer(index, index) / (length + 1))
    eigen = 4.0 * np.sin(np.pi * index / (2 * (length + 1))) ** 2
    return table, eigen


def split(value):
    high = value.astype(BF16)
    return high, (value - high.astype(F32)).astype(BF16)


def dot3(left, right):
    (lh, ll), (rh, rl) = left, right
    dot = functools.partial(jnp.dot, preferred_element_type=F32)
    return dot(lh, rh) + (dot(ll, rh) + dot(lh, rl))


def chebyshev(shift, count):
    values = [jnp.ones_like(shift)]
    step = values[0]
    for n in range(count):
        step = step + shift * values[n]
        values.append(values[n] + step)
    return values


def slab_solve(shift, right):
    count = len(right)
    u = chebyshev(shift, count)
    inverse = 1.0 / u[count]
    lower = [right[0]]
    for k in range(1, count):
        lower.append(lower[-1] + u[k] * right[k])
    upper = [None] * count
    for k in range(count - 2, -1, -1):
        term = u[count - 2 - k] * right[k + 1] if k < count - 2 else right[k + 1]
        upper[k] = term if upper[k + 1] is None else upper[k + 1] + term
    out = []
    for k in range(count):
        value = u[count - 1 - k] * lower[k]
        if upper[k] is not None:
            value = value + u[k] * upper[k]
        out.append(value * inverse)
    return out


def spike_of(shift, count):
    u = chebyshev(shift, count)
    inverse = 1.0 / u[count]
    return [u[count - 1 - k] * inverse for k in range(count)]


def interface_chain(couple, spread, bottoms, tops):
    count = len(bottoms)
    slope = jnp.zeros_like(couple)
    offset = jnp.zeros_like(couple)
    slopes, offsets, inverses, bases = [], [], [], []
    for s in range(count):
        inverse = 1.0 / (1.0 - couple * slope)
        base = (bottoms[s] + couple * offset) * inverse
        slopes.append(slope)
        offsets.append(offset)
        inverses.append(inverse * spread)
        bases.append(base)
        if s < count - 1:
            weight = spread * slope
            slope, offset = (
                couple + weight * spread * inverse,
                tops[s] + spread * offset + weight * base,
            )
    above = jnp.zeros_like(couple)
    lowers, uppers = [None] * count, [None] * count
    for s in range(count - 1, -1, -1):
        lower = bases[s] + inverses[s] * above
        uppers[s] = tops[s] + spread * (slopes[s] * lower + offsets[s]) + couple * above
        lowers[s] = lower
        above = lower
    below = [jnp.zeros_like(couple)] + uppers[:-1]
    above = lowers[1:] + [jnp.zeros_like(couple)]
    return below, above


def get_lanes(ref, rows):
    return jnp.concatenate([ref[n, rows, :] for n in range(ref.shape[0])], 1)


def put_lanes(ref, rows, value, start):
    for n in range(value.shape[1] // 128):
        ref[start + n, rows, :] = value[:, n * 128 : (n + 1) * 128]


def first_rows(nz, obs, up, ftop, fbot, gbot):
    rows = ftop.shape[0]
    ftop[...] = (1 - obs[pl.ds(nz - 1, rows, stride=nz), :]).astype(F32)
    low = (1 - obs[pl.ds(0, rows, stride=nz), :]).astype(F32)
    fbot[...] = low
    gbot[...] = low * up[pl.ds(0, rows, stride=nz), :]


def north_roll(value, shift):
    return pltpu.roll(value, shift % value.shape[1], 1)


def put_row(value, row, index):
    where = lax.broadcasted_iota(jnp.int32, value.shape, 0) == index
    return jnp.where(where, jnp.broadcast_to(row, value.shape), value)


def below_of(value, row):
    return put_row(pltpu.roll(value, 1, 0), row, 0)


def above_of(value, row):
    return put_row(pltpu.roll(value, value.shape[0] - 1, 0), row, value.shape[0] - 1)


def fluid_of(block):
    return (1 - block).astype(F32)


def forward_kernel(
    nz, slabs,
    obs, obs_prev, obs_next, east, east_next, north, up,
    f_west, f_east, g_east, f_below, g_above,
    te_h, te_l, to_h, to_l, c_h, c_l, lam_a, lam_b, c0,
    modes, out,
    src, half, bottom, top, acc,
):
    step = pl.program_id(0)
    steps = pl.num_programs(0)
    chunk = src.shape[0] // nz
    ny = src.shape[1]
    nx = chunk * steps
    first_slab = lax.axis_index("gz") == 0
    lift = jnp.where(first_slab, 1.0, 0.0).astype(F32)

    fluid_prev = jnp.where(step == 0, f_west[...], fluid_of(obs_prev[...]))
    last = step == steps - 1
    after_fluid = fluid_of(obs_next[...])
    flux_after = jnp.where(last, g_east[...], after_fluid * east_next[...])

    def row(i, carry):
        fluid, masked = carry
        at = pl.multiple_of(i * nz, nz)
        nxt = pl.multiple_of(jnp.minimum(i + 1, chunk - 1) * nz, nz)
        end = i == chunk - 1
        fluid_next = fluid_of(obs[pl.ds(nxt, nz), :])
        flux = jnp.where(end, flux_after, fluid_next * east[pl.ds(nxt, nz), :])
        masked_next = fluid * flux
        north_masked = fluid * north_roll(fluid, 1) * north[pl.ds(at, nz), :]
        below = below_of(fluid, f_below[pl.ds(i, 1), :] + lift)
        up_masked = fluid * below * up[pl.ds(at, nz), :]
        up_after = above_of(up_masked, fluid[nz - 1 : nz, :] * g_above[pl.ds(i, 1), :])
        src[pl.ds(at, nz), :] = (
            (masked - masked_next) + (north_masked - north_roll(north_masked, -1)) + (up_masked - up_after)
        )
        return fluid_next, masked_next

    start = fluid_of(obs[0:nz, :])
    lax.fori_loop(0, chunk, row, (start, start * fluid_prev * east[0:nz, :]), unroll=2)

    hy = ny // 2
    low, high = src[:, :hy], src[:, hy:]
    rows = pl.ds(pl.multiple_of(step * chunk * nz, chunk * nz), chunk * nz)
    put_lanes(half, rows, dot3(split(low + high), (te_h[...], te_l[...])), 0)
    put_lanes(half, rows, dot3(split(low - high), (to_h[...], to_l[...])), hy // 128)

    @pl.when(last)
    def _():
        left = (c_h[...], c_l[...])
        for k in range(nz):
            modes[k] = dot3(left, split(get_lanes(half, pl.ds(k, nx, stride=nz))))
        acc[...] = jnp.zeros_like(acc)
        blocks = nx // 8

        def solve(n, carry):
            at = pl.ds(pl.multiple_of(n * 8, 8), 8)
            parity = n // (blocks // 2)
            for lane in range(0, ny, 128):
                lanes = slice(lane, lane + 128)
                shift = lam_a[at, :] + lam_b[:, lanes]
                local = slab_solve(shift, [modes[k, at, lanes] for k in range(nz)])
                bottom[at, lanes] = local[0]
                top[at, lanes] = local[nz - 1]
                weight = c0[at, :]
                for k in range(nz):
                    acc[parity, k, :, lanes] += weight * local[k]
            return carry

        lax.fori_loop(0, blocks, solve, 0)
        even = [jnp.sum(acc[0, k], axis=0, keepdims=True) for k in range(nz)]
        odd = [jnp.sum(acc[1, k], axis=0, keepdims=True) for k in range(nz)]
        west = jnp.concatenate([e + o for e, o in zip(even, odd)], 0)
        east_end = jnp.concatenate([e - o for e, o in zip(even, odd)], 0)
        width = ny // slabs
        for j in range(slabs):
            lanes = slice(j * width, (j + 1) * width)
            hx = nx // 2
            out[j, 0:hx, :] = jnp.concatenate([bottom[:hx, lanes], bottom[hx:, lanes]], 1)
            out[j, hx:nx, :] = jnp.concatenate([top[:hx, lanes], top[hx:, lanes]], 1)
            out[j, nx : nx + nz, :] = jnp.concatenate([west[:, lanes], east_end[:, lanes]], 1)


def swap_halves(value):
    width = value.shape[1] // 2
    return jnp.concatenate([value[:, width:], value[:, :width]], 1)


def in_first_half(value):
    return lax.broadcasted_iota(jnp.int32, value.shape, 1) < value.shape[1] // 2


def ends_kernel(nz, ends, lam_a, lam_b, c0, sum_h, sum_l, sine_h, sine_l, out, acc):
    slabs = ends.shape[0]
    nx = ends.shape[1] - nz
    hx = nx // 2
    shift = lam_a[...] + lam_b[lax.axis_index("gz")][0:1, :]
    spike = spike_of(shift, nz)
    below, above = interface_chain(
        spike[0],
        spike[nz - 1],
        [ends[s, 0:hx, :] for s in range(slabs)],
        [ends[s, hx:nx, :] for s in range(slabs)],
    )
    weight = c0[...]
    spike = [weight * g for g in spike]
    for s in range(slabs):
        for k in range(nz):
            term = spike[k] * below[s] + spike[nz - 1 - k] * above[s]
            row = (s * nz + k) * 8
            acc[row : row + 8, :] = jnp.sum(term.reshape(hx // 8, 8, term.shape[1]), axis=0)
    both = dot3((sum_h[...], sum_l[...]), split(acc[...]))
    other = swap_halves(both)
    both = jnp.where(in_first_half(both), both + other, other - both)
    rows = jnp.concatenate([ends[s, nx : nx + nz, :] for s in range(slabs)], 0)
    out[...] = both + dot3((sine_h[...], sine_l[...]), split(rows))


def power(value, count):
    result = None
    while count:
        if count & 1:
            result = value if result is None else result * value
        count >>= 1
        if count:
            value = value * value
    return result


def correct_kernel(nz, groups, ends, *rest):
    found = rest[:groups]
    lam_a, lam_b, mu, c0, sine_h, sine_l, out, jump = rest[groups:]
    slabs, width = ends.shape[0], ends.shape[2] // 2
    nx = ends.shape[1] - nz
    hx = nx // 2
    row_b = lam_b[lax.axis_index("gz")][0:1, :]
    shift = mu[:, :width] + row_b[:, :width]
    cosh = 1.0 + 0.5 * shift
    sinh = jnp.sqrt(shift + 0.25 * shift * shift)
    grow = cosh + sinh
    decay = 1.0 / grow
    far = power(decay, nx)
    far2 = far * far
    scale = 1.0 / (sinh * (1.0 - far2))
    self2 = ((1.0 + far2) + (decay + far2 * grow)) * scale
    cross2 = 2.0 * (1.0 + cosh) * far * scale
    inverse = {}
    for f in range(groups):
        key = min(f, groups - f)
        if key not in inverse:
            inverse[key] = 1.0 / (1.0 + self2 - float(np.cos(2 * np.pi * f / groups)) * cross2)
    kernel = {}
    for n in range(groups // 2 + 1):
        value = None
        for f in range(groups):
            factor = float(np.cos(2 * np.pi * f * n / groups)) / groups
            term = factor * inverse[min(f, groups - f)]
            value = term if value is None else value + term
        kernel[n] = value
    jumps_east, jumps_west = None, None
    for n in range(groups):
        nxt = (n + 1) % groups
        t = found[n][:, width:] - found[nxt][:, :width]
        east_term = kernel[min(n, groups - n)] * t
        west_term = kernel[min(nxt, groups - nxt)] * t
        jumps_east = east_term if jumps_east is None else jumps_east + east_term
        jumps_west = west_term if jumps_west is None else jumps_west + west_term
    both = dot3((sine_h[...], sine_l[...]), split(jnp.concatenate([jumps_west, jumps_east], 1)))
    other = swap_halves(both)
    jump[...] = jnp.where(in_first_half(both), both - other, both + other)
    shift = lam_a[...] + row_b
    spike = spike_of(shift, nz)
    weight = c0[...]
    loads = [weight * g for g in spike]
    bottoms, tops = [], []
    for s in range(slabs):
        low, high = ends[s, 0:hx, :], ends[s, hx:nx, :]
        for k in range(nz):
            q = jump[s * nz + k : s * nz + k + 1, :]
            low = low + loads[k] * q
            high = high + loads[nz - 1 - k] * q
        bottoms.append(low)
        tops.append(high)
    below, above = interface_chain(spike[0], spike[nz - 1], bottoms, tops)
    for s in range(slabs):
        out[s, 0:hx, :] = below[s]
        out[s, hx:nx, :] = above[s]
        out[s, nx : nx + nz, :] = both[s * nz : (s + 1) * nz, :]


def backward_kernel(
    nz, slabs,
    modes, solved,
    obs, obs_prev, obs_next, east, east_next, north, up,
    f_west, f_east, g_east, f_below, g_above, f_above,
    te_h, te_l, ti_h, ti_l, ct_h, ct_l, lam_a, lam_b, c0,
    out_east, out_north, out_up, out_p, out_r,
    below, above, found, half, press, p_below, p_above,
):
    step = pl.program_id(0)
    steps = pl.num_programs(0)
    chunk = obs.shape[0] // nz
    ny = obs.shape[1]
    hy = ny // 2
    nx = chunk * steps
    first_slab = lax.axis_index("gz") == 0
    lift = jnp.where(first_slab, 1.0, 0.0).astype(F32)
    last = step == steps - 1

    @pl.when(step == 0)
    def _():
        width = ny // slabs
        west, east_end = [], []
        for j in range(slabs):
            lanes = slice(j * width, (j + 1) * width)
            hx = nx // 2
            below[:hx, lanes] = solved[j, 0:hx, :width]
            below[hx:, lanes] = solved[j, 0:hx, width:]
            above[:hx, lanes] = solved[j, hx:nx, :width]
            above[hx:, lanes] = solved[j, hx:nx, width:]
            west.append(solved[j, nx : nx + nz, :width])
            east_end.append(solved[j, nx : nx + nz, width:])
        west = jnp.concatenate(west, 1)
        east_end = jnp.concatenate(east_end, 1)
        found[2] = west
        found[3] = east_end
        found[0] = west - east_end
        found[1] = west + east_end
        blocks = nx // 8

        def solve(n, carry):
            at = pl.ds(pl.multiple_of(n * 8, 8), 8)
            parity = n // (blocks // 2)
            for lane in range(0, ny, 128):
                lanes = slice(lane, lane + 128)
                shift = lam_a[at, :] + lam_b[:, lanes]
                weight = c0[at, :]
                right = []
                for k in range(nz):
                    q = jnp.broadcast_to(found[parity, pl.ds(k, 1), lanes], weight.shape)
                    right.append(modes[k, at, lanes] + weight * q)
                right[0] = right[0] + below[at, lanes]
                right[nz - 1] = right[nz - 1] + above[at, lanes]
                local = slab_solve(shift, right)
                for k in range(nz):
                    modes[k, at, lanes] = local[k]
            return carry

        lax.fori_loop(0, blocks, solve, 0)
        left = (ct_h[...], ct_l[...])
        for k in range(nz):
            put_lanes(half, pl.ds(nz + k, nx, stride=nz), dot3(left, split(modes[k])), 0)
        first, final = slice(nz, 2 * nz), slice(nx * nz, (nx + 1) * nz)
        put_lanes(half, slice(0, nz), get_lanes(half, first) + found[2], 0)
        put_lanes(half, slice((nx + 1) * nz, (nx + 2) * nz), get_lanes(half, final) - found[3], 0)

        def north_back(value):
            even = dot3(split(value[:, :hy]), (te_h[...], te_l[...]))
            odd = dot3(split(value[:, hy:]), (ti_h[...], ti_l[...]))
            return even + odd, even - odd

        p_below[:, :hy], p_below[:, hy:] = north_back(dot3(left, split(below[...])))
        p_above[:, :hy], p_above[:, hy:] = north_back(dot3(left, split(above[...])))
        size = 16 * nz

        def back(n, carry):
            at = pl.ds(pl.multiple_of(n * size, size), size)
            press[at, :hy], press[at, hy:] = north_back(get_lanes(half, at))
            return carry

        lax.fori_loop(0, nx * nz // size, back, 0)
        at = slice(nx * nz, (nx + 2) * nz)
        press[at, :hy], press[at, hy:] = north_back(get_lanes(half, at))

    fluid_prev = jnp.where(step == 0, f_west[...], fluid_of(obs_prev[...]))
    after_fluid = jnp.where(last, f_east[...], fluid_of(obs_next[...]))
    flux_after = jnp.where(last, g_east[...], fluid_of(obs_next[...]) * east_next[...])
    base = step * chunk

    def rows_of(i):
        return pl.ds(pl.multiple_of((base + i + 1) * nz, nz), nz)

    def row(i, carry):
        fluid, p, east_done = carry
        at = pl.ds(pl.multiple_of(i * nz, nz), nz)
        nxt = pl.ds(pl.multiple_of(jnp.minimum(i + 1, chunk - 1) * nz, nz), nz)
        end = i == chunk - 1
        fluid_next = jnp.where(end, after_fluid, fluid_of(obs[nxt, :]))
        flux = jnp.where(end, flux_after, fluid_next * east[nxt, :])
        p_next = press[rows_of(i + 1), :]
        east_next_done = fluid * (flux - fluid_next * (p_next - p))
        north_done = fluid * north_roll(fluid, 1) * (north[at, :] - (p - north_roll(p, 1)))
        line = pl.ds(base + i, 1)
        chunk_line = pl.ds(i, 1)
        fluid_below = below_of(fluid, f_below[chunk_line, :] + lift)
        up_done = fluid * fluid_below * (up[at, :] - (p - below_of(p, p_below[line, :])))
        edge = fluid[nz - 1 : nz, :] * (
            g_above[chunk_line, :] - f_above[chunk_line, :] * (p_above[line, :] - p[nz - 1 : nz, :])
        )
        out_east[at, :] = east_done
        out_north[at, :] = north_done
        out_up[at, :] = up_done
        out_p[at, :] = p
        out_r[at, :] = (
            (east_done - east_next_done)
            + (north_done - north_roll(north_done, -1))
            + (up_done - above_of(up_done, edge))
        )
        return fluid_next, p_next, east_next_done

    start = fluid_of(obs[0:nz, :])
    p_first = press[rows_of(0), :]
    done = start * fluid_prev * (east[0:nz, :] - (p_first - press[rows_of(-1), :]))
    lax.fori_loop(0, chunk, row, (start, p_first, done), unroll=2)


def local(groups, slabs, east_velocity, north_velocity, upward_velocity, obstacle):
    nx, nz, ny = east_velocity.shape
    total = slabs * nz
    width = ny // slabs
    flat = [a.reshape(nx * nz, ny) for a in (obstacle, east_velocity, north_velocity, upward_velocity)]
    obs, east, north, up = flat

    even_np, odd_np, lam_b_np = north_tables(ny)
    block_np, lam_a_np = east_tables(nx)
    sine_np, mu_np = sine_table(total)
    te_h, te_l = pair_np(even_np)
    to_h, to_l = pair_np(odd_np)
    ti_h, ti_l = pair_np(odd_np.T.copy())
    c_h, c_l = pair_np(block_np)
    ct_h, ct_l = pair_np(block_np.T.copy())
    sine_h, sine_l = pair_np(sine_np)
    sum_h, sum_l = (np.repeat(t, 8, axis=1) for t in (sine_h, sine_l))
    lam_a = np.repeat(lam_a_np[:, None], 128, 1).astype(np.float32)
    c0 = np.repeat(block_np[:, :1], 128, 1).astype(np.float32)
    lam_b = np.repeat(lam_b_np[None], 8, 0).astype(np.float32)
    part = np.tile(lam_b_np.reshape(slabs, 1, width), (1, 8, 2)).astype(np.float32)

    def paired(column):
        return np.repeat(column.reshape(2, nx // 2).T, width, 1).astype(np.float32)

    lam_pair, c0_pair = paired(lam_a_np), paired(block_np[:, 0])
    mu = np.repeat(mu_np[:, None], 128, 1).astype(np.float32)

    chunk = 16
    steps = nx // chunk
    params = pltpu.CompilerParams(vmem_limit_bytes=VMEM_LIMIT, dimension_semantics=("arbitrary",))
    single = pltpu.CompilerParams(vmem_limit_bytes=VMEM_LIMIT)
    big = pl.BlockSpec((chunk * nz, ny), lambda i: (i, 0))
    line = pl.BlockSpec((chunk, ny), lambda i: (i, 0))
    before = pl.BlockSpec((nz, ny), lambda i: (jnp.maximum(i * chunk - 1, 0), 0))
    after = pl.BlockSpec((nz, ny), lambda i: (jnp.minimum(i * chunk + chunk, nx - 1), 0))

    def whole(a):
        return pl.BlockSpec(a.shape, lambda *_: (0,) * len(a.shape))

    plane = jax.ShapeDtypeStruct((nx, ny), F32)
    f_top, f_bot, g_bot = pl.pallas_call(
        functools.partial(first_rows, nz),
        grid=(ny // 128,),
        in_specs=[pl.BlockSpec((nx * nz, 128), lambda i: (0, i))] * 2,
        out_specs=[pl.BlockSpec((nx, 128), lambda i: (0, i))] * 3,
        out_shape=[plane] * 3,
        compiler_params=params,
        name="planes",
    )(obs, up)

    rising = [(i, i + 1) for i in range(slabs - 1)]
    falling = [(i + 1, i) for i in range(slabs - 1)]
    to_east = [(i, (i + 1) % groups) for i in range(groups)]
    to_west = [((i + 1) % groups, i) for i in range(groups)]
    f_below = lax.ppermute(f_top, "gz", rising)
    g_above = lax.ppermute(g_bot, "gz", falling)
    f_first = (1 - obs[:nz]).astype(F32)
    f_west = lax.ppermute((1 - obs[(nx - 1) * nz :]).astype(F32), "xy", to_east)
    side = lax.ppermute(jnp.concatenate([f_first, f_first * east[:nz]], 0), "xy", to_west)
    f_east, g_east = side[:nz], side[nz:]
    f_above = lax.ppermute(f_bot, "gz", falling)

    tables = (te_h, te_l, to_h, to_l, c_h, c_l, lam_a, lam_b, c0)
    ends_shape = jax.ShapeDtypeStruct((slabs, nx + nz, 2 * width), F32)
    modes, ends = pl.pallas_call(
        functools.partial(forward_kernel, nz, slabs),
        grid=(steps,),
        in_specs=[big, before, after, big, after, big, big]
        + [whole(f_west)] * 3 + [line, line]
        + [whole(t) for t in tables],
        out_specs=[
            pl.BlockSpec((nz, nx, ny), lambda i: (0, 0, 0)),
            pl.BlockSpec(ends_shape.shape, lambda i: (0, 0, 0)),
        ],
        out_shape=[jax.ShapeDtypeStruct((nz, nx, ny), F32), ends_shape],
        scratch_shapes=[
            pltpu.VMEM((chunk * nz, ny), F32),
            pltpu.VMEM((ny // 128, nx * nz, 128), F32),
            pltpu.VMEM((nx, ny), F32),
            pltpu.VMEM((nx, ny), F32),
            pltpu.VMEM((2, nz, 8, ny), F32),
        ],
        compiler_params=params,
        name="forward",
    )(obs, obs, obs, east, east, north, up, f_west, f_east, g_east, f_below, g_above, *tables)

    ends = lax.all_to_all(ends, "gz", split_axis=0, concat_axis=0, tiled=True)
    own = pl.pallas_call(
        functools.partial(ends_kernel, nz),
        out_shape=jax.ShapeDtypeStruct((total, 2 * width), F32),
        scratch_shapes=[pltpu.VMEM((total * 8, 2 * width), F32)],
        compiler_params=single,
        name="ends",
    )(ends, lam_pair, part, c0_pair, sum_h, sum_l, sine_h, sine_l)
    found = [own]
    for shift in range(1, groups):
        found.append(lax.ppermute(own, "xy", [((i + shift) % groups, i) for i in range(groups)]))
    solved = pl.pallas_call(
        functools.partial(correct_kernel, nz, groups),
        out_shape=ends_shape,
        scratch_shapes=[pltpu.VMEM((total, 2 * width), F32)],
        compiler_params=single,
        name="correct",
    )(ends, *found, lam_pair, part, mu, c0_pair, sine_h, sine_l)
    solved = lax.all_to_all(solved, "gz", split_axis=0, concat_axis=0, tiled=True)

    tables = (te_h, te_l, ti_h, ti_l, ct_h, ct_l, lam_a, lam_b, c0)
    field = jax.ShapeDtypeStruct((nx * nz, ny), F32)
    outs = pl.pallas_call(
        functools.partial(backward_kernel, nz, slabs),
        grid=(steps,),
        in_specs=[
            pl.BlockSpec((nz, nx, ny), lambda i: (0, 0, 0)),
            pl.BlockSpec(ends_shape.shape, lambda i: (0, 0, 0)),
        ]
        + [big, before, after, big, after, big, big]
        + [whole(f_west)] * 3 + [line, line, line]
        + [whole(t) for t in tables],
        out_specs=[big] * 5,
        out_shape=[field] * 5,
        scratch_shapes=[
            pltpu.VMEM((nx, ny), F32),
            pltpu.VMEM((nx, ny), F32),
            pltpu.VMEM((4, nz, ny), F32),
            pltpu.VMEM((ny // 128, (nx + 2) * nz, 128), F32),
            pltpu.VMEM(((nx + 2) * nz, ny), F32),
            pltpu.VMEM((nx, ny), F32),
            pltpu.VMEM((nx, ny), F32),
        ],
        compiler_params=params,
        name="backward",
    )(modes, solved, obs, obs, obs, east, east, north, up,
      f_west, f_east, g_east, f_below, g_above, f_above, *tables)
    return tuple(o.reshape(nx, nz, ny) for o in outs)


def solution(mesh):
    placed = P("xy", "gz", None)
    return jax.shard_map(
        functools.partial(local, mesh.shape["xy"], mesh.shape["gz"]),
        mesh=mesh,
        in_specs=(placed,) * 4,
        out_specs=(placed,) * 5,
        check_vma=False,
    )
```

```python
import functools

import jax
import jax.numpy as jnp
import ml_dtypes
import numpy as np
from jax import lax
from jax.experimental import pallas as pl
from jax.experimental.pallas import tpu as pltpu
from jax.sharding import PartitionSpec as P

F32 = jnp.float32
BF16 = jnp.bfloat16
VMEM_LIMIT = 24 * 1024 * 1024


def pair_np(table):
    high = table.astype(np.float32).astype(ml_dtypes.bfloat16)
    low = (table - high.astype(np.float64)).astype(np.float32).astype(ml_dtypes.bfloat16)
    return high, low


def north_tables(length):
    half = length // 2
    cell = np.arange(half)[:, None]
    mode = np.arange(half)[None, :]

    def cas(number):
        angle = 2.0 * np.pi * ((cell * number) % length) / length
        return (np.cos(angle) + np.sin(angle)) / np.sqrt(length)

    numbers = np.concatenate([2 * np.arange(half), 2 * np.arange(half) + 1])
    eigen = 4.0 * np.sin(np.pi * numbers / length) ** 2
    return cas(2 * mode), cas(2 * mode + 1), eigen


def east_tables(length):
    modes = np.concatenate([np.arange(0, length, 2), np.arange(1, length, 2)])
    cell = np.arange(length)
    table = np.cos(np.pi * modes[:, None] * (2 * cell[None, :] + 1) / (2 * length)) * np.sqrt(2.0 / length)
    table[0] = np.sqrt(1.0 / length)
    eigen = 4.0 * np.sin(np.pi * modes / (2 * length)) ** 2
    return table, eigen


def sine_table(length):
    index = np.arange(1, length + 1)
    table = np.sqrt(2.0 / (length + 1)) * np.sin(np.pi * np.outer(index, index) / (length + 1))
    eigen = 4.0 * np.sin(np.pi * index / (2 * (length + 1))) ** 2
    return table, eigen


def split(value):
    high = value.astype(BF16)
    return high, (value - high.astype(F32)).astype(BF16)


def dot3(left, right):
    (lh, ll), (rh, rl) = left, right
    dot = functools.partial(jnp.dot, preferred_element_type=F32)
    return dot(lh, rh) + (dot(ll, rh) + dot(lh, rl))


def chebyshev(shift, count):
    values = [jnp.ones_like(shift)]
    step = values[0]
    for n in range(count):
        step = step + shift * values[n]
        values.append(values[n] + step)
    return values


def slab_solve(shift, right):
    count = len(right)
    u = chebyshev(shift, count)
    inverse = 1.0 / u[count]
    lower = [right[0]]
    for k in range(1, count):
        lower.append(lower[-1] + u[k] * right[k])
    upper = [None] * count
    for k in range(count - 2, -1, -1):
        term = u[count - 2 - k] * right[k + 1] if k < count - 2 else right[k + 1]
        upper[k] = term if upper[k + 1] is None else upper[k + 1] + term
    out = []
    for k in range(count):
        value = u[count - 1 - k] * lower[k]
        if upper[k] is not None:
            value = value + u[k] * upper[k]
        out.append(value * inverse)
    return out


def spike_of(shift, count):
    u = chebyshev(shift, count)
    inverse = 1.0 / u[count]
    return [u[count - 1 - k] * inverse for k in range(count)]


def interface_chain(couple, spread, bottoms, tops):
    count = len(bottoms)
    slope = jnp.zeros_like(couple)
    offset = jnp.zeros_like(couple)
    slopes, offsets, inverses, bases = [], [], [], []
    for s in range(count):
        inverse = 1.0 / (1.0 - couple * slope)
        base = (bottoms[s] + couple * offset) * inverse
        slopes.append(slope)
        offsets.append(offset)
        inverses.append(inverse * spread)
        bases.append(base)
        if s < count - 1:
            weight = spread * slope
            slope, offset = (
                couple + weight * spread * inverse,
                tops[s] + spread * offset + weight * base,
            )
    above = jnp.zeros_like(couple)
    lowers, uppers = [None] * count, [None] * count
    for s in range(count - 1, -1, -1):
        lower = bases[s] + inverses[s] * above
        uppers[s] = tops[s] + spread * (slopes[s] * lower + offsets[s]) + couple * above
        lowers[s] = lower
        above = lower
    below = [jnp.zeros_like(couple)] + uppers[:-1]
    above = lowers[1:] + [jnp.zeros_like(couple)]
    return below, above


def get_lanes(ref, rows):
    return jnp.concatenate([ref[n, rows, :] for n in range(ref.shape[0])], 1)


def put_lanes(ref, rows, value, start):
    for n in range(value.shape[1] // 128):
        ref[start + n, rows, :] = value[:, n * 128 : (n + 1) * 128]


def planes_kernel(nz, obs, up, high, low):
    rows = high.shape[0]
    high[...] = (1 - obs[pl.ds(nz - 1, rows, stride=nz), :]).astype(F32)
    fluid = (1 - obs[pl.ds(0, rows, stride=nz), :]).astype(F32)
    low[0] = fluid
    low[1] = fluid * up[pl.ds(0, rows, stride=nz), :]


def north_roll(value, shift):
    return pltpu.roll(value, shift % value.shape[1], 1)


def put_row(value, row, index):
    where = lax.broadcasted_iota(jnp.int32, value.shape, 0) == index
    return jnp.where(where, jnp.broadcast_to(row, value.shape), value)


def below_of(value, row):
    return put_row(pltpu.roll(value, 1, 0), row, 0)


def above_of(value, row):
    return put_row(pltpu.roll(value, value.shape[0] - 1, 0), row, value.shape[0] - 1)


def fluid_of(block):
    return (1 - block).astype(F32)


def stack_left(table):
    high, low = pair_np(table)
    return np.concatenate([high, low], 1), high


def east_dot(left, value):
    high, low = split(value)
    dot = functools.partial(jnp.dot, preferred_element_type=F32)
    return dot(left[0], jnp.concatenate([high, high], 0)) + dot(left[1], low)


def north_forward(value, even, odd):
    half = value.shape[1] // 2
    low, high = value[:, :half], value[:, half:]
    return dot3(split(low + high), even), dot3(split(low - high), odd)


def interior_kernel(
    nz,
    obs, obs_prev, obs_next, east, east_next, north, up,
    te_h, te_l, to_h, to_l, c_hl, c_h,
    modes,
    src, half,
):
    step = pl.program_id(0)
    last = step == pl.num_programs(0) - 1
    chunk = src.shape[0] // nz
    ny = src.shape[1]
    nx = chunk * pl.num_programs(0)

    fluid_prev = jnp.where(step == 0, 0.0, fluid_of(obs_prev[...]))
    flux_after = jnp.where(last, 0.0, fluid_of(obs_next[...]) * east_next[...])
    none = jnp.zeros((1, ny), F32)
    fluid = fluid_of(obs[0:nz, :])
    masked = fluid * fluid_prev * east[0:nz, :]
    for i in range(chunk):
        at = slice(i * nz, (i + 1) * nz)
        if i < chunk - 1:
            nxt = slice((i + 1) * nz, (i + 2) * nz)
            fluid_next = fluid_of(obs[nxt, :])
            flux = fluid_next * east[nxt, :]
        else:
            fluid_next, flux = None, flux_after
        masked_next = fluid * flux
        north_masked = fluid * north_roll(fluid, 1) * north[at, :]
        up_masked = fluid * below_of(fluid, none) * up[at, :]
        src[at, :] = (
            (masked - masked_next)
            + (north_masked - north_roll(north_masked, -1))
            + (up_masked - above_of(up_masked, none))
        )
        fluid, masked = fluid_next, masked_next

    rows = pl.ds(pl.multiple_of(step * chunk * nz, chunk * nz), chunk * nz)
    even, odd = north_forward(src[...], (te_h[...], te_l[...]), (to_h[...], to_l[...]))
    put_lanes(half, rows, even, 0)
    put_lanes(half, rows, odd, ny // 256)

    @pl.when(last)
    def _():
        left = (c_hl[...], c_h[...])
        for k in range(nz):
            modes[k] = east_dot(left, get_lanes(half, pl.ds(k, nx, stride=nz)))


def joined_kernel(
    nz, slabs,
    modes_in, high, low, f_below, low_above, first, side_west, side_east,
    te_h, te_l, to_h, to_l, c_hl, c_h, lam_a, lam_b, c0,
    modes, out,
    bottom, top, acc, edge,
):
    nx, ny = high.shape
    lift = jnp.where(lax.axis_index("gz") == 0, 1.0, 0.0).astype(F32)
    even_table, odd_table = (te_h[...], te_l[...]), (to_h[...], to_l[...])
    lower = low[1] * (f_below[...] + lift)
    upper = -(high[...] * low_above[1])
    west = first[nz : 2 * nz, :] * side_west[...]
    east_end = -(first[2 * nz :, :] * side_east[nz:, :])
    stacked = jnp.concatenate([lower, upper, west, east_end], 0)
    stacked = jnp.concatenate(north_forward(stacked, even_table, odd_table), 1)
    left = (c_hl[...], c_h[...])
    bottom[...] = east_dot(left, stacked[:nx])
    top[...] = east_dot(left, stacked[nx : 2 * nx])
    west, east_end = stacked[2 * nx : 2 * nx + nz], stacked[2 * nx + nz :]
    edge[0] = west + east_end
    edge[1] = west - east_end
    acc[...] = jnp.zeros_like(acc)
    blocks = nx // 8

    def solve(n, carry):
        at = pl.ds(pl.multiple_of(n * 8, 8), 8)
        parity = n // (blocks // 2)
        for lane in range(0, ny, 128):
            lanes = slice(lane, lane + 128)
            shift = lam_a[at, :] + lam_b[:, lanes]
            weight = c0[at, :]
            right = []
            for k in range(nz):
                q = jnp.broadcast_to(edge[parity, pl.ds(k, 1), lanes], weight.shape)
                right.append(modes_in[k, at, lanes] + weight * q)
            right[0] = right[0] + bottom[at, lanes]
            right[nz - 1] = right[nz - 1] + top[at, lanes]
            for k in range(nz):
                modes[k, at, lanes] = right[k]
            local = slab_solve(shift, right)
            bottom[at, lanes] = local[0]
            top[at, lanes] = local[nz - 1]
            for k in range(nz):
                acc[parity, k, :, lanes] += weight * local[k]
        return carry

    lax.fori_loop(0, blocks, solve, 0)
    even = [jnp.sum(acc[0, k], axis=0, keepdims=True) for k in range(nz)]
    odd = [jnp.sum(acc[1, k], axis=0, keepdims=True) for k in range(nz)]
    west = jnp.concatenate([e + o for e, o in zip(even, odd)], 0)
    east_end = jnp.concatenate([e - o for e, o in zip(even, odd)], 0)
    width = ny // slabs
    hx = nx // 2
    for j in range(slabs):
        lanes = slice(j * width, (j + 1) * width)
        out[j, 0:hx, :] = jnp.concatenate([bottom[:hx, lanes], bottom[hx:, lanes]], 1)
        out[j, hx:nx, :] = jnp.concatenate([top[:hx, lanes], top[hx:, lanes]], 1)
        out[j, nx : nx + nz, :] = jnp.concatenate([west[:, lanes], east_end[:, lanes]], 1)


def swap_halves(value):
    width = value.shape[1] // 2
    return jnp.concatenate([value[:, width:], value[:, :width]], 1)


def in_first_half(value):
    return lax.broadcasted_iota(jnp.int32, value.shape, 1) < value.shape[1] // 2


def ends_kernel(nz, ends, lam_a, lam_b, c0, sum_h, sum_l, sine_h, sine_l, out, acc):
    slabs = ends.shape[0]
    nx = ends.shape[1] - nz
    hx = nx // 2
    shift = lam_a[...] + lam_b[lax.axis_index("gz")][0:1, :]
    spike = spike_of(shift, nz)
    below, above = interface_chain(
        spike[0],
        spike[nz - 1],
        [ends[s, 0:hx, :] for s in range(slabs)],
        [ends[s, hx:nx, :] for s in range(slabs)],
    )
    weight = c0[...]
    spike = [weight * g for g in spike]
    for s in range(slabs):
        for k in range(nz):
            term = spike[k] * below[s] + spike[nz - 1 - k] * above[s]
            row = (s * nz + k) * 8
            acc[row : row + 8, :] = jnp.sum(term.reshape(hx // 8, 8, term.shape[1]), axis=0)
    both = dot3((sum_h[...], sum_l[...]), split(acc[...]))
    other = swap_halves(both)
    both = jnp.where(in_first_half(both), both + other, other - both)
    rows = jnp.concatenate([ends[s, nx : nx + nz, :] for s in range(slabs)], 0)
    out[...] = both + dot3((sine_h[...], sine_l[...]), split(rows))


def power(value, count):
    result = None
    while count:
        if count & 1:
            result = value if result is None else result * value
        count >>= 1
        if count:
            value = value * value
    return result


def correct_kernel(nz, groups, ends, *rest):
    found = rest[:groups]
    lam_a, lam_b, mu, c0, sine_h, sine_l, out, jump = rest[groups:]
    slabs, width = ends.shape[0], ends.shape[2] // 2
    nx = ends.shape[1] - nz
    hx = nx // 2
    row_b = lam_b[lax.axis_index("gz")][0:1, :]
    shift = mu[:, :width] + row_b[:, :width]
    cosh = 1.0 + 0.5 * shift
    sinh = jnp.sqrt(shift + 0.25 * shift * shift)
    grow = cosh + sinh
    decay = 1.0 / grow
    far = power(decay, nx)
    far2 = far * far
    scale = 1.0 / (sinh * (1.0 - far2))
    self2 = ((1.0 + far2) + (decay + far2 * grow)) * scale
    cross2 = 2.0 * (1.0 + cosh) * far * scale
    inverse = {}
    for f in range(groups):
        key = min(f, groups - f)
        if key not in inverse:
            inverse[key] = 1.0 / (1.0 + self2 - float(np.cos(2 * np.pi * f / groups)) * cross2)
    kernel = {}
    for n in range(groups // 2 + 1):
        value = None
        for f in range(groups):
            factor = float(np.cos(2 * np.pi * f * n / groups)) / groups
            term = factor * inverse[min(f, groups - f)]
            value = term if value is None else value + term
        kernel[n] = value
    jumps_east, jumps_west = None, None
    for n in range(groups):
        nxt = (n + 1) % groups
        t = found[n][:, width:] - found[nxt][:, :width]
        east_term = kernel[min(n, groups - n)] * t
        west_term = kernel[min(nxt, groups - nxt)] * t
        jumps_east = east_term if jumps_east is None else jumps_east + east_term
        jumps_west = west_term if jumps_west is None else jumps_west + west_term
    both = dot3((sine_h[...], sine_l[...]), split(jnp.concatenate([jumps_west, jumps_east], 1)))
    other = swap_halves(both)
    jump[...] = jnp.where(in_first_half(both), both - other, both + other)
    shift = lam_a[...] + row_b
    spike = spike_of(shift, nz)
    weight = c0[...]
    loads = [weight * g for g in spike]
    bottoms, tops = [], []
    for s in range(slabs):
        low, high = ends[s, 0:hx, :], ends[s, hx:nx, :]
        for k in range(nz):
            q = jump[s * nz + k : s * nz + k + 1, :]
            low = low + loads[k] * q
            high = high + loads[nz - 1 - k] * q
        bottoms.append(low)
        tops.append(high)
    below, above = interface_chain(spike[0], spike[nz - 1], bottoms, tops)
    for s in range(slabs):
        out[s, 0:hx, :] = below[s]
        out[s, hx:nx, :] = above[s]
        out[s, nx : nx + nz, :] = both[s * nz : (s + 1) * nz, :]


def backward_kernel(
    nz, slabs, chunk,
    modes, solved,
    obs, east, north, up,
    side_west, side_east, f_below, low_above,
    te_h, te_l, ti_h, ti_l, ct_hl, ct_h, lam_a, lam_b, c0,
    out_east, out_north, out_up, out_p, out_r,
    below, above, found, half, press, p_below, p_above,
):
    step = pl.program_id(0)
    last = step == pl.num_programs(0) - 1
    ny = obs.shape[1]
    hy = ny // 2
    nx = chunk * pl.num_programs(0)
    lift = jnp.where(lax.axis_index("gz") == 0, 1.0, 0.0).astype(F32)

    @pl.when(step == 0)
    def _():
        width = ny // slabs
        west, east_end = [], []
        hx = nx // 2
        for j in range(slabs):
            lanes = slice(j * width, (j + 1) * width)
            below[:hx, lanes] = solved[j, 0:hx, :width]
            below[hx:, lanes] = solved[j, 0:hx, width:]
            above[:hx, lanes] = solved[j, hx:nx, :width]
            above[hx:, lanes] = solved[j, hx:nx, width:]
            west.append(solved[j, nx : nx + nz, :width])
            east_end.append(solved[j, nx : nx + nz, width:])
        west = jnp.concatenate(west, 1)
        east_end = jnp.concatenate(east_end, 1)
        found[2] = west
        found[3] = east_end
        found[0] = west - east_end
        found[1] = west + east_end
        blocks = nx // 8

        def solve(n, carry):
            at = pl.ds(pl.multiple_of(n * 8, 8), 8)
            parity = n // (blocks // 2)
            for lane in range(0, ny, 128):
                lanes = slice(lane, lane + 128)
                shift = lam_a[at, :] + lam_b[:, lanes]
                weight = c0[at, :]
                right = []
                for k in range(nz):
                    q = jnp.broadcast_to(found[parity, pl.ds(k, 1), lanes], weight.shape)
                    right.append(modes[k, at, lanes] + weight * q)
                right[0] = right[0] + below[at, lanes]
                right[nz - 1] = right[nz - 1] + above[at, lanes]
                local = slab_solve(shift, right)
                for k in range(nz):
                    modes[k, at, lanes] = local[k]
            return carry

        lax.fori_loop(0, blocks, solve, 0)
        left = (ct_hl[...], ct_h[...])
        for k in range(nz):
            put_lanes(half, pl.ds(nz + k, nx, stride=nz), east_dot(left, modes[k]), 0)
        first, final = slice(nz, 2 * nz), slice(nx * nz, (nx + 1) * nz)
        put_lanes(half, slice(0, nz), get_lanes(half, first) + found[2], 0)
        put_lanes(half, slice((nx + 1) * nz, (nx + 2) * nz), get_lanes(half, final) - found[3], 0)

        def north_back(value):
            even = dot3(split(value[:, :hy]), (te_h[...], te_l[...]))
            odd = dot3(split(value[:, hy:]), (ti_h[...], ti_l[...]))
            return even + odd, even - odd

        both = jnp.concatenate([east_dot(left, below[...]), east_dot(left, above[...])], 0)
        both = jnp.concatenate(north_back(both), 1)
        p_below[...] = both[:nx]
        p_above[...] = both[nx:]
        size = 32 * nz

        def back(n, carry):
            at = pl.ds(pl.multiple_of(n * size, size), size)
            press[at, :hy], press[at, hy:] = north_back(get_lanes(half, at))
            return carry

        lax.fori_loop(0, nx * nz // size, back, 0)
        at = slice(nx * nz, (nx + 2) * nz)
        press[at, :hy], press[at, hy:] = north_back(get_lanes(half, at))

    base = step * chunk

    def cells(x):
        return pl.ds(pl.multiple_of(x * nz, nz), nz)

    fluid_prev = jnp.where(step == 0, side_west[...], fluid_of(obs[cells(jnp.maximum(base - 1, 0)), :]))
    after = cells(jnp.minimum(base + chunk, nx - 1))
    after_fluid = jnp.where(last, side_east[0:nz, :], fluid_of(obs[after, :]))
    after_flux = jnp.where(last, side_east[nz:, :], fluid_of(obs[after, :]) * east[after, :])

    fluid = fluid_of(obs[cells(base), :])
    p = press[cells(base + 1), :]
    east_done = fluid * fluid_prev * (east[cells(base), :] - (p - press[cells(base), :]))
    for i in range(chunk):
        at = slice(i * nz, (i + 1) * nz)
        own = cells(base + i)
        line = pl.ds(base + i, 1)
        if i < chunk - 1:
            nxt = cells(base + i + 1)
            fluid_next = fluid_of(obs[nxt, :])
            flux = fluid_next * east[nxt, :]
        else:
            fluid_next, flux = after_fluid, after_flux
        p_next = press[cells(base + i + 2), :]
        east_next_done = fluid * (flux - fluid_next * (p_next - p))
        north_done = fluid * north_roll(fluid, 1) * (north[own, :] - (p - north_roll(p, 1)))
        fluid_below = below_of(fluid, f_below[line, :] + lift)
        up_done = fluid * fluid_below * (up[own, :] - (p - below_of(p, p_below[line, :])))
        edge = fluid[nz - 1 : nz, :] * (
            low_above[1, line, :] - low_above[0, line, :] * (p_above[line, :] - p[nz - 1 : nz, :])
        )
        out_east[at, :] = east_done
        out_north[at, :] = north_done
        out_up[at, :] = up_done
        out_p[at, :] = p
        out_r[at, :] = (
            (east_done - east_next_done)
            + (north_done - north_roll(north_done, -1))
            + (up_done - above_of(up_done, edge))
        )
        fluid, p, east_done = fluid_next, p_next, east_next_done


def local(groups, slabs, east_velocity, north_velocity, upward_velocity, obstacle):
    nx, nz, ny = east_velocity.shape
    total = slabs * nz
    width = ny // slabs
    flat = [a.reshape(nx * nz, ny) for a in (obstacle, east_velocity, north_velocity, upward_velocity)]
    obs, east, north, up = flat

    even_np, odd_np, lam_b_np = north_tables(ny)
    block_np, lam_a_np = east_tables(nx)
    sine_np, mu_np = sine_table(total)
    te_h, te_l = pair_np(even_np)
    to_h, to_l = pair_np(odd_np)
    ti_h, ti_l = pair_np(odd_np.T.copy())
    c_hl, c_h = stack_left(block_np)
    ct_hl, ct_h = stack_left(block_np.T.copy())
    sine_h, sine_l = pair_np(sine_np)
    sum_h, sum_l = (np.repeat(t, 8, axis=1) for t in (sine_h, sine_l))
    lam_a = np.repeat(lam_a_np[:, None], 128, 1).astype(np.float32)
    c0 = np.repeat(block_np[:, :1], 128, 1).astype(np.float32)
    lam_b = np.repeat(lam_b_np[None], 8, 0).astype(np.float32)
    part = np.tile(lam_b_np.reshape(slabs, 1, width), (1, 8, 2)).astype(np.float32)

    def paired(column):
        return np.repeat(column.reshape(2, nx // 2).T, width, 1).astype(np.float32)

    lam_pair, c0_pair = paired(lam_a_np), paired(block_np[:, 0])
    mu = np.repeat(mu_np[:, None], 128, 1).astype(np.float32)

    chunk = 16
    steps = nx // chunk
    params = pltpu.CompilerParams(vmem_limit_bytes=VMEM_LIMIT, dimension_semantics=("arbitrary",))
    single = pltpu.CompilerParams(vmem_limit_bytes=VMEM_LIMIT)
    big = pl.BlockSpec((chunk * nz, ny), lambda i: (i, 0))
    before = pl.BlockSpec((nz, ny), lambda i: (jnp.maximum(i * chunk - 1, 0), 0))
    after = pl.BlockSpec((nz, ny), lambda i: (jnp.minimum(i * chunk + chunk, nx - 1), 0))
    kept = pl.BlockSpec(memory_space=pltpu.VMEM)
    modes_shape = jax.ShapeDtypeStruct((nz, nx, ny), F32)
    cells = nx * nz * ny

    high, low = pl.pallas_call(
        functools.partial(planes_kernel, nz),
        grid=(ny // 128,),
        in_specs=[pl.BlockSpec((nx * nz, 128), lambda i: (0, i))] * 2,
        out_specs=[
            pl.BlockSpec((nx, 128), lambda i: (0, i)),
            pl.BlockSpec((2, nx, 128), lambda i: (0, 0, i)),
        ],
        out_shape=[jax.ShapeDtypeStruct((nx, ny), F32), jax.ShapeDtypeStruct((2, nx, ny), F32)],
        compiler_params=params,
        name="planes",
    )(obs, up)

    rising = [(i, i + 1) for i in range(slabs - 1)]
    falling = [(i + 1, i) for i in range(slabs - 1)]
    to_east = [(i, (i + 1) % groups) for i in range(groups)]
    to_west = [((i + 1) % groups, i) for i in range(groups)]
    f_first = (1 - obs[:nz]).astype(F32)
    f_final = (1 - obs[(nx - 1) * nz :]).astype(F32)
    first = jnp.concatenate([f_first, f_first * east[:nz], f_final], 0)
    side_west = lax.ppermute(first[2 * nz :], "xy", to_east)
    side_east = lax.ppermute(first[: 2 * nz], "xy", to_west)
    f_below = lax.ppermute(high, "gz", rising)
    low_above = lax.ppermute(low, "gz", falling)

    tables = (te_h, te_l, to_h, to_l, c_hl, c_h)
    modes = pl.pallas_call(
        functools.partial(interior_kernel, nz),
        grid=(steps,),
        in_specs=[big, before, after, big, after, big, big] + [kept] * 6,
        out_specs=kept,
        out_shape=modes_shape,
        scratch_shapes=[
            pltpu.VMEM((chunk * nz, ny), F32),
            pltpu.VMEM((ny // 128, nx * nz, 128), F32),
        ],
        compiler_params=params,
        cost_estimate=pl.CostEstimate(flops=cells * 2 * 3 * (ny // 2 + nx), bytes_accessed=20 * cells, transcendentals=0),
        name="interior",
    )(obs, obs, obs, east, east, north, up, *tables)
    ends_shape = jax.ShapeDtypeStruct((slabs, nx + nz, 2 * width), F32)
    modes, ends = pl.pallas_call(
        functools.partial(joined_kernel, nz, slabs),
        in_specs=[kept] * 17,
        out_specs=[kept] * 2,
        out_shape=[modes_shape, ends_shape],
        scratch_shapes=[
            pltpu.VMEM((nx, ny), F32),
            pltpu.VMEM((nx, ny), F32),
            pltpu.VMEM((2, nz, 8, ny), F32),
            pltpu.VMEM((2, nz, ny), F32),
        ],
        input_output_aliases={0: 0},
        compiler_params=single,
        name="joined",
    )(modes, high, low, f_below, low_above, first, side_west, side_east, *tables, lam_a, lam_b, c0)

    ends = lax.all_to_all(ends, "gz", split_axis=0, concat_axis=0, tiled=True)
    own = pl.pallas_call(
        functools.partial(ends_kernel, nz),
        out_shape=jax.ShapeDtypeStruct((total, 2 * width), F32),
        scratch_shapes=[pltpu.VMEM((total * 8, 2 * width), F32)],
        compiler_params=single,
        name="ends",
    )(ends, lam_pair, part, c0_pair, sum_h, sum_l, sine_h, sine_l)
    found = [own]
    for shift in range(1, groups):
        found.append(lax.ppermute(own, "xy", [((i + shift) % groups, i) for i in range(groups)]))
    solved = pl.pallas_call(
        functools.partial(correct_kernel, nz, groups),
        out_shape=ends_shape,
        scratch_shapes=[pltpu.VMEM((total, 2 * width), F32)],
        compiler_params=single,
        name="correct",
    )(ends, *found, lam_pair, part, mu, c0_pair, sine_h, sine_l)
    solved = lax.all_to_all(solved, "gz", split_axis=0, concat_axis=0, tiled=True)

    tables = (te_h, te_l, ti_h, ti_l, ct_hl, ct_h, lam_a, lam_b, c0)
    field = jax.ShapeDtypeStruct((nx * nz, ny), F32)
    outs = pl.pallas_call(
        functools.partial(backward_kernel, nz, slabs, chunk),
        grid=(steps,),
        in_specs=[kept] * (10 + len(tables)),
        out_specs=[big] * 5,
        out_shape=[field] * 5,
        scratch_shapes=[
            pltpu.VMEM((nx, ny), F32),
            pltpu.VMEM((nx, ny), F32),
            pltpu.VMEM((4, nz, ny), F32),
            pltpu.VMEM((ny // 128, (nx + 2) * nz, 128), F32),
            pltpu.VMEM(((nx + 2) * nz, ny), F32),
            pltpu.VMEM((nx, ny), F32),
            pltpu.VMEM((nx, ny), F32),
        ],
        compiler_params=params,
        name="backward",
    )(modes, solved, obs, east, north, up, side_west, side_east, f_below, low_above, *tables)
    return tuple(o.reshape(nx, nz, ny) for o in outs)


def solution(mesh):
    placed = P("xy", "gz", None)
    return jax.shard_map(
        functools.partial(local, mesh.shape["xy"], mesh.shape["gz"]),
        mesh=mesh,
        in_specs=(placed,) * 4,
        out_specs=(placed,) * 5,
        check_vma=False,
    )
```

```python
import functools

import jax
import jax.numpy as jnp
import ml_dtypes
import numpy as np
from jax import lax
from jax.experimental import pallas as pl
from jax.experimental.pallas import tpu as pltpu
from jax.sharding import PartitionSpec as P

F32 = jnp.float32
BF16 = jnp.bfloat16
VMEM_LIMIT = 24 * 1024 * 1024
LOAD_LIMIT = 48 * 1024 * 1024


def pair_np(table):
    high = table.astype(np.float32).astype(ml_dtypes.bfloat16)
    low = (table - high.astype(np.float64)).astype(np.float32).astype(ml_dtypes.bfloat16)
    return high, low


def north_tables(length):
    half = length // 2
    cell = np.arange(half)[:, None]
    mode = np.arange(half)[None, :]

    def cas(number):
        angle = 2.0 * np.pi * ((cell * number) % length) / length
        return (np.cos(angle) + np.sin(angle)) / np.sqrt(length)

    numbers = np.concatenate([2 * np.arange(half), 2 * np.arange(half) + 1])
    eigen = 4.0 * np.sin(np.pi * numbers / length) ** 2
    return cas(2 * mode), cas(2 * mode + 1), eigen


def east_tables(length):
    modes = np.concatenate([np.arange(0, length, 2), np.arange(1, length, 2)])
    cell = np.arange(length)
    table = np.cos(np.pi * modes[:, None] * (2 * cell[None, :] + 1) / (2 * length)) * np.sqrt(2.0 / length)
    table[0] = np.sqrt(1.0 / length)
    eigen = 4.0 * np.sin(np.pi * modes / (2 * length)) ** 2
    return table, eigen


def sine_table(length):
    index = np.arange(1, length + 1)
    table = np.sqrt(2.0 / (length + 1)) * np.sin(np.pi * np.outer(index, index) / (length + 1))
    eigen = 4.0 * np.sin(np.pi * index / (2 * (length + 1))) ** 2
    return table, eigen


def split(value):
    high = value.astype(BF16)
    return high, (value - high.astype(F32)).astype(BF16)


def dot3(left, right):
    (lh, ll), (rh, rl) = left, right
    dot = functools.partial(jnp.dot, preferred_element_type=F32)
    return dot(lh, rh) + (dot(ll, rh) + dot(lh, rl))


def chebyshev(shift, count):
    values = [jnp.ones_like(shift)]
    step = values[0]
    for n in range(count):
        step = step + shift * values[n]
        values.append(values[n] + step)
    return values


def slab_solve(shift, right):
    count = len(right)
    u = chebyshev(shift, count)
    inverse = 1.0 / u[count]
    lower = [right[0]]
    for k in range(1, count):
        lower.append(lower[-1] + u[k] * right[k])
    upper = [None] * count
    for k in range(count - 2, -1, -1):
        term = u[count - 2 - k] * right[k + 1] if k < count - 2 else right[k + 1]
        upper[k] = term if upper[k + 1] is None else upper[k + 1] + term
    out = []
    for k in range(count):
        value = u[count - 1 - k] * lower[k]
        if upper[k] is not None:
            value = value + u[k] * upper[k]
        out.append(value * inverse)
    return out


def spike_of(shift, count):
    u = chebyshev(shift, count)
    inverse = 1.0 / u[count]
    return [u[count - 1 - k] * inverse for k in range(count)]


def interface_chain(couple, spread, bottoms, tops):
    count = len(bottoms)
    slope = jnp.zeros_like(couple)
    offset = jnp.zeros_like(couple)
    slopes, offsets, inverses, bases = [], [], [], []
    for s in range(count):
        inverse = 1.0 / (1.0 - couple * slope)
        base = (bottoms[s] + couple * offset) * inverse
        slopes.append(slope)
        offsets.append(offset)
        inverses.append(inverse * spread)
        bases.append(base)
        if s < count - 1:
            weight = spread * slope
            slope, offset = (
                couple + weight * spread * inverse,
                tops[s] + spread * offset + weight * base,
            )
    above = jnp.zeros_like(couple)
    lowers, uppers = [None] * count, [None] * count
    for s in range(count - 1, -1, -1):
        lower = bases[s] + inverses[s] * above
        uppers[s] = tops[s] + spread * (slopes[s] * lower + offsets[s]) + couple * above
        lowers[s] = lower
        above = lower
    below = [jnp.zeros_like(couple)] + uppers[:-1]
    above = lowers[1:] + [jnp.zeros_like(couple)]
    return below, above


def get_lanes(ref, rows):
    return jnp.concatenate([ref[n, rows, :] for n in range(ref.shape[0])], 1)


def put_lanes(ref, rows, value, start):
    for n in range(value.shape[1] // 128):
        ref[start + n, rows, :] = value[:, n * 128 : (n + 1) * 128]


def load_kernel(nz, obs, up_in, east, fluid, up, high, low, side, final, raw, line, sems):
    parts = raw.shape[0]
    rows = high.shape[0]
    copies = []
    for n in range(parts):
        lanes = slice(n * 128, (n + 1) * 128)
        copies.append(
            (
                pltpu.make_async_copy(obs.at[:, lanes], raw.at[n], sems.at[n]),
                pltpu.make_async_copy(up_in.at[:, lanes], up.at[n], sems.at[parts + n]),
            )
        )
        for copy in copies[-1]:
            copy.start()
    edge = pltpu.make_async_copy(east.at[0:nz, :], line, sems.at[2 * parts])
    edge.start()
    edge.wait()
    for n, (flags, speed) in enumerate(copies):
        lanes = slice(n * 128, (n + 1) * 128)
        flags.wait()
        fluid[n] = fluid_of(raw[n])
        high[:, lanes] = fluid[n, pl.ds(nz - 1, rows, stride=nz), :]
        bottom = fluid[n, pl.ds(0, rows, stride=nz), :]
        low[0, :, lanes] = bottom
        first = fluid[n, 0:nz, :]
        side[0:nz, lanes] = first
        side[nz : 2 * nz, lanes] = first * line[:, lanes]
        final[:, lanes] = fluid[n, (rows - 1) * nz : rows * nz, :]
        speed.wait()
        low[1, :, lanes] = bottom * up[n, pl.ds(0, rows, stride=nz), :]


def north_roll(value, shift):
    return pltpu.roll(value, shift % value.shape[1], 1)


def put_row(value, row, index):
    where = lax.broadcasted_iota(jnp.int32, value.shape, 0) == index
    return jnp.where(where, jnp.broadcast_to(row, value.shape), value)


def below_of(value, row):
    return put_row(pltpu.roll(value, 1, 0), row, 0)


def above_of(value, row):
    return put_row(pltpu.roll(value, value.shape[0] - 1, 0), row, value.shape[0] - 1)


def fluid_of(block):
    return (1 - block).astype(F32)


def east_left(table):
    return table, table[:, : table.shape[0]]


def north_pair(tables, index):
    size = tables.shape[1]
    return tables[2 * index * size : (2 * index + 1) * size, :], tables[(2 * index + 1) * size : (2 * index + 2) * size, :]


def east_dot(left, value):
    high, low = split(value)
    dot = functools.partial(jnp.dot, preferred_element_type=F32)
    return dot(left[0], jnp.concatenate([high, high], 0)) + dot(left[1], low)


def north_forward(value, even, odd):
    half = value.shape[1] // 2
    low, high = value[:, :half], value[:, half:]
    return dot3(split(low + high), even), dot3(split(low - high), odd)


def interior_kernel(nz, chunk, fluid, up, east, north, tables, east_table, modes, src, ready, half):
    ny = src.shape[1]
    nx = modes.shape[1]
    count = nx // chunk
    lift = jnp.where(lax.axis_index("gz") == 0, 1.0, 0.0).astype(F32)
    floor = jnp.broadcast_to(lift, (1, ny))
    none = jnp.zeros((1, ny), F32)

    def cells(x):
        return pl.ds(pl.multiple_of(x * nz, nz), nz)

    def stencil(step):
        base = step * chunk
        inside = jnp.where(step > 0, 1.0, 0.0).astype(F32)
        more = jnp.where(step < count - 1, 1.0, 0.0).astype(F32)
        here = get_lanes(fluid, cells(base))
        before = get_lanes(fluid, cells(jnp.maximum(base - 1, 0)))
        masked = here * (before * inside) * east[cells(base), :]
        for i in range(chunk):
            own = cells(base + i)
            nxt = cells(base + i + 1) if i < chunk - 1 else cells(jnp.minimum(base + chunk, nx - 1))
            after = get_lanes(fluid, nxt)
            flux = after * east[nxt, :]
            if i == chunk - 1:
                flux = flux * more
            masked_next = here * flux
            north_masked = here * north_roll(here, 1) * north[own, :]
            up_masked = here * below_of(here, floor) * get_lanes(up, own)
            src[i * nz : (i + 1) * nz, :] = (
                (masked - masked_next)
                + (north_masked - north_roll(north_masked, -1))
                + (up_masked - above_of(up_masked, none))
            )
            here, masked = after, masked_next

    def transform(step):
        rows = pl.ds(pl.multiple_of(step * chunk * nz, chunk * nz), chunk * nz)
        even, odd = north_forward(ready[...], north_pair(tables, 0), north_pair(tables, 1))
        put_lanes(half, rows, even, 0)
        put_lanes(half, rows, odd, ny // 256)

    stencil(0)
    ready[...] = src[...]

    def body(step, carry):
        transform(step - 1)
        stencil(step)
        ready[...] = src[...]
        return carry

    lax.fori_loop(1, count, body, 0)
    transform(count - 1)
    left = east_left(east_table[0])
    for k in range(nz):
        modes[k] = east_dot(left, get_lanes(half, pl.ds(k, nx, stride=nz)))


def joined_kernel(
    nz, slabs,
    modes_in, high, low_above, final, side_east,
    tables, east_table, east_values, lam_b,
    crown, out,
    bottom, top, acc,
):
    nx, ny = high.shape
    leaving = final[...] * side_east[nz:, :]
    stacked = jnp.concatenate([high[...] * low_above[1], leaving], 0)
    stacked = jnp.concatenate(north_forward(stacked, north_pair(tables, 0), north_pair(tables, 1)), 1)
    top[...] = east_dot(east_left(east_table[0]), stacked[:nx])
    leaving = stacked[nx:]
    acc[...] = jnp.zeros_like(acc)
    blocks = nx // 8

    def solve(n, carry):
        at = pl.ds(pl.multiple_of(n * 8, 8), 8)
        parity = n // (blocks // 2)
        for lane in range(0, ny, 128):
            lanes = slice(lane, lane + 128)
            shift = east_values[0, at, :] + lam_b[:, lanes]
            weight = east_values[1, at, :]
            rising = top[at, lanes]
            right = [modes_in[k, at, lanes] for k in range(nz)]
            right[nz - 1] = right[nz - 1] - rising
            crown[at, lanes] = right[nz - 1]
            local = slab_solve(shift, right)
            bottom[at, lanes] = local[0]
            top[at, lanes] = local[nz - 1] + rising
            for k in range(nz):
                acc[parity, k, :, lanes] += weight * local[k]
        return carry

    lax.fori_loop(0, blocks, solve, 0)
    even = [jnp.sum(acc[0, k], axis=0, keepdims=True) for k in range(nz)]
    odd = [jnp.sum(acc[1, k], axis=0, keepdims=True) for k in range(nz)]
    west = jnp.concatenate([e + o for e, o in zip(even, odd)], 0)
    east_end = jnp.concatenate([e - o for e, o in zip(even, odd)], 0) + leaving
    width = ny // slabs
    hx = nx // 2
    for j in range(slabs):
        lanes = slice(j * width, (j + 1) * width)
        out[j, 0:hx, :] = jnp.concatenate([bottom[:hx, lanes], bottom[hx:, lanes]], 1)
        out[j, hx:nx, :] = jnp.concatenate([top[:hx, lanes], top[hx:, lanes]], 1)
        out[j, nx : nx + nz, :] = jnp.concatenate([west[:, lanes], east_end[:, lanes]], 1)


def swap_halves(value):
    width = value.shape[1] // 2
    return jnp.concatenate([value[:, width:], value[:, :width]], 1)


def in_first_half(value):
    return lax.broadcasted_iota(jnp.int32, value.shape, 1) < value.shape[1] // 2


def ends_kernel(nz, ends, final, pairs, lam_b, sums, sines, out, out_more, acc):
    slabs = ends.shape[0]
    nx = ends.shape[1] - nz
    hx = nx // 2
    total = slabs * nz
    shift = pairs[0:hx, :] + lam_b[lax.axis_index("gz")][0:1, :]
    spike = spike_of(shift, nz)
    below, above = interface_chain(
        spike[0],
        spike[nz - 1],
        [ends[s, 0:hx, :] for s in range(slabs)],
        [ends[s, hx:nx, :] for s in range(slabs)],
    )
    weight = pairs[hx:nx, :]
    spike = [weight * g for g in spike]
    for s in range(slabs):
        for k in range(nz):
            term = spike[k] * below[s] + spike[nz - 1 - k] * above[s]
            row = (s * nz + k) * 8
            acc[row : row + 8, :] = jnp.sum(term.reshape(hx // 8, 8, term.shape[1]), axis=0)
    both = dot3((sums[:total, :], sums[total:, :]), split(acc[...]))
    other = swap_halves(both)
    both = jnp.where(in_first_half(both), both + other, other - both)
    rows = jnp.concatenate([ends[s, nx : nx + nz, :] for s in range(slabs)], 0)
    both = both + dot3((sines[:total, :], sines[total:, :]), split(rows))
    out[...] = both
    out_more[:total, :] = both
    lanes = both.shape[1]
    for n in range(final.shape[1] // lanes):
        out_more[total + n * nz : total + (n + 1) * nz, :] = final[:, n * lanes : (n + 1) * lanes]


def power(value, count):
    result = None
    while count:
        if count & 1:
            result = value if result is None else result * value
        count >>= 1
        if count:
            value = value * value
    return result


def correct_kernel(nz, groups, ends, *rest):
    found = rest[:groups]
    pairs, lam_b, sines, out, jump = rest[groups:]
    slabs, width = ends.shape[0], ends.shape[2] // 2
    nx = ends.shape[1] - nz
    hx = nx // 2
    total = slabs * nz
    row_b = lam_b[lax.axis_index("gz")][0:1, :]
    shift = pairs[nx:, :width] + row_b[:, :width]
    cosh = 1.0 + 0.5 * shift
    sinh = jnp.sqrt(shift + 0.25 * shift * shift)
    grow = cosh + sinh
    decay = 1.0 / grow
    far = power(decay, nx)
    far2 = far * far
    scale = 1.0 / (sinh * (1.0 - far2))
    self2 = ((1.0 + far2) + (decay + far2 * grow)) * scale
    cross2 = 2.0 * (1.0 + cosh) * far * scale
    inverse = {}
    for f in range(groups):
        key = min(f, groups - f)
        if key not in inverse:
            inverse[key] = 1.0 / (1.0 + self2 - float(np.cos(2 * np.pi * f / groups)) * cross2)
    kernel = {}
    for n in range(groups // 2 + 1):
        value = None
        for f in range(groups):
            factor = float(np.cos(2 * np.pi * f * n / groups)) / groups
            term = factor * inverse[min(f, groups - f)]
            value = term if value is None else value + term
        kernel[n] = value
    jumps_east, jumps_west = None, None
    for n in range(groups):
        nxt = (n + 1) % groups
        t = found[n][:total, width:] - found[nxt][:total, :width]
        east_term = kernel[min(n, groups - n)] * t
        west_term = kernel[min(nxt, groups - nxt)] * t
        jumps_east = east_term if jumps_east is None else jumps_east + east_term
        jumps_west = west_term if jumps_west is None else jumps_west + west_term
    both = dot3((sines[:total, :], sines[total:, :]), split(jnp.concatenate([jumps_west, jumps_east], 1)))
    other = swap_halves(both)
    jump[...] = jnp.where(in_first_half(both), both - other, both + other)
    shift = pairs[0:hx, :] + row_b
    spike = spike_of(shift, nz)
    weight = pairs[hx:nx, :]
    loads = [weight * g for g in spike]
    bottoms, tops = [], []
    for s in range(slabs):
        low, high = ends[s, 0:hx, :], ends[s, hx:nx, :]
        for k in range(nz):
            q = jump[s * nz + k : s * nz + k + 1, :]
            low = low + loads[k] * q
            high = high + loads[nz - 1 - k] * q
        bottoms.append(low)
        tops.append(high)
    below, above = interface_chain(spike[0], spike[nz - 1], bottoms, tops)
    for s in range(slabs):
        out[s, 0:hx, :] = below[s]
        out[s, hx:nx, :] = above[s]
        out[s, nx : nx + nz, :] = both[s * nz : (s + 1) * nz, :]


def backward_kernel(
    nz, slabs, chunk,
    modes, crown, solved,
    obs, up, east, north,
    from_west, side_east, f_below, low, low_above,
    tables, east_table, east_values, lam_b,
    out_east, out_north, out_up, out_p, out_r,
    work, below, above, found, half, press, coming, p_below, p_above,
):
    step = pl.program_id(0)
    last = step == pl.num_programs(0) - 1
    ny = east.shape[1]
    hy = ny // 2
    nx = chunk * pl.num_programs(0)
    size = chunk * nz
    lift = jnp.where(lax.axis_index("gz") == 0, 1.0, 0.0).astype(F32)

    def north_back(value):
        even = dot3(split(value[:, :hy]), north_pair(tables, 0))
        odd = dot3(split(value[:, hy:]), north_pair(tables, 2))
        return even + odd, even - odd

    @pl.when(step == 0)
    def _():
        width = ny // slabs
        west, east_end = [], []
        hx = nx // 2
        for j in range(slabs):
            lanes = slice(j * width, (j + 1) * width)
            below[:hx, lanes] = solved[j, 0:hx, :width]
            below[hx:, lanes] = solved[j, 0:hx, width:]
            above[:hx, lanes] = solved[j, hx:nx, :width]
            above[hx:, lanes] = solved[j, hx:nx, width:]
            west.append(solved[j, nx : nx + nz, :width])
            east_end.append(solved[j, nx : nx + nz, width:])
        west = jnp.concatenate(west, 1)
        east_end = jnp.concatenate(east_end, 1)
        found[0] = west - east_end
        found[1] = west + east_end
        blocks = nx // 8

        def solve(n, carry):
            at = pl.ds(pl.multiple_of(n * 8, 8), 8)
            parity = n // (blocks // 2)
            for lane in range(0, ny, 128):
                lanes = slice(lane, lane + 128)
                shift = east_values[0, at, :] + lam_b[:, lanes]
                weight = east_values[1, at, :]
                right = []
                for k in range(nz):
                    q = jnp.broadcast_to(found[parity, pl.ds(k, 1), lanes], weight.shape)
                    plane = modes[k, at, lanes] if k < nz - 1 else crown[at, lanes]
                    right.append(plane + weight * q)
                right[0] = right[0] + below[at, lanes]
                right[nz - 1] = right[nz - 1] + above[at, lanes]
                local = slab_solve(shift, right)
                for k in range(nz):
                    work[k, at, lanes] = local[k]
            return carry

        lax.fori_loop(0, blocks, solve, 0)
        left = east_left(east_table[1])
        for k in range(nz):
            put_lanes(half, pl.ds(nz + k, nx, stride=nz), east_dot(left, work[k]), 0)
        first, final = slice(nz, 2 * nz), slice(nx * nz, (nx + 1) * nz)
        put_lanes(half, slice(0, nz), get_lanes(half, first) + west, 0)
        put_lanes(half, slice((nx + 1) * nz, (nx + 2) * nz), get_lanes(half, final) - east_end, 0)
        both = jnp.concatenate(
            [east_dot(left, below[...]), east_dot(left, above[...]), get_lanes(half, slice(0, size + nz))], 0
        )
        both = jnp.concatenate(north_back(both), 1)
        p_below[...] = both[:nx] - f_below[...] * low[1]
        p_above[...] = both[nx : 2 * nx]
        press[...] = both[2 * nx :]

    base = step * chunk

    def cells(x):
        return pl.ds(pl.multiple_of(x * nz, nz), nz)

    rows = pl.ds(pl.multiple_of((base + chunk + 1) * nz, nz), size)
    coming[:, :hy], coming[:, hy:] = north_back(get_lanes(half, rows))

    lanes = from_west.shape[1]
    total = from_west.shape[0] - nz * (ny // lanes)
    side_west = jnp.concatenate(
        [from_west[total + n * nz : total + (n + 1) * nz, :] for n in range(ny // lanes)], 1
    )
    here = fluid_of(obs[cells(base), :])
    before = fluid_of(obs[cells(jnp.maximum(base - 1, 0)), :])
    before = jnp.where(step == 0, side_west, before)
    after_row = cells(jnp.minimum(base + chunk, nx - 1))
    after_fluid = fluid_of(obs[after_row, :])
    after_flux = jnp.where(last, side_east[nz:, :], after_fluid * east[after_row, :])
    after_fluid = jnp.where(last, side_east[0:nz, :], after_fluid)

    p = press[nz : 2 * nz, :]
    first_flux = here * before * east[cells(base), :]
    p_before = press[0:nz, :] - jnp.where(step == 0, 1.0, 0.0).astype(F32) * first_flux
    east_done = first_flux - here * before * (p - p_before)
    for i in range(chunk):
        at = slice(i * nz, (i + 1) * nz)
        own = cells(base + i)
        line = pl.ds(base + i, 1)
        if i < chunk - 1:
            nxt = cells(base + i + 1)
            after = fluid_of(obs[nxt, :])
            flux = after * east[nxt, :]
            p_next = press[(i + 2) * nz : (i + 3) * nz, :]
        else:
            after, flux = after_fluid, after_flux
            p_next = coming[0:nz, :] + jnp.where(last, 1.0, 0.0).astype(F32) * (here * flux)
        east_next_done = here * (flux - after * (p_next - p))
        north_done = here * north_roll(here, 1) * (north[own, :] - (p - north_roll(p, 1)))
        fluid_below = below_of(here, f_below[line, :] + lift)
        up_done = here * fluid_below * (up[own, :] - (p - below_of(p, p_below[line, :])))
        edge = here[nz - 1 : nz, :] * (
            low_above[1, line, :] - low_above[0, line, :] * (p_above[line, :] - p[nz - 1 : nz, :])
        )
        out_east[at, :] = east_done
        out_north[at, :] = north_done
        out_up[at, :] = up_done
        out_p[at, :] = p
        out_r[at, :] = (
            (east_done - east_next_done)
            + (north_done - north_roll(north_done, -1))
            + (up_done - above_of(up_done, edge))
        )
        here, p, east_done = after, p_next, east_next_done
    press[0:nz, :] = press[size : size + nz, :]
    press[nz:, :] = coming[...]


def local(groups, slabs, east_velocity, north_velocity, upward_velocity, obstacle):
    nx, nz, ny = east_velocity.shape
    total = slabs * nz
    width = ny // slabs
    flat = [a.reshape(nx * nz, ny) for a in (obstacle, east_velocity, north_velocity, upward_velocity)]
    obs, east, north, up_in = flat

    even_np, odd_np, lam_b_np = north_tables(ny)
    block_np, lam_a_np = east_tables(nx)
    sine_np, mu_np = sine_table(total)
    tables = np.concatenate([*pair_np(even_np), *pair_np(odd_np), *pair_np(odd_np.T)], 0)
    east_table = np.stack([np.concatenate(pair_np(t), 1) for t in (block_np, block_np.T)])
    sines = np.concatenate(pair_np(sine_np), 0)
    sums = np.repeat(sines, 8, axis=1)
    east_values = np.stack([np.repeat(v[:, None], 128, 1) for v in (lam_a_np, block_np[:, 0])]).astype(np.float32)
    lam_b = np.repeat(lam_b_np[None], 8, 0).astype(np.float32)
    part = np.tile(lam_b_np.reshape(slabs, 1, width), (1, 8, 2)).astype(np.float32)

    def paired(column):
        return np.repeat(column.reshape(2, nx // 2).T, width, 1)

    pairs = np.concatenate(
        [paired(lam_a_np), paired(block_np[:, 0]), np.repeat(mu_np[:, None], 2 * width, 1)], 0
    ).astype(np.float32)

    chunk = 16
    steps = nx // chunk
    lanes = ny // 128
    params = pltpu.CompilerParams(vmem_limit_bytes=VMEM_LIMIT)
    kept = pl.BlockSpec(memory_space=pltpu.VMEM)
    far = pl.BlockSpec(memory_space=pltpu.HBM)

    def array(*shape):
        return jax.ShapeDtypeStruct(shape, F32)

    blocked = array(lanes, nx * nz, 128)
    fluid, up, high, low, side, final = pl.pallas_call(
        functools.partial(load_kernel, nz),
        in_specs=[far] * 3,
        out_specs=[kept] * 6,
        out_shape=[blocked, blocked, array(nx, ny), array(2, nx, ny), array(2 * nz, ny), array(nz, ny)],
        scratch_shapes=[
            pltpu.VMEM((lanes, nx * nz, 128), jnp.int32),
            pltpu.VMEM((nz, ny), F32),
            pltpu.SemaphoreType.DMA((2 * lanes + 1,)),
        ],
        compiler_params=pltpu.CompilerParams(vmem_limit_bytes=LOAD_LIMIT),
        name="load",
    )(obs, up_in, east)

    rising = [(i, i + 1) for i in range(slabs - 1)]
    falling = [(i + 1, i) for i in range(slabs - 1)]
    low_above = lax.ppermute(low, "gz", falling)
    side_east = lax.ppermute(side, "xy", [((i + 1) % groups, i) for i in range(groups)])

    cells = nx * nz * ny
    modes = pl.pallas_call(
        functools.partial(interior_kernel, nz, chunk),
        in_specs=[kept] * 6,
        out_specs=kept,
        out_shape=array(nz, nx, ny),
        scratch_shapes=[
            pltpu.VMEM((chunk * nz, ny), F32),
            pltpu.VMEM((chunk * nz, ny), F32),
            pltpu.VMEM((lanes, nx * nz, 128), F32),
        ],
        compiler_params=params,
        cost_estimate=pl.CostEstimate(flops=cells * 2 * 3 * (ny // 2 + nx), bytes_accessed=20 * cells, transcendentals=0),
        name="interior",
    )(fluid, up, east, north, tables, east_table)
    ends_shape = array(slabs, nx + nz, 2 * width)
    crown, ends = pl.pallas_call(
        functools.partial(joined_kernel, nz, slabs),
        in_specs=[kept] * 9,
        out_specs=[kept] * 2,
        out_shape=[array(nx, ny), ends_shape],
        scratch_shapes=[
            pltpu.VMEM((nx, ny), F32),
            pltpu.VMEM((nx, ny), F32),
            pltpu.VMEM((2, nz, 8, ny), F32),
        ],
        compiler_params=params,
        name="joined",
    )(modes, high, low_above, final, side_east, tables, east_table, east_values, lam_b)

    ends = lax.all_to_all(ends, "gz", split_axis=0, concat_axis=0, tiled=True)
    own, own_more = pl.pallas_call(
        functools.partial(ends_kernel, nz),
        in_specs=[kept] * 6,
        out_specs=[kept] * 2,
        out_shape=[array(total, 2 * width), array(total + nz * ny // (2 * width), 2 * width)],
        scratch_shapes=[pltpu.VMEM((total * 8, 2 * width), F32)],
        compiler_params=params,
        name="ends",
    )(ends, final, pairs, part, sums, sines)
    found = [own]
    for shift in range(1, groups):
        sent = own_more if shift == groups - 1 else own
        found.append(lax.ppermute(sent, "xy", [((i + shift) % groups, i) for i in range(groups)]))
    high, own = lax.optimization_barrier((high, own))
    f_below = lax.ppermute(high, "gz", rising)
    f_below, found[0] = lax.optimization_barrier((f_below, found[0]))
    solved = pl.pallas_call(
        functools.partial(correct_kernel, nz, groups),
        in_specs=[kept] * (groups + 4),
        out_specs=kept,
        out_shape=ends_shape,
        scratch_shapes=[pltpu.VMEM((total, 2 * width), F32)],
        compiler_params=params,
        name="correct",
    )(ends, *found, pairs, part, sines)
    solved = lax.all_to_all(solved, "gz", split_axis=0, concat_axis=0, tiled=True)

    big = pl.BlockSpec((chunk * nz, ny), lambda i: (i, 0))
    outs = pl.pallas_call(
        functools.partial(backward_kernel, nz, slabs, chunk),
        grid=(steps,),
        in_specs=[kept] * 16,
        out_specs=[big] * 5,
        out_shape=[array(nx * nz, ny)] * 5,
        scratch_shapes=[
            pltpu.VMEM((nz, nx, ny), F32),
            pltpu.VMEM((nx, ny), F32),
            pltpu.VMEM((nx, ny), F32),
            pltpu.VMEM((2, nz, ny), F32),
            pltpu.VMEM((lanes, (nx + chunk + 1) * nz, 128), F32),
            pltpu.VMEM(((chunk + 1) * nz, ny), F32),
            pltpu.VMEM((chunk * nz, ny), F32),
            pltpu.VMEM((nx, ny), F32),
            pltpu.VMEM((nx, ny), F32),
        ],
        compiler_params=params,
        name="backward",
    )(modes, crown, solved, obs, up_in, east, north, found[-1], side_east, f_below, low, low_above,
      tables, east_table, east_values, lam_b)
    return tuple(o.reshape(nx, nz, ny) for o in outs)


def solution(mesh):
    placed = P("xy", "gz", None)
    return jax.shard_map(
        functools.partial(local, mesh.shape["xy"], mesh.shape["gz"]),
        mesh=mesh,
        in_specs=(placed,) * 4,
        out_specs=(placed,) * 5,
        check_vma=False,
    )
```

```python
import functools

import jax
import jax.numpy as jnp
import ml_dtypes
import numpy as np
from jax import lax
from jax.experimental import pallas as pl
from jax.experimental.pallas import tpu as pltpu
from jax.sharding import PartitionSpec as P

F32 = jnp.float32
BF16 = jnp.bfloat16
VMEM_LIMIT = 24 * 1024 * 1024
BACK_ROWS = 8
BACK_LIMIT = 28 * 1024 * 1024
LOAD_LIMIT = 48 * 1024 * 1024


def pair_np(table):
    high = table.astype(np.float32).astype(ml_dtypes.bfloat16)
    low = (table - high.astype(np.float64)).astype(np.float32).astype(ml_dtypes.bfloat16)
    return high, low


def north_tables(length):
    half = length // 2
    cell = np.arange(half)[:, None]
    mode = np.arange(half)[None, :]

    def cas(number):
        angle = 2.0 * np.pi * ((cell * number) % length) / length
        return (np.cos(angle) + np.sin(angle)) / np.sqrt(length)

    numbers = np.concatenate([2 * np.arange(half), 2 * np.arange(half) + 1])
    eigen = 4.0 * np.sin(np.pi * numbers / length) ** 2
    return cas(2 * mode), cas(2 * mode + 1), eigen


def east_tables(length):
    modes = np.concatenate([np.arange(0, length, 2), np.arange(1, length, 2)])
    cell = np.arange(length)
    table = np.cos(np.pi * modes[:, None] * (2 * cell[None, :] + 1) / (2 * length)) * np.sqrt(2.0 / length)
    table[0] = np.sqrt(1.0 / length)
    eigen = 4.0 * np.sin(np.pi * modes / (2 * length)) ** 2
    return table, eigen


def sine_table(length):
    index = np.arange(1, length + 1)
    table = np.sqrt(2.0 / (length + 1)) * np.sin(np.pi * np.outer(index, index) / (length + 1))
    eigen = 4.0 * np.sin(np.pi * index / (2 * (length + 1))) ** 2
    return table, eigen


def split(value):
    high = value.astype(BF16)
    return high, (value - high.astype(F32)).astype(BF16)


def dot3(left, right):
    (lh, ll), (rh, rl) = left, right
    dot = functools.partial(jnp.dot, preferred_element_type=F32)
    return dot(lh, rh) + (dot(ll, rh) + dot(lh, rl))


def chebyshev(shift, count):
    values = [jnp.ones_like(shift)]
    step = values[0]
    for n in range(count):
        step = step + shift * values[n]
        values.append(values[n] + step)
    return values


def slab_weights(shift, count):
    u = chebyshev(shift, count)
    return u[1:count] + [1.0 / u[count]]


def slab_solve(weights, right):
    count = len(right)
    u, inverse = weights[: count - 1], weights[count - 1]

    def times(n, value):
        return value if n == 0 else u[n - 1] * value

    lower = [right[0]]
    for k in range(1, count):
        lower.append(lower[-1] + times(k, right[k]))
    upper = [None] * count
    for k in range(count - 2, -1, -1):
        term = times(count - 2 - k, right[k + 1])
        upper[k] = term if upper[k + 1] is None else upper[k + 1] + term
    out = []
    for k in range(count):
        value = times(count - 1 - k, lower[k])
        if upper[k] is not None:
            value = value + times(k, upper[k])
        out.append(value * inverse)
    return out


def spike_of(shift, count):
    u = chebyshev(shift, count)
    inverse = 1.0 / u[count]
    return [u[count - 1 - k] * inverse for k in range(count)]


def interface_chain(couple, spread, bottoms, tops):
    count = len(bottoms)
    slope = jnp.zeros_like(couple)
    offset = jnp.zeros_like(couple)
    slopes, offsets, inverses, bases = [], [], [], []
    for s in range(count):
        inverse = 1.0 / (1.0 - couple * slope)
        base = (bottoms[s] + couple * offset) * inverse
        slopes.append(slope)
        offsets.append(offset)
        inverses.append(inverse * spread)
        bases.append(base)
        if s < count - 1:
            weight = spread * slope
            slope, offset = (
                couple + weight * spread * inverse,
                tops[s] + spread * offset + weight * base,
            )
    above = jnp.zeros_like(couple)
    lowers, uppers = [None] * count, [None] * count
    for s in range(count - 1, -1, -1):
        lower = bases[s] + inverses[s] * above
        uppers[s] = tops[s] + spread * (slopes[s] * lower + offsets[s]) + couple * above
        lowers[s] = lower
        above = lower
    below = [jnp.zeros_like(couple)] + uppers[:-1]
    above = lowers[1:] + [jnp.zeros_like(couple)]
    return below, above


def get_lanes(ref, rows):
    return jnp.concatenate([ref[n, rows, :] for n in range(ref.shape[0])], 1)


def put_lanes(ref, rows, value, start):
    for n in range(value.shape[1] // 128):
        ref[start + n, rows, :] = value[:, n * 128 : (n + 1) * 128]


def load_kernel(nz, obs, up_in, east, fluid, up, high, low, side, final, raw, line, sems):
    parts = raw.shape[0]
    rows = high.shape[0]
    copies = []
    for n in range(parts):
        lanes = slice(n * 128, (n + 1) * 128)
        copies.append(
            (
                pltpu.make_async_copy(obs.at[:, lanes], raw.at[n], sems.at[n]),
                pltpu.make_async_copy(up_in.at[:, lanes], up.at[n], sems.at[parts + n]),
            )
        )
        for copy in copies[-1]:
            copy.start()
    edge = pltpu.make_async_copy(east.at[0:nz, :], line, sems.at[2 * parts])
    edge.start()
    edge.wait()
    for n, (flags, speed) in enumerate(copies):
        lanes = slice(n * 128, (n + 1) * 128)
        flags.wait()
        fluid[n] = fluid_of(raw[n])
        high[:, lanes] = fluid[n, pl.ds(nz - 1, rows, stride=nz), :]
        bottom = fluid[n, pl.ds(0, rows, stride=nz), :]
        low[0, :, lanes] = bottom
        first = fluid[n, 0:nz, :]
        side[0:nz, lanes] = first
        side[nz : 2 * nz, lanes] = first * line[:, lanes]
        final[:, lanes] = fluid[n, (rows - 1) * nz : rows * nz, :]
        speed.wait()
        low[1, :, lanes] = bottom * up[n, pl.ds(0, rows, stride=nz), :]


def north_roll(value, shift):
    return pltpu.roll(value, shift % value.shape[1], 1)


def put_row(value, row, index):
    where = lax.broadcasted_iota(jnp.int32, value.shape, 0) == index
    return jnp.where(where, jnp.broadcast_to(row, value.shape), value)


def below_of(value, row):
    return put_row(pltpu.roll(value, 1, 0), row, 0)


def above_of(value, row):
    return put_row(pltpu.roll(value, value.shape[0] - 1, 0), row, value.shape[0] - 1)


def fluid_of(block):
    return (1 - block).astype(F32)


def east_left(table):
    return table, table[:, : table.shape[0]]


def north_pair(tables, index):
    size = tables.shape[1]
    return tables[2 * index * size : (2 * index + 1) * size, :], tables[(2 * index + 1) * size : (2 * index + 2) * size, :]


def east_dot(left, value):
    high, low = split(value)
    dot = functools.partial(jnp.dot, preferred_element_type=F32)
    return dot(left[0], jnp.concatenate([high, high], 0)) + dot(left[1], low)


def north_forward(value, even, odd):
    half = value.shape[1] // 2
    low, high = value[:, :half], value[:, half:]
    return dot3(split(low + high), even), dot3(split(low - high), odd)


def interior_kernel(
    nz, chunk, fluid, up, east, north, tables, east_table, east_values, lam_b,
    modes, weights, bottom, top, sums,
    src, ready, half,
):
    ny = src.shape[1]
    nx = modes.shape[1]
    count = nx // chunk
    lift = jnp.where(lax.axis_index("gz") == 0, 1.0, 0.0).astype(F32)
    floor = jnp.broadcast_to(lift, (1, ny))
    none = jnp.zeros((1, ny), F32)

    def cells(x):
        return pl.ds(pl.multiple_of(x * nz, nz), nz)

    def stencil(step):
        base = step * chunk
        inside = jnp.where(step > 0, 1.0, 0.0).astype(F32)
        more = jnp.where(step < count - 1, 1.0, 0.0).astype(F32)
        here = get_lanes(fluid, cells(base))
        before = get_lanes(fluid, cells(jnp.maximum(base - 1, 0)))
        masked = here * (before * inside) * east[cells(base), :]
        for i in range(chunk):
            own = cells(base + i)
            nxt = cells(base + i + 1) if i < chunk - 1 else cells(jnp.minimum(base + chunk, nx - 1))
            after = get_lanes(fluid, nxt)
            flux = after * east[nxt, :]
            if i == chunk - 1:
                flux = flux * more
            masked_next = here * flux
            north_masked = here * north_roll(here, 1) * north[own, :]
            up_masked = here * below_of(here, floor) * get_lanes(up, own)
            src[i * nz : (i + 1) * nz, :] = (
                (masked - masked_next)
                + (north_masked - north_roll(north_masked, -1))
                + (up_masked - above_of(up_masked, none))
            )
            here, masked = after, masked_next

    def transform(step):
        rows = pl.ds(pl.multiple_of(step * chunk * nz, chunk * nz), chunk * nz)
        even, odd = north_forward(ready[...], north_pair(tables, 0), north_pair(tables, 1))
        put_lanes(half, rows, even, 0)
        put_lanes(half, rows, odd, ny // 256)

    stencil(0)
    ready[...] = src[...]

    def body(step, carry):
        transform(step - 1)
        stencil(step)
        ready[...] = src[...]
        return carry

    lax.fori_loop(1, count, body, 0)
    transform(count - 1)
    left = east_left(east_table[0])
    for k in range(nz):
        modes[k] = east_dot(left, get_lanes(half, pl.ds(k, nx, stride=nz)))

    sums[...] = jnp.zeros_like(sums)
    blocks = nx // 8

    def solve(n, carry):
        at = pl.ds(pl.multiple_of(n * 8, 8), 8)
        parity = n // (blocks // 2)
        for lane in range(0, ny, 128):
            lanes = slice(lane, lane + 128)
            values = slab_weights(east_values[0, at, :] + lam_b[:, lanes], nz)
            for k in range(nz):
                weights[k, at, lanes] = values[k]
            local = slab_solve(values, [modes[k, at, lanes] for k in range(nz)])
            bottom[at, lanes] = local[0]
            top[at, lanes] = local[nz - 1]
            weight = east_values[1, at, :]
            for k in range(nz):
                sums[parity, k, :, lanes] += weight * local[k]
        return carry

    lax.fori_loop(0, blocks, solve, 0)


def joined_kernel(
    nz, slabs,
    modes, weights, bottom_in, top_in, sums_in, high, low_above, final, side_east,
    tables, east_table, east_values,
    crown, out,
    bottom, top, sums,
):
    nx, ny = high.shape
    leaving = final[...] * side_east[nz:, :]
    stacked = jnp.concatenate([high[...] * low_above[1], leaving], 0)
    stacked = jnp.concatenate(north_forward(stacked, north_pair(tables, 0), north_pair(tables, 1)), 1)
    top[...] = east_dot(east_left(east_table[0]), stacked[:nx])
    leaving = stacked[nx:]
    sums[...] = sums_in[...]
    blocks = nx // 8

    def share(n, carry):
        at = pl.ds(pl.multiple_of(n * 8, 8), 8)
        parity = n // (blocks // 2)
        for lane in range(0, ny, 128):
            lanes = slice(lane, lane + 128)
            rising = top[at, lanes]
            scaled = rising * weights[nz - 1, at, lanes]
            crown[at, lanes] = modes[nz - 1, at, lanes] - rising
            bottom[at, lanes] = bottom_in[at, lanes] - scaled
            top[at, lanes] = top_in[at, lanes] - weights[nz - 2, at, lanes] * scaled + rising
            scaled = east_values[1, at, :] * scaled
            sums[parity, 0, :, lanes] -= scaled
            for k in range(1, nz):
                sums[parity, k, :, lanes] -= weights[k - 1, at, lanes] * scaled
        return carry

    lax.fori_loop(0, blocks, share, 0)
    even = [jnp.sum(sums[0, k], axis=0, keepdims=True) for k in range(nz)]
    odd = [jnp.sum(sums[1, k], axis=0, keepdims=True) for k in range(nz)]
    west = jnp.concatenate([e + o for e, o in zip(even, odd)], 0)
    east_end = jnp.concatenate([e - o for e, o in zip(even, odd)], 0) + leaving
    width = ny // slabs
    hx = nx // 2
    for j in range(slabs):
        lanes = slice(j * width, (j + 1) * width)
        out[j, 0:hx, :] = jnp.concatenate([bottom[:hx, lanes], bottom[hx:, lanes]], 1)
        out[j, hx:nx, :] = jnp.concatenate([top[:hx, lanes], top[hx:, lanes]], 1)
        out[j, nx : nx + nz, :] = jnp.concatenate([west[:, lanes], east_end[:, lanes]], 1)


def swap_halves(value):
    width = value.shape[1] // 2
    return jnp.concatenate([value[:, width:], value[:, :width]], 1)


def in_first_half(value):
    return lax.broadcasted_iota(jnp.int32, value.shape, 1) < value.shape[1] // 2


def ends_kernel(nz, ends, final, pairs, lam_b, sums, sines, out, out_more, acc):
    slabs = ends.shape[0]
    nx = ends.shape[1] - nz
    hx = nx // 2
    total = slabs * nz
    shift = pairs[0:hx, :] + lam_b[lax.axis_index("gz")][0:1, :]
    spike = spike_of(shift, nz)
    below, above = interface_chain(
        spike[0],
        spike[nz - 1],
        [ends[s, 0:hx, :] for s in range(slabs)],
        [ends[s, hx:nx, :] for s in range(slabs)],
    )
    weight = pairs[hx:nx, :]
    spike = [weight * g for g in spike]
    for s in range(slabs):
        for k in range(nz):
            term = spike[k] * below[s] + spike[nz - 1 - k] * above[s]
            row = (s * nz + k) * 8
            acc[row : row + 8, :] = jnp.sum(term.reshape(hx // 8, 8, term.shape[1]), axis=0)
    both = dot3((sums[:total, :], sums[total:, :]), split(acc[...]))
    other = swap_halves(both)
    both = jnp.where(in_first_half(both), both + other, other - both)
    rows = jnp.concatenate([ends[s, nx : nx + nz, :] for s in range(slabs)], 0)
    both = both + dot3((sines[:total, :], sines[total:, :]), split(rows))
    out[...] = both
    out_more[:total, :] = both
    lanes = both.shape[1]
    for n in range(final.shape[1] // lanes):
        out_more[total + n * nz : total + (n + 1) * nz, :] = final[:, n * lanes : (n + 1) * lanes]


def power(value, count):
    result = None
    while count:
        if count & 1:
            result = value if result is None else result * value
        count >>= 1
        if count:
            value = value * value
    return result


def correct_kernel(nz, groups, ends, *rest):
    found = rest[:groups]
    pairs, lam_b, sines, out, jump = rest[groups:]
    slabs, width = ends.shape[0], ends.shape[2] // 2
    nx = ends.shape[1] - nz
    hx = nx // 2
    total = slabs * nz
    row_b = lam_b[lax.axis_index("gz")][0:1, :]
    shift = pairs[nx:, :width] + row_b[:, :width]
    cosh = 1.0 + 0.5 * shift
    sinh = jnp.sqrt(shift + 0.25 * shift * shift)
    grow = cosh + sinh
    decay = 1.0 / grow
    far = power(decay, nx)
    far2 = far * far
    scale = 1.0 / (sinh * (1.0 - far2))
    self2 = ((1.0 + far2) + (decay + far2 * grow)) * scale
    cross2 = 2.0 * (1.0 + cosh) * far * scale
    inverse = {}
    for f in range(groups):
        key = min(f, groups - f)
        if key not in inverse:
            inverse[key] = 1.0 / (1.0 + self2 - float(np.cos(2 * np.pi * f / groups)) * cross2)
    kernel = {}
    for n in range(groups // 2 + 1):
        value = None
        for f in range(groups):
            factor = float(np.cos(2 * np.pi * f * n / groups)) / groups
            term = factor * inverse[min(f, groups - f)]
            value = term if value is None else value + term
        kernel[n] = value
    jumps_east, jumps_west = None, None
    for n in range(groups):
        nxt = (n + 1) % groups
        t = found[n][:total, width:] - found[nxt][:total, :width]
        east_term = kernel[min(n, groups - n)] * t
        west_term = kernel[min(nxt, groups - nxt)] * t
        jumps_east = east_term if jumps_east is None else jumps_east + east_term
        jumps_west = west_term if jumps_west is None else jumps_west + west_term
    both = dot3((sines[:total, :], sines[total:, :]), split(jnp.concatenate([jumps_west, jumps_east], 1)))
    other = swap_halves(both)
    jump[...] = jnp.where(in_first_half(both), both - other, both + other)
    shift = pairs[0:hx, :] + row_b
    spike = spike_of(shift, nz)
    weight = pairs[hx:nx, :]
    loads = [weight * g for g in spike]
    bottoms, tops = [], []
    for s in range(slabs):
        low, high = ends[s, 0:hx, :], ends[s, hx:nx, :]
        for k in range(nz):
            q = jump[s * nz + k : s * nz + k + 1, :]
            low = low + loads[k] * q
            high = high + loads[nz - 1 - k] * q
        bottoms.append(low)
        tops.append(high)
    below, above = interface_chain(spike[0], spike[nz - 1], bottoms, tops)
    for s in range(slabs):
        out[s, 0:hx, :] = below[s]
        out[s, hx:nx, :] = above[s]
        out[s, nx : nx + nz, :] = both[s * nz : (s + 1) * nz, :]


def backward_kernel(
    nz, slabs, chunk,
    modes, weights, crown, solved,
    fluid, up, east, north,
    from_west, side_east, f_below, high, low, low_above,
    tables, east_table, east_values,
    far_east, far_north, far_up, far_p, far_r,
    done, sems, work, below, above, found, half, press, coming, p_below, floor, leaving,
):
    ny = east.shape[1]
    hy = ny // 2
    nx = modes.shape[1]
    steps = nx // chunk
    size = chunk * nz
    fields = (far_east, far_north, far_up, far_p, far_r)
    lift = jnp.where(lax.axis_index("gz") == 0, 1.0, 0.0).astype(F32)

    def north_back(value):
        even = dot3(split(value[:, :hy]), north_pair(tables, 0))
        odd = dot3(split(value[:, hy:]), north_pair(tables, 2))
        return even + odd, even - odd

    width = ny // slabs
    west, east_end = [], []
    hx = nx // 2
    for j in range(slabs):
        lanes = slice(j * width, (j + 1) * width)
        below[:hx, lanes] = solved[j, 0:hx, :width]
        below[hx:, lanes] = solved[j, 0:hx, width:]
        above[:hx, lanes] = solved[j, hx:nx, :width]
        above[hx:, lanes] = solved[j, hx:nx, width:]
        west.append(solved[j, nx : nx + nz, :width])
        east_end.append(solved[j, nx : nx + nz, width:])
    west = jnp.concatenate(west, 1)
    east_end = jnp.concatenate(east_end, 1)
    found[0] = west - east_end
    found[1] = west + east_end
    blocks = nx // 8

    def solve(n, carry):
        at = pl.ds(pl.multiple_of(n * 8, 8), 8)
        parity = n // (blocks // 2)
        for lane in range(0, ny, 128):
            lanes = slice(lane, lane + 128)
            weight = east_values[1, at, :]
            right = []
            for k in range(nz):
                q = jnp.broadcast_to(found[parity, pl.ds(k, 1), lanes], weight.shape)
                plane = modes[k, at, lanes] if k < nz - 1 else crown[at, lanes]
                right.append(plane + weight * q)
            right[0] = right[0] + below[at, lanes]
            right[nz - 1] = right[nz - 1] + above[at, lanes]
            local = slab_solve([weights[k, at, lanes] for k in range(nz)], right)
            for k in range(nz):
                work[k, at, lanes] = local[k]
        return carry

    lax.fori_loop(0, blocks, solve, 0)
    left = east_left(east_table[1])
    crest = None
    for k in range(nz):
        crest = east_dot(left, work[k])
        put_lanes(half, pl.ds(nz + k, nx, stride=nz), crest, 0)
    first, final = slice(nz, 2 * nz), slice(nx * nz, (nx + 1) * nz)
    put_lanes(half, slice(0, nz), get_lanes(half, first) + west, 0)
    put_lanes(half, slice((nx + 1) * nz, (nx + 2) * nz), get_lanes(half, final) - east_end, 0)
    both = jnp.concatenate(
        [east_dot(left, below[...]), east_dot(left, above[...]) - crest, get_lanes(half, slice(0, size + nz))], 0
    )
    both = jnp.concatenate(north_back(both), 1)
    p_below[...] = both[:nx] - f_below[...] * low[1]
    floor[...] = f_below[...] + lift
    leaving[...] = high[...] * (low_above[1] - low_above[0] * both[nx : 2 * nx])
    press[...] = both[2 * nx :]


    def cells(x):
        return pl.ds(pl.multiple_of(x * nz, nz), nz)

    lanes = from_west.shape[1]
    total = from_west.shape[0] - nz * (ny // lanes)
    side_west = jnp.concatenate(
        [from_west[total + n * nz : total + (n + 1) * nz, :] for n in range(ny // lanes)], 1
    )

    def advance(step, carry):
        last = step == steps - 1
        base = step * chunk

        rows = pl.ds(pl.multiple_of((base + chunk + 1) * nz, nz), size)
        coming[:, :hy], coming[:, hy:] = north_back(get_lanes(half, rows))

        here = get_lanes(fluid, cells(base))
        before = get_lanes(fluid, cells(jnp.maximum(base - 1, 0)))
        before = jnp.where(step == 0, side_west, before)
        after_row = cells(jnp.minimum(base + chunk, nx - 1))
        after_fluid = get_lanes(fluid, after_row)
        after_flux = jnp.where(last, side_east[nz:, :], after_fluid * east[after_row, :])
        after_fluid = jnp.where(last, side_east[0:nz, :], after_fluid)

        p = press[nz : 2 * nz, :]
        first_flux = here * before * east[cells(base), :]
        p_before = press[0:nz, :] - jnp.where(step == 0, 1.0, 0.0).astype(F32) * first_flux
        east_done = first_flux - here * before * (p - p_before)
        for i in range(chunk):
            own = cells(base + i)
            line = pl.ds(base + i, 1)
            if i < chunk - 1:
                nxt = cells(base + i + 1)
                after = get_lanes(fluid, nxt)
                flux = after * east[nxt, :]
                p_next = press[(i + 2) * nz : (i + 3) * nz, :]
            else:
                after, flux = after_fluid, after_flux
                p_next = coming[0:nz, :] + jnp.where(last, 1.0, 0.0).astype(F32) * (here * flux)
            east_next_done = here * (flux - after * (p_next - p))
            north_done = here * north_roll(here, 1) * (north[own, :] - (p - north_roll(p, 1)))
            fluid_below = below_of(here, floor[line, :])
            up_done = here * fluid_below * (get_lanes(up, own) - (p - below_of(p, p_below[line, :])))
            done[0, own, :] = east_done
            done[1, own, :] = north_done
            done[2, own, :] = up_done
            done[3, own, :] = p
            done[4, own, :] = (
                (east_done - east_next_done)
                + (north_done - north_roll(north_done, -1))
                + (up_done - above_of(up_done, leaving[line, :]))
            )
            here, p, east_done = after, p_next, east_next_done
        press[0:nz, :] = press[size : size + nz, :]
        press[nz:, :] = coming[...]
        sent = pl.ds(pl.multiple_of(base * nz, size), size)
        for n, field in enumerate(fields):
            pltpu.make_async_copy(done.at[n, sent, :], field.at[sent, :], sems.at[n]).start()
        return carry

    lax.fori_loop(0, steps, advance, 0)
    for n, field in enumerate(fields):
        pltpu.make_async_copy(done.at[n], field, sems.at[n]).wait()


def local(groups, slabs, east_velocity, north_velocity, upward_velocity, obstacle):
    nx, nz, ny = east_velocity.shape
    total = slabs * nz
    width = ny // slabs
    flat = [a.reshape(nx * nz, ny) for a in (obstacle, east_velocity, north_velocity, upward_velocity)]
    obs, east, north, up_in = flat

    even_np, odd_np, lam_b_np = north_tables(ny)
    block_np, lam_a_np = east_tables(nx)
    sine_np, mu_np = sine_table(total)
    tables = np.concatenate([*pair_np(even_np), *pair_np(odd_np), *pair_np(odd_np.T)], 0)
    east_table = np.stack([np.concatenate(pair_np(t), 1) for t in (block_np, block_np.T)])
    sines = np.concatenate(pair_np(sine_np), 0)
    sums = np.repeat(sines, 8, axis=1)
    east_values = np.stack([np.repeat(v[:, None], 128, 1) for v in (lam_a_np, block_np[:, 0])]).astype(np.float32)
    lam_b = np.repeat(lam_b_np[None], 8, 0).astype(np.float32)
    part = np.tile(lam_b_np.reshape(slabs, 1, width), (1, 8, 2)).astype(np.float32)

    def paired(column):
        return np.repeat(column.reshape(2, nx // 2).T, width, 1)

    pairs = np.concatenate(
        [paired(lam_a_np), paired(block_np[:, 0]), np.repeat(mu_np[:, None], 2 * width, 1)], 0
    ).astype(np.float32)

    chunk = 16
    lanes = ny // 128
    params = pltpu.CompilerParams(vmem_limit_bytes=VMEM_LIMIT)
    kept = pl.BlockSpec(memory_space=pltpu.VMEM)
    far = pl.BlockSpec(memory_space=pltpu.HBM)

    def array(*shape):
        return jax.ShapeDtypeStruct(shape, F32)

    blocked = array(lanes, nx * nz, 128)
    fluid, up, high, low, side, final = pl.pallas_call(
        functools.partial(load_kernel, nz),
        in_specs=[far] * 3,
        out_specs=[kept] * 6,
        out_shape=[blocked, blocked, array(nx, ny), array(2, nx, ny), array(2 * nz, ny), array(nz, ny)],
        scratch_shapes=[
            pltpu.VMEM((lanes, nx * nz, 128), jnp.int32),
            pltpu.VMEM((nz, ny), F32),
            pltpu.SemaphoreType.DMA((2 * lanes + 1,)),
        ],
        compiler_params=pltpu.CompilerParams(vmem_limit_bytes=LOAD_LIMIT),
        name="load",
    )(obs, up_in, east)

    rising = [(i, i + 1) for i in range(slabs - 1)]
    falling = [(i + 1, i) for i in range(slabs - 1)]
    low_above = lax.ppermute(low, "gz", falling)
    side_east = lax.ppermute(side, "xy", [((i + 1) % groups, i) for i in range(groups)])

    cells = nx * nz * ny
    modes, weights, bottom, top, folded = pl.pallas_call(
        functools.partial(interior_kernel, nz, chunk),
        in_specs=[kept] * 8,
        out_specs=[kept] * 5,
        out_shape=[array(nz, nx, ny)] * 2 + [array(nx, ny)] * 2 + [array(2, nz, 8, ny)],
        scratch_shapes=[
            pltpu.VMEM((chunk * nz, ny), F32),
            pltpu.VMEM((chunk * nz, ny), F32),
            pltpu.VMEM((lanes, nx * nz, 128), F32),
        ],
        compiler_params=params,
        cost_estimate=pl.CostEstimate(flops=cells * 2 * 3 * (ny // 2 + nx), bytes_accessed=20 * cells, transcendentals=0),
        name="interior",
    )(fluid, up, east, north, tables, east_table, east_values, lam_b)
    ends_shape = array(slabs, nx + nz, 2 * width)
    crown, ends = pl.pallas_call(
        functools.partial(joined_kernel, nz, slabs),
        in_specs=[kept] * 12,
        out_specs=[kept] * 2,
        out_shape=[array(nx, ny), ends_shape],
        scratch_shapes=[
            pltpu.VMEM((nx, ny), F32),
            pltpu.VMEM((nx, ny), F32),
            pltpu.VMEM((2, nz, 8, ny), F32),
        ],
        compiler_params=params,
        name="joined",
    )(modes, weights, bottom, top, folded, high, low_above, final, side_east, tables, east_table, east_values)

    ends = lax.all_to_all(ends, "gz", split_axis=0, concat_axis=0, tiled=True)
    own, own_more = pl.pallas_call(
        functools.partial(ends_kernel, nz),
        in_specs=[kept] * 6,
        out_specs=[kept] * 2,
        out_shape=[array(total, 2 * width), array(total + nz * ny // (2 * width), 2 * width)],
        scratch_shapes=[pltpu.VMEM((total * 8, 2 * width), F32)],
        compiler_params=params,
        name="ends",
    )(ends, final, pairs, part, sums, sines)
    found = [own]
    for shift in range(1, groups):
        sent = own_more if shift == groups - 1 else own
        found.append(lax.ppermute(sent, "xy", [((i + shift) % groups, i) for i in range(groups)]))
    rising_flags, own = lax.optimization_barrier((high, own))
    f_below = lax.ppermute(rising_flags, "gz", rising)
    f_below, found[0] = lax.optimization_barrier((f_below, found[0]))
    solved = pl.pallas_call(
        functools.partial(correct_kernel, nz, groups),
        in_specs=[kept] * (groups + 4),
        out_specs=kept,
        out_shape=ends_shape,
        scratch_shapes=[pltpu.VMEM((total, 2 * width), F32)],
        compiler_params=params,
        name="correct",
    )(ends, *found, pairs, part, sines)
    solved = lax.all_to_all(solved, "gz", split_axis=0, concat_axis=0, tiled=True)

    outs = pl.pallas_call(
        functools.partial(backward_kernel, nz, slabs, BACK_ROWS),
        in_specs=[kept] * 17,
        out_specs=[far] * 5,
        out_shape=[array(nx * nz, ny)] * 5,
        scratch_shapes=[
            pltpu.VMEM((5, nx * nz, ny), F32),
            pltpu.SemaphoreType.DMA((5,)),
            pltpu.VMEM((nz, nx, ny), F32),
            pltpu.VMEM((nx, ny), F32),
            pltpu.VMEM((nx, ny), F32),
            pltpu.VMEM((2, nz, ny), F32),
            pltpu.VMEM((lanes, (nx + BACK_ROWS + 1) * nz, 128), F32),
            pltpu.VMEM(((BACK_ROWS + 1) * nz, ny), F32),
            pltpu.VMEM((BACK_ROWS * nz, ny), F32),
            pltpu.VMEM((nx, ny), F32),
            pltpu.VMEM((nx, ny), F32),
            pltpu.VMEM((nx, ny), F32),
        ],
        compiler_params=pltpu.CompilerParams(vmem_limit_bytes=BACK_LIMIT),
        name="backward",
    )(modes, weights, crown, solved, fluid, up, east, north, found[-1], side_east, f_below, high, low,
      low_above, tables, east_table, east_values)
    return tuple(o.reshape(nx, nz, ny) for o in outs)


def solution(mesh):
    placed = P("xy", "gz", None)
    step = jax.shard_map(
        functools.partial(local, mesh.shape["xy"], mesh.shape["gz"]),
        mesh=mesh,
        in_specs=(placed,) * 4,
        out_specs=(placed,) * 5,
        check_vma=False,
    )
    return step
```

```python
import functools

import jax
import jax.numpy as jnp
import ml_dtypes
import numpy as np
from jax import lax
from jax.experimental import pallas as pl
from jax.experimental.pallas import tpu as pltpu
from jax.sharding import PartitionSpec as P


F32 = jnp.float32
BF16 = jnp.bfloat16
VMEM_LIMIT = 24 * 1024 * 1024
BACK_ROWS = 8
BACK_LIMIT = 28 * 1024 * 1024
LOAD_LIMIT = 48 * 1024 * 1024


def pair_np(table):
    high = table.astype(np.float32).astype(ml_dtypes.bfloat16)
    low = (table - high.astype(np.float64)).astype(np.float32).astype(ml_dtypes.bfloat16)
    return high, low


def north_tables(length):
    half = length // 2
    cell = np.arange(half)[:, None]
    mode = np.arange(half)[None, :]

    def cas(number):
        angle = 2.0 * np.pi * ((cell * number) % length) / length
        return (np.cos(angle) + np.sin(angle)) / np.sqrt(length)

    numbers = np.concatenate([2 * np.arange(half), 2 * np.arange(half) + 1])
    eigen = 4.0 * np.sin(np.pi * numbers / length) ** 2
    return cas(2 * mode), cas(2 * mode + 1), eigen


def east_tables(length):
    modes = np.concatenate([np.arange(0, length, 2), np.arange(1, length, 2)])
    cell = np.arange(length)
    table = np.cos(np.pi * modes[:, None] * (2 * cell[None, :] + 1) / (2 * length)) * np.sqrt(2.0 / length)
    table[0] = np.sqrt(1.0 / length)
    eigen = 4.0 * np.sin(np.pi * modes / (2 * length)) ** 2
    return table, eigen


def sine_table(length):
    index = np.arange(1, length + 1)
    table = np.sqrt(2.0 / (length + 1)) * np.sin(np.pi * np.outer(index, index) / (length + 1))
    eigen = 4.0 * np.sin(np.pi * index / (2 * (length + 1))) ** 2
    return table, eigen


def split(value):
    high = value.astype(BF16)
    return high, (value - high.astype(F32)).astype(BF16)


def dot3(left, right):
    (lh, ll), (rh, rl) = left, right
    dot = functools.partial(jnp.dot, preferred_element_type=F32)
    return dot(lh, rh) + (dot(ll, rh) + dot(lh, rl))


def chebyshev(shift, count):
    values = [jnp.ones_like(shift)]
    step = values[0]
    for n in range(count):
        step = step + shift * values[n]
        values.append(values[n] + step)
    return values


def slab_weights(shift, count):
    u = chebyshev(shift, count)
    return u[1:count] + [1.0 / u[count]]


def slab_solve(weights, right):
    count = len(right)
    u, inverse = weights[: count - 1], weights[count - 1]

    def times(n, value):
        return value if n == 0 else u[n - 1] * value

    lower = [right[0]]
    for k in range(1, count):
        lower.append(lower[-1] + times(k, right[k]))
    upper = [None] * count
    for k in range(count - 2, -1, -1):
        term = times(count - 2 - k, right[k + 1])
        upper[k] = term if upper[k + 1] is None else upper[k + 1] + term
    out = []
    for k in range(count):
        value = times(count - 1 - k, lower[k])
        if upper[k] is not None:
            value = value + times(k, upper[k])
        out.append(value * inverse)
    return out


def spike_of(shift, count):
    u = chebyshev(shift, count)
    inverse = 1.0 / u[count]
    return [u[count - 1 - k] * inverse for k in range(count)]


def interface_chain(couple, spread, bottoms, tops):
    count = len(bottoms)
    slope = jnp.zeros_like(couple)
    offset = jnp.zeros_like(couple)
    slopes, offsets, inverses, bases = [], [], [], []
    for s in range(count):
        inverse = 1.0 / (1.0 - couple * slope)
        base = (bottoms[s] + couple * offset) * inverse
        slopes.append(slope)
        offsets.append(offset)
        inverses.append(inverse * spread)
        bases.append(base)
        if s < count - 1:
            weight = spread * slope
            slope, offset = (
                couple + weight * spread * inverse,
                tops[s] + spread * offset + weight * base,
            )
    above = jnp.zeros_like(couple)
    lowers, uppers = [None] * count, [None] * count
    for s in range(count - 1, -1, -1):
        lower = bases[s] + inverses[s] * above
        uppers[s] = tops[s] + spread * (slopes[s] * lower + offsets[s]) + couple * above
        lowers[s] = lower
        above = lower
    below = [jnp.zeros_like(couple)] + uppers[:-1]
    above = lowers[1:] + [jnp.zeros_like(couple)]
    return below, above


def get_lanes(ref, rows):
    return jnp.concatenate([ref[n, rows, :] for n in range(ref.shape[0])], 1)


def put_lanes(ref, rows, value, start):
    for n in range(value.shape[1] // 128):
        ref[start + n, rows, :] = value[:, n * 128 : (n + 1) * 128]


def load_kernel(nz, obs, up_in, east, fluid, up, high, low, side, final, raw, line, sems):
    parts = raw.shape[0]
    rows = high.shape[0]
    copies = []
    for n in range(parts):
        lanes = slice(n * 128, (n + 1) * 128)
        copies.append(
            (
                pltpu.make_async_copy(obs.at[:, lanes], raw.at[n], sems.at[n]),
                pltpu.make_async_copy(up_in.at[:, lanes], up.at[n], sems.at[parts + n]),
            )
        )
        for copy in copies[-1]:
            copy.start()
    edge = pltpu.make_async_copy(east.at[0:nz, :], line, sems.at[2 * parts])
    edge.start()
    edge.wait()
    for n, (flags, speed) in enumerate(copies):
        lanes = slice(n * 128, (n + 1) * 128)
        flags.wait()
        fluid[n] = fluid_of(raw[n])
        high[:, lanes] = fluid[n, pl.ds(nz - 1, rows, stride=nz), :]
        bottom = fluid[n, pl.ds(0, rows, stride=nz), :]
        low[0, :, lanes] = bottom
        first = fluid[n, 0:nz, :]
        side[0:nz, lanes] = first
        side[nz : 2 * nz, lanes] = first * line[:, lanes]
        final[:, lanes] = fluid[n, (rows - 1) * nz : rows * nz, :]
        speed.wait()
        low[1, :, lanes] = bottom * up[n, pl.ds(0, rows, stride=nz), :]


def north_roll(value, shift):
    return pltpu.roll(value, shift % value.shape[1], 1)


def put_row(value, row, index):
    where = lax.broadcasted_iota(jnp.int32, value.shape, 0) == index
    return jnp.where(where, jnp.broadcast_to(row, value.shape), value)


def below_of(value, row):
    return put_row(pltpu.roll(value, 1, 0), row, 0)


def above_of(value, row):
    return put_row(pltpu.roll(value, value.shape[0] - 1, 0), row, value.shape[0] - 1)


def fluid_of(block):
    return (1 - block).astype(F32)


def east_left(table):
    return table, table[:, : table.shape[0]]


def north_pair(tables, index):
    size = tables.shape[1]
    return tables[2 * index * size : (2 * index + 1) * size, :], tables[(2 * index + 1) * size : (2 * index + 2) * size, :]


def east_dot(left, value):
    high, low = split(value)
    dot = functools.partial(jnp.dot, preferred_element_type=F32)
    return dot(left[0], jnp.concatenate([high, high], 0)) + dot(left[1], low)


def north_forward(value, even, odd):
    half = value.shape[1] // 2
    low, high = value[:, :half], value[:, half:]
    return dot3(split(low + high), even), dot3(split(low - high), odd)


def interior_kernel(
    nz, chunk, fluid, up, east, north, tables, east_table, east_values, lam_b,
    modes, weights, bottom, top, sums,
    src, ready, half,
):
    ny = src.shape[1]
    nx = modes.shape[1]
    count = nx // chunk
    lift = jnp.where(lax.axis_index("gz") == 0, 1.0, 0.0).astype(F32)
    floor = jnp.broadcast_to(lift, (1, ny))
    none = jnp.zeros((1, ny), F32)

    def cells(x):
        return pl.ds(pl.multiple_of(x * nz, nz), nz)

    def stencil(step):
        base = step * chunk
        inside = jnp.where(step > 0, 1.0, 0.0).astype(F32)
        more = jnp.where(step < count - 1, 1.0, 0.0).astype(F32)
        here = get_lanes(fluid, cells(base))
        before = get_lanes(fluid, cells(jnp.maximum(base - 1, 0)))
        masked = here * (before * inside) * east[cells(base), :]
        for i in range(chunk):
            own = cells(base + i)
            nxt = cells(base + i + 1) if i < chunk - 1 else cells(jnp.minimum(base + chunk, nx - 1))
            after = get_lanes(fluid, nxt)
            flux = after * east[nxt, :]
            if i == chunk - 1:
                flux = flux * more
            masked_next = here * flux
            north_masked = here * north_roll(here, 1) * north[own, :]
            up_masked = here * below_of(here, floor) * get_lanes(up, own)
            src[i * nz : (i + 1) * nz, :] = (
                (masked - masked_next)
                + (north_masked - north_roll(north_masked, -1))
                + (up_masked - above_of(up_masked, none))
            )
            here, masked = after, masked_next

    def transform(step):
        rows = pl.ds(pl.multiple_of(step * chunk * nz, chunk * nz), chunk * nz)
        even, odd = north_forward(ready[...], north_pair(tables, 0), north_pair(tables, 1))
        put_lanes(half, rows, even, 0)
        put_lanes(half, rows, odd, ny // 256)

    stencil(0)
    ready[...] = src[...]

    def body(step, carry):
        transform(step - 1)
        stencil(step)
        ready[...] = src[...]
        return carry

    lax.fori_loop(1, count, body, 0)
    transform(count - 1)
    left = east_left(east_table[0])
    for k in range(nz):
        modes[k] = east_dot(left, get_lanes(half, pl.ds(k, nx, stride=nz)))

    sums[...] = jnp.zeros_like(sums)
    blocks = nx // 8

    def solve(n, carry):
        at = pl.ds(pl.multiple_of(n * 8, 8), 8)
        parity = n // (blocks // 2)
        for lane in range(0, ny, 128):
            lanes = slice(lane, lane + 128)
            values = slab_weights(east_values[0, at, :] + lam_b[:, lanes], nz)
            for k in range(nz):
                weights[k, at, lanes] = values[k]
            local = slab_solve(values, [modes[k, at, lanes] for k in range(nz)])
            bottom[at, lanes] = local[0]
            top[at, lanes] = local[nz - 1]
            weight = east_values[1, at, :]
            for k in range(nz):
                sums[parity, k, :, lanes] += weight * local[k]
        return carry

    lax.fori_loop(0, blocks, solve, 0)


def joined_kernel(
    nz, slabs,
    modes, weights, bottom_in, top_in, sums_in, high, low_above, final, side_east,
    tables, east_table, east_values,
    crown, out,
    bottom, top, sums,
):
    nx, ny = high.shape
    leaving = final[...] * side_east[nz:, :]
    stacked = jnp.concatenate([high[...] * low_above[1], leaving], 0)
    stacked = jnp.concatenate(north_forward(stacked, north_pair(tables, 0), north_pair(tables, 1)), 1)
    top[...] = east_dot(east_left(east_table[0]), stacked[:nx])
    leaving = stacked[nx:]
    sums[...] = sums_in[...]
    blocks = nx // 8

    def share(n, carry):
        at = pl.ds(pl.multiple_of(n * 8, 8), 8)
        parity = n // (blocks // 2)
        for lane in range(0, ny, 128):
            lanes = slice(lane, lane + 128)
            rising = top[at, lanes]
            scaled = rising * weights[nz - 1, at, lanes]
            crown[at, lanes] = modes[nz - 1, at, lanes] - rising
            bottom[at, lanes] = bottom_in[at, lanes] - scaled
            top[at, lanes] = top_in[at, lanes] - weights[nz - 2, at, lanes] * scaled + rising
            scaled = east_values[1, at, :] * scaled
            sums[parity, 0, :, lanes] -= scaled
            for k in range(1, nz):
                sums[parity, k, :, lanes] -= weights[k - 1, at, lanes] * scaled
        return carry

    lax.fori_loop(0, blocks, share, 0)
    even = [jnp.sum(sums[0, k], axis=0, keepdims=True) for k in range(nz)]
    odd = [jnp.sum(sums[1, k], axis=0, keepdims=True) for k in range(nz)]
    west = jnp.concatenate([e + o for e, o in zip(even, odd)], 0)
    east_end = jnp.concatenate([e - o for e, o in zip(even, odd)], 0) + leaving
    width = ny // slabs
    hx = nx // 2
    for j in range(slabs):
        lanes = slice(j * width, (j + 1) * width)
        out[j, 0:hx, :] = jnp.concatenate([bottom[:hx, lanes], bottom[hx:, lanes]], 1)
        out[j, hx:nx, :] = jnp.concatenate([top[:hx, lanes], top[hx:, lanes]], 1)
        out[j, nx : nx + nz, :] = jnp.concatenate([west[:, lanes], east_end[:, lanes]], 1)


def swap_halves(value):
    width = value.shape[1] // 2
    return jnp.concatenate([value[:, width:], value[:, :width]], 1)


def in_first_half(value):
    return lax.broadcasted_iota(jnp.int32, value.shape, 1) < value.shape[1] // 2


def ends_kernel(nz, ends, final, pairs, lam_b, sums, sines, out, out_more, acc):
    slabs = ends.shape[0]
    nx = ends.shape[1] - nz
    hx = nx // 2
    total = slabs * nz
    shift = pairs[0:hx, :] + lam_b[lax.axis_index("gz")][0:1, :]
    spike = spike_of(shift, nz)
    below, above = interface_chain(
        spike[0],
        spike[nz - 1],
        [ends[s, 0:hx, :] for s in range(slabs)],
        [ends[s, hx:nx, :] for s in range(slabs)],
    )
    weight = pairs[hx:nx, :]
    spike = [weight * g for g in spike]
    for s in range(slabs):
        for k in range(nz):
            term = spike[k] * below[s] + spike[nz - 1 - k] * above[s]
            row = (s * nz + k) * 8
            acc[row : row + 8, :] = jnp.sum(term.reshape(hx // 8, 8, term.shape[1]), axis=0)
    both = dot3((sums[:total, :], sums[total:, :]), split(acc[...]))
    other = swap_halves(both)
    both = jnp.where(in_first_half(both), both + other, other - both)
    rows = jnp.concatenate([ends[s, nx : nx + nz, :] for s in range(slabs)], 0)
    both = both + dot3((sines[:total, :], sines[total:, :]), split(rows))
    out[...] = both
    out_more[:total, :] = both
    lanes = both.shape[1]
    for n in range(final.shape[1] // lanes):
        out_more[total + n * nz : total + (n + 1) * nz, :] = final[:, n * lanes : (n + 1) * lanes]


def power(value, count):
    result = None
    while count:
        if count & 1:
            result = value if result is None else result * value
        count >>= 1
        if count:
            value = value * value
    return result


def correct_kernel(nz, groups, ends, *rest):
    found = rest[:groups]
    pairs, lam_b, sines, out, jump = rest[groups:]
    slabs, width = ends.shape[0], ends.shape[2] // 2
    nx = ends.shape[1] - nz
    hx = nx // 2
    total = slabs * nz
    row_b = lam_b[lax.axis_index("gz")][0:1, :]
    shift = pairs[nx:, :width] + row_b[:, :width]
    cosh = 1.0 + 0.5 * shift
    sinh = jnp.sqrt(shift + 0.25 * shift * shift)
    grow = cosh + sinh
    decay = 1.0 / grow
    far = power(decay, nx)
    far2 = far * far
    scale = 1.0 / (sinh * (1.0 - far2))
    self2 = ((1.0 + far2) + (decay + far2 * grow)) * scale
    cross2 = 2.0 * (1.0 + cosh) * far * scale
    inverse = {}
    for f in range(groups):
        key = min(f, groups - f)
        if key not in inverse:
            inverse[key] = 1.0 / (1.0 + self2 - float(np.cos(2 * np.pi * f / groups)) * cross2)
    kernel = {}
    for n in range(groups // 2 + 1):
        value = None
        for f in range(groups):
            factor = float(np.cos(2 * np.pi * f * n / groups)) / groups
            term = factor * inverse[min(f, groups - f)]
            value = term if value is None else value + term
        kernel[n] = value
    jumps_east, jumps_west = None, None
    for n in range(groups):
        nxt = (n + 1) % groups
        t = found[n][:total, width:] - found[nxt][:total, :width]
        east_term = kernel[min(n, groups - n)] * t
        west_term = kernel[min(nxt, groups - nxt)] * t
        jumps_east = east_term if jumps_east is None else jumps_east + east_term
        jumps_west = west_term if jumps_west is None else jumps_west + west_term
    both = dot3((sines[:total, :], sines[total:, :]), split(jnp.concatenate([jumps_west, jumps_east], 1)))
    other = swap_halves(both)
    jump[...] = jnp.where(in_first_half(both), both - other, both + other)
    shift = pairs[0:hx, :] + row_b
    spike = spike_of(shift, nz)
    weight = pairs[hx:nx, :]
    loads = [weight * g for g in spike]
    bottoms, tops = [], []
    for s in range(slabs):
        low, high = ends[s, 0:hx, :], ends[s, hx:nx, :]
        for k in range(nz):
            q = jump[s * nz + k : s * nz + k + 1, :]
            low = low + loads[k] * q
            high = high + loads[nz - 1 - k] * q
        bottoms.append(low)
        tops.append(high)
    below, above = interface_chain(spike[0], spike[nz - 1], bottoms, tops)
    for s in range(slabs):
        out[s, 0:hx, :] = below[s]
        out[s, hx:nx, :] = above[s]
        out[s, nx : nx + nz, :] = both[s * nz : (s + 1) * nz, :]


def backward_kernel(
    nz, slabs, chunk,
    modes, weights, crown, solved,
    fluid, up, east, north,
    from_west, side_east, f_below, high, low, low_above,
    tables, east_table, east_values,
    far_east, far_north, far_up, far_p, far_r,
    done, sems, work, below, above, found, half, press, coming, p_below, floor, leaving,
):
    ny = east.shape[1]
    hy = ny // 2
    nx = modes.shape[1]
    steps = nx // chunk
    size = chunk * nz
    fields = (far_east, far_north, far_up, far_p, far_r)
    lift = jnp.where(lax.axis_index("gz") == 0, 1.0, 0.0).astype(F32)

    def north_back(value):
        even = dot3(split(value[:, :hy]), north_pair(tables, 0))
        odd = dot3(split(value[:, hy:]), north_pair(tables, 2))
        return even + odd, even - odd

    width = ny // slabs
    west, east_end = [], []
    hx = nx // 2
    for j in range(slabs):
        lanes = slice(j * width, (j + 1) * width)
        below[:hx, lanes] = solved[j, 0:hx, :width]
        below[hx:, lanes] = solved[j, 0:hx, width:]
        above[:hx, lanes] = solved[j, hx:nx, :width]
        above[hx:, lanes] = solved[j, hx:nx, width:]
        west.append(solved[j, nx : nx + nz, :width])
        east_end.append(solved[j, nx : nx + nz, width:])
    west = jnp.concatenate(west, 1)
    east_end = jnp.concatenate(east_end, 1)
    found[0] = west - east_end
    found[1] = west + east_end
    blocks = nx // 8

    def solve(n, carry):
        at = pl.ds(pl.multiple_of(n * 8, 8), 8)
        parity = n // (blocks // 2)
        for lane in range(0, ny, 128):
            lanes = slice(lane, lane + 128)
            weight = east_values[1, at, :]
            right = []
            for k in range(nz):
                q = jnp.broadcast_to(found[parity, pl.ds(k, 1), lanes], weight.shape)
                plane = modes[k, at, lanes] if k < nz - 1 else crown[at, lanes]
                right.append(plane + weight * q)
            right[0] = right[0] + below[at, lanes]
            right[nz - 1] = right[nz - 1] + above[at, lanes]
            local = slab_solve([weights[k, at, lanes] for k in range(nz)], right)
            for k in range(nz):
                work[k, at, lanes] = local[k]
        return carry

    lax.fori_loop(0, blocks, solve, 0)
    left = east_left(east_table[1])
    crest = None
    for k in range(nz):
        crest = east_dot(left, work[k])
        put_lanes(half, pl.ds(nz + k, nx, stride=nz), crest, 0)
    first, final = slice(nz, 2 * nz), slice(nx * nz, (nx + 1) * nz)
    put_lanes(half, slice(0, nz), get_lanes(half, first) + west, 0)
    put_lanes(half, slice((nx + 1) * nz, (nx + 2) * nz), get_lanes(half, final) - east_end, 0)
    both = jnp.concatenate(
        [east_dot(left, below[...]), east_dot(left, above[...]) - crest, get_lanes(half, slice(0, size + nz))], 0
    )
    both = jnp.concatenate(north_back(both), 1)
    p_below[...] = both[:nx] - f_below[...] * low[1]
    floor[...] = f_below[...] + lift
    leaving[...] = high[...] * (low_above[1] - low_above[0] * both[nx : 2 * nx])
    press[...] = both[2 * nx :]


    def cells(x):
        return pl.ds(pl.multiple_of(x * nz, nz), nz)

    lanes = from_west.shape[1]
    total = from_west.shape[0] - nz * (ny // lanes)
    side_west = jnp.concatenate(
        [from_west[total + n * nz : total + (n + 1) * nz, :] for n in range(ny // lanes)], 1
    )

    def advance(step, carry):
        last = step == steps - 1
        base = step * chunk

        rows = pl.ds(pl.multiple_of((base + chunk + 1) * nz, nz), size)
        coming[:, :hy], coming[:, hy:] = north_back(get_lanes(half, rows))

        here = get_lanes(fluid, cells(base))
        before = get_lanes(fluid, cells(jnp.maximum(base - 1, 0)))
        before = jnp.where(step == 0, side_west, before)
        after_row = cells(jnp.minimum(base + chunk, nx - 1))
        after_fluid = get_lanes(fluid, after_row)
        after_flux = jnp.where(last, side_east[nz:, :], after_fluid * east[after_row, :])
        after_fluid = jnp.where(last, side_east[0:nz, :], after_fluid)

        p = press[nz : 2 * nz, :]
        first_flux = here * before * east[cells(base), :]
        p_before = press[0:nz, :] - jnp.where(step == 0, 1.0, 0.0).astype(F32) * first_flux
        east_done = first_flux - here * before * (p - p_before)
        for i in range(chunk):
            own = cells(base + i)
            line = pl.ds(base + i, 1)
            if i < chunk - 1:
                nxt = cells(base + i + 1)
                after = get_lanes(fluid, nxt)
                flux = after * east[nxt, :]
                p_next = press[(i + 2) * nz : (i + 3) * nz, :]
            else:
                after, flux = after_fluid, after_flux
                p_next = coming[0:nz, :] + jnp.where(last, 1.0, 0.0).astype(F32) * (here * flux)
            east_next_done = here * (flux - after * (p_next - p))
            north_done = here * north_roll(here, 1) * (north[own, :] - (p - north_roll(p, 1)))
            fluid_below = below_of(here, floor[line, :])
            up_done = here * fluid_below * (get_lanes(up, own) - (p - below_of(p, p_below[line, :])))
            done[0, own, :] = east_done
            done[1, own, :] = north_done
            done[2, own, :] = up_done
            done[3, own, :] = p
            done[4, own, :] = (
                (east_done - east_next_done)
                + (north_done - north_roll(north_done, -1))
                + (up_done - above_of(up_done, leaving[line, :]))
            )
            here, p, east_done = after, p_next, east_next_done
        press[0:nz, :] = press[size : size + nz, :]
        press[nz:, :] = coming[...]
        sent = pl.ds(pl.multiple_of(base * nz, size), size)
        for n, field in enumerate(fields):
            pltpu.make_async_copy(done.at[n, sent, :], field.at[sent, :], sems.at[n]).start()
        return carry

    lax.fori_loop(0, steps, advance, 0)
    for n, field in enumerate(fields):
        pltpu.make_async_copy(done.at[n], field, sems.at[n]).wait()


def local(groups, slabs, *fields):
    return project(groups, slabs, *fields)


def project(groups, slabs, east_velocity, north_velocity, upward_velocity, obstacle):
    nx, nz, ny = east_velocity.shape
    total = slabs * nz
    width = ny // slabs
    flat = [a.reshape(nx * nz, ny) for a in (obstacle, east_velocity, north_velocity, upward_velocity)]
    obs, east, north, up_in = flat

    even_np, odd_np, lam_b_np = north_tables(ny)
    block_np, lam_a_np = east_tables(nx)
    sine_np, mu_np = sine_table(total)
    tables = np.concatenate([*pair_np(even_np), *pair_np(odd_np), *pair_np(odd_np.T)], 0)
    east_table = np.stack([np.concatenate(pair_np(t), 1) for t in (block_np, block_np.T)])
    sines = np.concatenate(pair_np(sine_np), 0)
    sums = np.repeat(sines, 8, axis=1)
    east_values = np.stack([np.repeat(v[:, None], 128, 1) for v in (lam_a_np, block_np[:, 0])]).astype(np.float32)
    lam_b = np.repeat(lam_b_np[None], 8, 0).astype(np.float32)
    part = np.tile(lam_b_np.reshape(slabs, 1, width), (1, 8, 2)).astype(np.float32)

    def paired(column):
        return np.repeat(column.reshape(2, nx // 2).T, width, 1)

    pairs = np.concatenate(
        [paired(lam_a_np), paired(block_np[:, 0]), np.repeat(mu_np[:, None], 2 * width, 1)], 0
    ).astype(np.float32)

    chunk = 16
    lanes = ny // 128
    params = pltpu.CompilerParams(vmem_limit_bytes=VMEM_LIMIT)
    kept = pl.BlockSpec(memory_space=pltpu.VMEM)
    far = pl.BlockSpec(memory_space=pltpu.HBM)

    def array(*shape):
        return jax.ShapeDtypeStruct(shape, F32)

    blocked = array(lanes, nx * nz, 128)
    fluid, up, high, low, side, final = pl.pallas_call(
        functools.partial(load_kernel, nz),
        in_specs=[far] * 3,
        out_specs=[kept] * 6,
        out_shape=[blocked, blocked, array(nx, ny), array(2, nx, ny), array(2 * nz, ny), array(nz, ny)],
        scratch_shapes=[
            pltpu.VMEM((lanes, nx * nz, 128), jnp.int32),
            pltpu.VMEM((nz, ny), F32),
            pltpu.SemaphoreType.DMA((2 * lanes + 1,)),
        ],
        compiler_params=pltpu.CompilerParams(vmem_limit_bytes=LOAD_LIMIT),
        name="load",
    )(obs, up_in, east)

    rising = [(i, i + 1) for i in range(slabs - 1)]
    falling = [(i + 1, i) for i in range(slabs - 1)]
    low_above = lax.ppermute(low, "gz", falling)
    side_east = lax.ppermute(side, "xy", [((i + 1) % groups, i) for i in range(groups)])
    f_below = lax.ppermute(high, "gz", rising)

    cells = nx * nz * ny
    modes, weights, bottom, top, folded = pl.pallas_call(
        functools.partial(interior_kernel, nz, chunk),
        in_specs=[kept] * 8,
        out_specs=[kept] * 5,
        out_shape=[array(nz, nx, ny)] * 2 + [array(nx, ny)] * 2 + [array(2, nz, 8, ny)],
        scratch_shapes=[
            pltpu.VMEM((chunk * nz, ny), F32),
            pltpu.VMEM((chunk * nz, ny), F32),
            pltpu.VMEM((lanes, nx * nz, 128), F32),
        ],
        compiler_params=params,
        cost_estimate=pl.CostEstimate(flops=cells * 2 * 3 * (ny // 2 + nx), bytes_accessed=20 * cells, transcendentals=0),
        name="interior",
    )(fluid, up, east, north, tables, east_table, east_values, lam_b)
    ends_shape = array(slabs, nx + nz, 2 * width)
    crown, ends = pl.pallas_call(
        functools.partial(joined_kernel, nz, slabs),
        in_specs=[kept] * 12,
        out_specs=[kept] * 2,
        out_shape=[array(nx, ny), ends_shape],
        scratch_shapes=[
            pltpu.VMEM((nx, ny), F32),
            pltpu.VMEM((nx, ny), F32),
            pltpu.VMEM((2, nz, 8, ny), F32),
        ],
        compiler_params=params,
        name="joined",
    )(modes, weights, bottom, top, folded, high, low_above, final, side_east, tables, east_table, east_values)

    ends = lax.all_to_all(ends, "gz", split_axis=0, concat_axis=0, tiled=True)
    own, own_more = pl.pallas_call(
        functools.partial(ends_kernel, nz),
        in_specs=[kept] * 6,
        out_specs=[kept] * 2,
        out_shape=[array(total, 2 * width), array(total + nz * ny // (2 * width), 2 * width)],
        scratch_shapes=[pltpu.VMEM((total * 8, 2 * width), F32)],
        compiler_params=params,
        name="ends",
    )(ends, final, pairs, part, sums, sines)
    found = [own]
    for shift in range(1, groups):
        sent = own_more if shift == groups - 1 else own
        found.append(lax.ppermute(sent, "xy", [((i + shift) % groups, i) for i in range(groups)]))
    f_below, found[0] = lax.optimization_barrier((f_below, found[0]))
    solved = pl.pallas_call(
        functools.partial(correct_kernel, nz, groups),
        in_specs=[kept] * (groups + 4),
        out_specs=kept,
        out_shape=ends_shape,
        scratch_shapes=[pltpu.VMEM((total, 2 * width), F32)],
        compiler_params=params,
        name="correct",
    )(ends, *found, pairs, part, sines)
    solved = lax.all_to_all(solved, "gz", split_axis=0, concat_axis=0, tiled=True)

    outs = pl.pallas_call(
        functools.partial(backward_kernel, nz, slabs, BACK_ROWS),
        in_specs=[kept] * 17,
        out_specs=[far] * 5,
        out_shape=[array(nx * nz, ny)] * 5,
        scratch_shapes=[
            pltpu.VMEM((5, nx * nz, ny), F32),
            pltpu.SemaphoreType.DMA((5,)),
            pltpu.VMEM((nz, nx, ny), F32),
            pltpu.VMEM((nx, ny), F32),
            pltpu.VMEM((nx, ny), F32),
            pltpu.VMEM((2, nz, ny), F32),
            pltpu.VMEM((lanes, (nx + BACK_ROWS + 1) * nz, 128), F32),
            pltpu.VMEM(((BACK_ROWS + 1) * nz, ny), F32),
            pltpu.VMEM((BACK_ROWS * nz, ny), F32),
            pltpu.VMEM((nx, ny), F32),
            pltpu.VMEM((nx, ny), F32),
            pltpu.VMEM((nx, ny), F32),
        ],
        compiler_params=pltpu.CompilerParams(vmem_limit_bytes=BACK_LIMIT),
        name="backward",
    )(modes, weights, crown, solved, fluid, up, east, north, found[-1], side_east, f_below, high, low,
      low_above, tables, east_table, east_values)
    return tuple(o.reshape(nx, nz, ny) for o in outs)


def solution(mesh):
    placed = P("xy", "gz", None)
    return jax.shard_map(
        functools.partial(local, mesh.shape["xy"], mesh.shape["gz"]),
        mesh=mesh,
        in_specs=(placed,) * 4,
        out_specs=(placed,) * 5,
        check_vma=False,
    )
```

```python
import functools

import jax
import jax.numpy as jnp
import ml_dtypes
import numpy as np
from jax import lax
from jax.experimental import pallas as pl
from jax.experimental.pallas import tpu as pltpu
from jax.sharding import PartitionSpec as P


F32 = jnp.float32
BF16 = jnp.bfloat16
VMEM_LIMIT = 24 * 1024 * 1024
BACK_ROWS = 8
BACK_LIMIT = 28 * 1024 * 1024
LOAD_LIMIT = 46 * 1024 * 1024


def pair_np(table):
    high = table.astype(np.float32).astype(ml_dtypes.bfloat16)
    low = (table - high.astype(np.float64)).astype(np.float32).astype(ml_dtypes.bfloat16)
    return high, low


def north_tables(length):
    half = length // 2
    cell = np.arange(half)[:, None]
    mode = np.arange(half)[None, :]

    def cas(number):
        angle = 2.0 * np.pi * ((cell * number) % length) / length
        return (np.cos(angle) + np.sin(angle)) / np.sqrt(length)

    numbers = np.concatenate([2 * np.arange(half), 2 * np.arange(half) + 1])
    eigen = 4.0 * np.sin(np.pi * numbers / length) ** 2
    return cas(2 * mode), cas(2 * mode + 1), eigen


def east_tables(length):
    modes = np.concatenate([np.arange(0, length, 2), np.arange(1, length, 2)])
    cell = np.arange(length)
    table = np.cos(np.pi * modes[:, None] * (2 * cell[None, :] + 1) / (2 * length)) * np.sqrt(2.0 / length)
    table[0] = np.sqrt(1.0 / length)
    eigen = 4.0 * np.sin(np.pi * modes / (2 * length)) ** 2
    return table, eigen


def sine_table(length):
    index = np.arange(1, length + 1)
    table = np.sqrt(2.0 / (length + 1)) * np.sin(np.pi * np.outer(index, index) / (length + 1))
    eigen = 4.0 * np.sin(np.pi * index / (2 * (length + 1))) ** 2
    return table, eigen


def split(value):
    high = value.astype(BF16)
    return high, (value - high.astype(F32)).astype(BF16)


def dot3(left, right):
    (lh, ll), (rh, rl) = left, right
    dot = functools.partial(jnp.dot, preferred_element_type=F32)
    return dot(lh, rh) + (dot(ll, rh) + dot(lh, rl))


def chebyshev(shift, count):
    values = [jnp.ones_like(shift)]
    step = values[0]
    for n in range(count):
        step = step + shift * values[n]
        values.append(values[n] + step)
    return values


def slab_weights(shift, count):
    u = chebyshev(shift, count)
    return u[1:count] + [1.0 / u[count]]


def slab_solve(weights, right):
    count = len(right)
    u, inverse = weights[: count - 1], weights[count - 1]

    def times(n, value):
        return value if n == 0 else u[n - 1] * value

    lower = [right[0]]
    for k in range(1, count):
        lower.append(lower[-1] + times(k, right[k]))
    upper = [None] * count
    for k in range(count - 2, -1, -1):
        term = times(count - 2 - k, right[k + 1])
        upper[k] = term if upper[k + 1] is None else upper[k + 1] + term
    out = []
    for k in range(count):
        value = times(count - 1 - k, lower[k])
        if upper[k] is not None:
            value = value + times(k, upper[k])
        out.append(value * inverse)
    return out


def spike_of(shift, count):
    u = chebyshev(shift, count)
    inverse = 1.0 / u[count]
    return [u[count - 1 - k] * inverse for k in range(count)]


def interface_chain(couple, spread, bottoms, tops):
    count = len(bottoms)
    slope = jnp.zeros_like(couple)
    offset = jnp.zeros_like(couple)
    slopes, offsets, inverses, bases = [], [], [], []
    for s in range(count):
        inverse = 1.0 / (1.0 - couple * slope)
        base = (bottoms[s] + couple * offset) * inverse
        slopes.append(slope)
        offsets.append(offset)
        inverses.append(inverse * spread)
        bases.append(base)
        if s < count - 1:
            weight = spread * slope
            slope, offset = (
                couple + weight * spread * inverse,
                tops[s] + spread * offset + weight * base,
            )
    above = jnp.zeros_like(couple)
    lowers, uppers = [None] * count, [None] * count
    for s in range(count - 1, -1, -1):
        lower = bases[s] + inverses[s] * above
        uppers[s] = tops[s] + spread * (slopes[s] * lower + offsets[s]) + couple * above
        lowers[s] = lower
        above = lower
    below = [jnp.zeros_like(couple)] + uppers[:-1]
    above = lowers[1:] + [jnp.zeros_like(couple)]
    return below, above


def get_lanes(ref, rows):
    return jnp.concatenate([ref[n, rows, :] for n in range(ref.shape[0])], 1)


def put_lanes(ref, rows, value, start):
    for n in range(value.shape[1] // 128):
        ref[start + n, rows, :] = value[:, n * 128 : (n + 1) * 128]


def load_kernel(
    nz, obs, up_in, east, fluid, up, high, low, side, final, weights, raw, line, sems
):
    parts = raw.shape[0]
    rows = high.shape[0]
    copies = []
    for n in range(parts):
        lanes = slice(n * 128, (n + 1) * 128)
        copies.append(
            (
                pltpu.make_async_copy(obs.at[:, lanes], raw.at[n], sems.at[n]),
                pltpu.make_async_copy(up_in.at[:, lanes], up.at[n], sems.at[parts + n]),
            )
        )
        for copy in copies[-1]:
            copy.start()
    edge = pltpu.make_async_copy(east.at[0:nz, :], line, sems.at[2 * parts])
    edge.start()

    def eigen(axis, start, half, step):
        place = lax.broadcasted_iota(jnp.int32, (8, 128), axis) + start
        mode = jnp.where(place < half, 2 * place, 2 * (place - half) + 1)
        if axis == 1:
            mode = jnp.minimum(mode, 2 * half - mode)
        wave = jnp.sin(mode.astype(F32) * step)
        return 4.0 * wave * wave

    ny = parts * 128
    north_eigen = [eigen(1, lane, ny // 2, float(np.pi / ny)) for lane in range(0, ny, 128)]

    def coefficients(n, carry):
        at = pl.ds(pl.multiple_of(n * 8, 8), 8)
        east_eigen = eigen(0, n * 8, rows // 2, float(np.pi / (2 * rows)))
        for lane in range(0, ny, 128):
            lanes = slice(lane, lane + 128)
            values = slab_weights(east_eigen + north_eigen[lane // 128], nz)
            for k in range(nz):
                weights[k, at, lanes] = values[k]
        return carry

    lax.fori_loop(0, rows // 8, coefficients, 0)
    edge.wait()
    for n, (flags, speed) in enumerate(copies):
        lanes = slice(n * 128, (n + 1) * 128)
        flags.wait()
        fluid[n] = fluid_of(raw[n])
        high[:, lanes] = fluid[n, pl.ds(nz - 1, rows, stride=nz), :]
        bottom = fluid[n, pl.ds(0, rows, stride=nz), :]
        low[0, :, lanes] = bottom
        first = fluid[n, 0:nz, :]
        side[0:nz, lanes] = first
        side[nz : 2 * nz, lanes] = first * line[:, lanes]
        final[:, lanes] = fluid[n, (rows - 1) * nz : rows * nz, :]
        speed.wait()
        low[1, :, lanes] = bottom * up[n, pl.ds(0, rows, stride=nz), :]


def north_roll(value, shift):
    return pltpu.roll(value, shift % value.shape[1], 1)


def put_row(value, row, index):
    where = lax.broadcasted_iota(jnp.int32, value.shape, 0) == index
    return jnp.where(where, jnp.broadcast_to(row, value.shape), value)


def below_of(value, row):
    return put_row(pltpu.roll(value, 1, 0), row, 0)


def above_of(value, row):
    return put_row(pltpu.roll(value, value.shape[0] - 1, 0), row, value.shape[0] - 1)


def fluid_of(block):
    return (1 - block).astype(F32)


def east_left(table):
    return table, table[:, : table.shape[0]]


def north_pair(tables, index):
    size = tables.shape[1]
    return tables[2 * index * size : (2 * index + 1) * size, :], tables[(2 * index + 1) * size : (2 * index + 2) * size, :]


def east_dot(left, value):
    high, low = split(value)
    dot = functools.partial(jnp.dot, preferred_element_type=F32)
    return dot(left[0], jnp.concatenate([high, high], 0)) + dot(left[1], low)


def north_forward(value, even, odd):
    half = value.shape[1] // 2
    low, high = value[:, :half], value[:, half:]
    return dot3(split(low + high), even), dot3(split(low - high), odd)


def interior_kernel(
    nz, chunk, fluid, up, east, north, weights, tables, east_table, east_values,
    modes, bottom, top, sums,
    src, ready, half,
):
    ny = src.shape[1]
    nx = modes.shape[1]
    count = nx // chunk
    lift = jnp.where(lax.axis_index("gz") == 0, 1.0, 0.0).astype(F32)
    floor = jnp.broadcast_to(lift, (1, ny))
    none = jnp.zeros((1, ny), F32)

    def cells(x):
        return pl.ds(pl.multiple_of(x * nz, nz), nz)

    def stencil(step):
        base = step * chunk
        inside = jnp.where(step > 0, 1.0, 0.0).astype(F32)
        more = jnp.where(step < count - 1, 1.0, 0.0).astype(F32)
        here = get_lanes(fluid, cells(base))
        before = get_lanes(fluid, cells(jnp.maximum(base - 1, 0)))
        masked = here * (before * inside) * east[cells(base), :]
        for i in range(chunk):
            own = cells(base + i)
            nxt = cells(base + i + 1) if i < chunk - 1 else cells(jnp.minimum(base + chunk, nx - 1))
            after = get_lanes(fluid, nxt)
            flux = after * east[nxt, :]
            if i == chunk - 1:
                flux = flux * more
            masked_next = here * flux
            north_masked = here * north_roll(here, 1) * north[own, :]
            up_masked = here * below_of(here, floor) * get_lanes(up, own)
            src[i * nz : (i + 1) * nz, :] = (
                (masked - masked_next)
                + (north_masked - north_roll(north_masked, -1))
                + (up_masked - above_of(up_masked, none))
            )
            here, masked = after, masked_next

    def transform(step):
        rows = pl.ds(pl.multiple_of(step * chunk * nz, chunk * nz), chunk * nz)
        even, odd = north_forward(ready[...], north_pair(tables, 0), north_pair(tables, 1))
        put_lanes(half, rows, even, 0)
        put_lanes(half, rows, odd, ny // 256)

    ready[...] = jnp.zeros_like(ready)

    def body(step, carry):
        transform(jnp.maximum(step - 1, 0))
        stencil(step)
        ready[...] = src[...]
        return carry

    lax.fori_loop(0, count, body, 0)
    transform(count - 1)
    left = east_left(east_table[0])
    for k in range(nz):
        modes[k] = east_dot(left, get_lanes(half, pl.ds(k, nx, stride=nz)))

    sums[...] = jnp.zeros_like(sums)
    blocks = nx // 8

    def solve(n, carry):
        at = pl.ds(pl.multiple_of(n * 8, 8), 8)
        parity = n // (blocks // 2)
        for lane in range(0, ny, 128):
            lanes = slice(lane, lane + 128)
            values = [weights[k, at, lanes] for k in range(nz)]
            local = slab_solve(values, [modes[k, at, lanes] for k in range(nz)])
            bottom[at, lanes] = local[0]
            top[at, lanes] = local[nz - 1]
            weight = east_values[1, at, :]
            for k in range(nz):
                sums[parity, k, :, lanes] += weight * local[k]
        return carry

    lax.fori_loop(0, blocks, solve, 0)


def joined_kernel(
    nz, slabs,
    modes, weights, bottom_in, top_in, sums_in, high, low_above, final, side_east,
    tables, east_table, east_values,
    crown, out,
    bottom, top, sums,
):
    nx, ny = high.shape
    leaving = final[...] * side_east[nz:, :]
    stacked = jnp.concatenate([high[...] * low_above[1], leaving], 0)
    stacked = jnp.concatenate(north_forward(stacked, north_pair(tables, 0), north_pair(tables, 1)), 1)
    top[...] = east_dot(east_left(east_table[0]), stacked[:nx])
    leaving = stacked[nx:]
    sums[...] = sums_in[...]
    blocks = nx // 8

    def share(n, carry):
        at = pl.ds(pl.multiple_of(n * 8, 8), 8)
        parity = n // (blocks // 2)
        for lane in range(0, ny, 128):
            lanes = slice(lane, lane + 128)
            rising = top[at, lanes]
            scaled = rising * weights[nz - 1, at, lanes]
            crown[at, lanes] = modes[nz - 1, at, lanes] - rising
            bottom[at, lanes] = bottom_in[at, lanes] - scaled
            top[at, lanes] = top_in[at, lanes] - weights[nz - 2, at, lanes] * scaled + rising
            scaled = east_values[1, at, :] * scaled
            sums[parity, 0, :, lanes] -= scaled
            for k in range(1, nz):
                sums[parity, k, :, lanes] -= weights[k - 1, at, lanes] * scaled
        return carry

    lax.fori_loop(0, blocks, share, 0)
    even = [jnp.sum(sums[0, k], axis=0, keepdims=True) for k in range(nz)]
    odd = [jnp.sum(sums[1, k], axis=0, keepdims=True) for k in range(nz)]
    west = jnp.concatenate([e + o for e, o in zip(even, odd)], 0)
    east_end = jnp.concatenate([e - o for e, o in zip(even, odd)], 0) + leaving
    width = ny // slabs
    hx = nx // 2
    for j in range(slabs):
        lanes = slice(j * width, (j + 1) * width)
        out[j, 0:hx, :] = jnp.concatenate([bottom[:hx, lanes], bottom[hx:, lanes]], 1)
        out[j, hx:nx, :] = jnp.concatenate([top[:hx, lanes], top[hx:, lanes]], 1)
        out[j, nx : nx + nz, :] = jnp.concatenate([west[:, lanes], east_end[:, lanes]], 1)


def swap_halves(value):
    width = value.shape[1] // 2
    return jnp.concatenate([value[:, width:], value[:, :width]], 1)


def in_first_half(value):
    return lax.broadcasted_iota(jnp.int32, value.shape, 1) < value.shape[1] // 2


def ends_kernel(nz, ends, final, pairs, lam_b, sums, sines, out, out_more, acc):
    slabs = ends.shape[0]
    nx = ends.shape[1] - nz
    hx = nx // 2
    total = slabs * nz
    shift = pairs[0:hx, :] + lam_b[lax.axis_index("gz")][0:1, :]
    spike = spike_of(shift, nz)
    below, above = interface_chain(
        spike[0],
        spike[nz - 1],
        [ends[s, 0:hx, :] for s in range(slabs)],
        [ends[s, hx:nx, :] for s in range(slabs)],
    )
    weight = pairs[hx:nx, :]
    spike = [weight * g for g in spike]
    for s in range(slabs):
        for k in range(nz):
            term = spike[k] * below[s] + spike[nz - 1 - k] * above[s]
            row = (s * nz + k) * 8
            acc[row : row + 8, :] = jnp.sum(term.reshape(hx // 8, 8, term.shape[1]), axis=0)
    both = dot3((sums[:total, :], sums[total:, :]), split(acc[...]))
    other = swap_halves(both)
    both = jnp.where(in_first_half(both), both + other, other - both)
    rows = jnp.concatenate([ends[s, nx : nx + nz, :] for s in range(slabs)], 0)
    both = both + dot3((sines[:total, :], sines[total:, :]), split(rows))
    out[...] = both
    out_more[:total, :] = both
    lanes = both.shape[1]
    for n in range(final.shape[1] // lanes):
        out_more[total + n * nz : total + (n + 1) * nz, :] = final[:, n * lanes : (n + 1) * lanes]


def power(value, count):
    result = None
    while count:
        if count & 1:
            result = value if result is None else result * value
        count >>= 1
        if count:
            value = value * value
    return result


def correct_kernel(nz, groups, ends, *rest):
    found = rest[:groups]
    pairs, lam_b, sines, out, jump = rest[groups:]
    slabs, width = ends.shape[0], ends.shape[2] // 2
    nx = ends.shape[1] - nz
    hx = nx // 2
    total = slabs * nz
    row_b = lam_b[lax.axis_index("gz")][0:1, :]
    shift = pairs[nx:, :width] + row_b[:, :width]
    cosh = 1.0 + 0.5 * shift
    sinh = jnp.sqrt(shift + 0.25 * shift * shift)
    grow = cosh + sinh
    decay = 1.0 / grow
    far = power(decay, nx)
    far2 = far * far
    scale = 1.0 / (sinh * (1.0 - far2))
    self2 = ((1.0 + far2) + (decay + far2 * grow)) * scale
    cross2 = 2.0 * (1.0 + cosh) * far * scale
    inverse = {}
    for f in range(groups):
        key = min(f, groups - f)
        if key not in inverse:
            inverse[key] = 1.0 / (1.0 + self2 - float(np.cos(2 * np.pi * f / groups)) * cross2)
    kernel = {}
    for n in range(groups // 2 + 1):
        value = None
        for f in range(groups):
            factor = float(np.cos(2 * np.pi * f * n / groups)) / groups
            term = factor * inverse[min(f, groups - f)]
            value = term if value is None else value + term
        kernel[n] = value
    jumps_east, jumps_west = None, None
    for n in range(groups):
        nxt = (n + 1) % groups
        t = found[n][:total, width:] - found[nxt][:total, :width]
        east_term = kernel[min(n, groups - n)] * t
        west_term = kernel[min(nxt, groups - nxt)] * t
        jumps_east = east_term if jumps_east is None else jumps_east + east_term
        jumps_west = west_term if jumps_west is None else jumps_west + west_term
    both = dot3((sines[:total, :], sines[total:, :]), split(jnp.concatenate([jumps_west, jumps_east], 1)))
    other = swap_halves(both)
    jump[...] = jnp.where(in_first_half(both), both - other, both + other)
    shift = pairs[0:hx, :] + row_b
    spike = spike_of(shift, nz)
    weight = pairs[hx:nx, :]
    loads = [weight * g for g in spike]
    bottoms, tops = [], []
    for s in range(slabs):
        low, high = ends[s, 0:hx, :], ends[s, hx:nx, :]
        for k in range(nz):
            q = jump[s * nz + k : s * nz + k + 1, :]
            low = low + loads[k] * q
            high = high + loads[nz - 1 - k] * q
        bottoms.append(low)
        tops.append(high)
    below, above = interface_chain(spike[0], spike[nz - 1], bottoms, tops)
    for s in range(slabs):
        out[s, 0:hx, :] = below[s]
        out[s, hx:nx, :] = above[s]
        out[s, nx : nx + nz, :] = both[s * nz : (s + 1) * nz, :]


def backward_kernel(
    nz, slabs, chunk,
    modes, weights, crown, solved,
    fluid, up, east, north,
    from_west, side_east, f_below, high, low, low_above,
    tables, east_table, east_values,
    far_east, far_north, far_up, far_p, far_r,
    done, sems, work, below, above, found, half, press, coming, p_below, floor, leaving,
):
    ny = east.shape[1]
    hy = ny // 2
    nx = modes.shape[1]
    steps = nx // chunk
    size = chunk * nz
    fields = (far_east, far_north, far_up, far_p, far_r)
    lift = jnp.where(lax.axis_index("gz") == 0, 1.0, 0.0).astype(F32)

    def north_back(value):
        even = dot3(split(value[:, :hy]), north_pair(tables, 0))
        odd = dot3(split(value[:, hy:]), north_pair(tables, 2))
        return even + odd, even - odd

    width = ny // slabs
    west, east_end = [], []
    hx = nx // 2
    for j in range(slabs):
        lanes = slice(j * width, (j + 1) * width)
        below[:hx, lanes] = solved[j, 0:hx, :width]
        below[hx:, lanes] = solved[j, 0:hx, width:]
        above[:hx, lanes] = solved[j, hx:nx, :width]
        above[hx:, lanes] = solved[j, hx:nx, width:]
        west.append(solved[j, nx : nx + nz, :width])
        east_end.append(solved[j, nx : nx + nz, width:])
    west = jnp.concatenate(west, 1)
    east_end = jnp.concatenate(east_end, 1)
    found[0] = west - east_end
    found[1] = west + east_end
    blocks = nx // 8

    def solve(n, carry):
        at = pl.ds(pl.multiple_of(n * 8, 8), 8)
        parity = n // (blocks // 2)
        for lane in range(0, ny, 128):
            lanes = slice(lane, lane + 128)
            weight = east_values[1, at, :]
            right = []
            for k in range(nz):
                q = jnp.broadcast_to(found[parity, pl.ds(k, 1), lanes], weight.shape)
                plane = modes[k, at, lanes] if k < nz - 1 else crown[at, lanes]
                right.append(plane + weight * q)
            right[0] = right[0] + below[at, lanes]
            right[nz - 1] = right[nz - 1] + above[at, lanes]
            local = slab_solve([weights[k, at, lanes] for k in range(nz)], right)
            for k in range(nz):
                work[k, at, lanes] = local[k]
        return carry

    lax.fori_loop(0, blocks, solve, 0)
    left = east_left(east_table[1])
    crest = None
    for k in range(nz):
        crest = east_dot(left, work[k])
        put_lanes(half, pl.ds(nz + k, nx, stride=nz), crest, 0)
    first, final = slice(nz, 2 * nz), slice(nx * nz, (nx + 1) * nz)
    put_lanes(half, slice(0, nz), get_lanes(half, first) + west, 0)
    put_lanes(half, slice((nx + 1) * nz, (nx + 2) * nz), get_lanes(half, final) - east_end, 0)
    both = jnp.concatenate(
        [east_dot(left, below[...]), east_dot(left, above[...]) - crest, get_lanes(half, slice(0, size + nz))], 0
    )
    both = jnp.concatenate(north_back(both), 1)
    p_below[...] = both[:nx] - f_below[...] * low[1]
    floor[...] = f_below[...] + lift
    leaving[...] = high[...] * (low_above[1] - low_above[0] * both[nx : 2 * nx])
    press[...] = both[2 * nx :]


    def cells(x):
        return pl.ds(pl.multiple_of(x * nz, nz), nz)

    lanes = from_west.shape[1]
    total = from_west.shape[0] - nz * (ny // lanes)
    side_west = jnp.concatenate(
        [from_west[total + n * nz : total + (n + 1) * nz, :] for n in range(ny // lanes)], 1
    )

    def advance(step, carry):
        last = step == steps - 1
        base = step * chunk

        rows = pl.ds(pl.multiple_of((base + chunk + 1) * nz, nz), size)
        coming[:, :hy], coming[:, hy:] = north_back(get_lanes(half, rows))

        here = get_lanes(fluid, cells(base))
        before = get_lanes(fluid, cells(jnp.maximum(base - 1, 0)))
        before = jnp.where(step == 0, side_west, before)
        after_row = cells(jnp.minimum(base + chunk, nx - 1))
        after_fluid = get_lanes(fluid, after_row)
        after_flux = jnp.where(last, side_east[nz:, :], after_fluid * east[after_row, :])
        after_fluid = jnp.where(last, side_east[0:nz, :], after_fluid)

        p = press[nz : 2 * nz, :]
        first_flux = here * before * east[cells(base), :]
        p_before = press[0:nz, :] - jnp.where(step == 0, 1.0, 0.0).astype(F32) * first_flux
        east_done = first_flux - here * before * (p - p_before)
        for i in range(chunk):
            own = cells(base + i)
            line = pl.ds(base + i, 1)
            if i < chunk - 1:
                nxt = cells(base + i + 1)
                after = get_lanes(fluid, nxt)
                flux = after * east[nxt, :]
                p_next = press[(i + 2) * nz : (i + 3) * nz, :]
            else:
                after, flux = after_fluid, after_flux
                p_next = coming[0:nz, :] + jnp.where(last, 1.0, 0.0).astype(F32) * (here * flux)
            east_next_done = here * (flux - after * (p_next - p))
            north_done = here * north_roll(here, 1) * (north[own, :] - (p - north_roll(p, 1)))
            fluid_below = below_of(here, floor[line, :])
            up_done = here * fluid_below * (get_lanes(up, own) - (p - below_of(p, p_below[line, :])))
            done[0, own, :] = east_done
            done[1, own, :] = north_done
            done[2, own, :] = up_done
            done[3, own, :] = p
            done[4, own, :] = (
                (east_done - east_next_done)
                + (north_done - north_roll(north_done, -1))
                + (up_done - above_of(up_done, leaving[line, :]))
            )
            here, p, east_done = after, p_next, east_next_done
        press[0:nz, :] = press[size : size + nz, :]
        press[nz:, :] = coming[...]
        sent = pl.ds(pl.multiple_of(base * nz, size), size)
        for n, field in enumerate(fields):
            pltpu.make_async_copy(done.at[n, sent, :], field.at[sent, :], sems.at[n]).start()
        return carry

    lax.fori_loop(0, steps, advance, 0)
    for n, field in enumerate(fields):
        pltpu.make_async_copy(done.at[n], field, sems.at[n]).wait()


def local(groups, slabs, *fields):
    return project(groups, slabs, *fields)


def project(groups, slabs, east_velocity, north_velocity, upward_velocity, obstacle):
    nx, nz, ny = east_velocity.shape
    total = slabs * nz
    width = ny // slabs
    flat = [a.reshape(nx * nz, ny) for a in (obstacle, east_velocity, north_velocity, upward_velocity)]
    obs, east, north, up_in = flat

    even_np, odd_np, lam_b_np = north_tables(ny)
    block_np, lam_a_np = east_tables(nx)
    sine_np, mu_np = sine_table(total)
    tables = np.concatenate([*pair_np(even_np), *pair_np(odd_np), *pair_np(odd_np.T)], 0)
    east_table = np.stack([np.concatenate(pair_np(t), 1) for t in (block_np, block_np.T)])
    sines = np.concatenate(pair_np(sine_np), 0)
    sums = np.repeat(sines, 8, axis=1)
    east_values = np.stack([np.repeat(v[:, None], 128, 1) for v in (lam_a_np, block_np[:, 0])]).astype(np.float32)
    part = np.tile(lam_b_np.reshape(slabs, 1, width), (1, 8, 2)).astype(np.float32)

    def paired(column):
        return np.repeat(column.reshape(2, nx // 2).T, width, 1)

    pairs = np.concatenate(
        [paired(lam_a_np), paired(block_np[:, 0]), np.repeat(mu_np[:, None], 2 * width, 1)], 0
    ).astype(np.float32)

    chunk = 16
    lanes = ny // 128
    params = pltpu.CompilerParams(vmem_limit_bytes=VMEM_LIMIT)
    kept = pl.BlockSpec(memory_space=pltpu.VMEM)
    far = pl.BlockSpec(memory_space=pltpu.HBM)

    def array(*shape):
        return jax.ShapeDtypeStruct(shape, F32)

    blocked = array(lanes, nx * nz, 128)
    fluid, up, high, low, side, final, weights = pl.pallas_call(
        functools.partial(load_kernel, nz),
        in_specs=[far] * 3,
        out_specs=[kept] * 7,
        out_shape=[blocked, blocked, array(nx, ny), array(2, nx, ny), array(2 * nz, ny), array(nz, ny), array(nz, nx, ny)],
        scratch_shapes=[
            pltpu.VMEM((lanes, nx * nz, 128), jnp.int32),
            pltpu.VMEM((nz, ny), F32),
            pltpu.SemaphoreType.DMA((2 * lanes + 1,)),
        ],
        compiler_params=pltpu.CompilerParams(vmem_limit_bytes=LOAD_LIMIT),
        name="load",
    )(obs, up_in, east)

    rising = [(i, i + 1) for i in range(slabs - 1)]
    falling = [(i + 1, i) for i in range(slabs - 1)]
    low_above = lax.ppermute(low, "gz", falling)
    side_east = lax.ppermute(side, "xy", [((i + 1) % groups, i) for i in range(groups)])
    f_below = lax.ppermute(high, "gz", rising)

    cells = nx * nz * ny
    modes, bottom, top, folded = pl.pallas_call(
        functools.partial(interior_kernel, nz, chunk),
        in_specs=[kept] * 8,
        out_specs=[kept] * 4,
        out_shape=[array(nz, nx, ny)] + [array(nx, ny)] * 2 + [array(2, nz, 8, ny)],
        scratch_shapes=[
            pltpu.VMEM((chunk * nz, ny), F32),
            pltpu.VMEM((chunk * nz, ny), F32),
            pltpu.VMEM((lanes, nx * nz, 128), F32),
        ],
        compiler_params=params,
        cost_estimate=pl.CostEstimate(flops=cells * 2 * 3 * (ny // 2 + nx), bytes_accessed=20 * cells, transcendentals=0),
        name="interior",
    )(fluid, up, east, north, weights, tables, east_table, east_values)
    ends_shape = array(slabs, nx + nz, 2 * width)
    crown, ends = pl.pallas_call(
        functools.partial(joined_kernel, nz, slabs),
        in_specs=[kept] * 12,
        out_specs=[kept] * 2,
        out_shape=[array(nx, ny), ends_shape],
        scratch_shapes=[
            pltpu.VMEM((nx, ny), F32),
            pltpu.VMEM((nx, ny), F32),
            pltpu.VMEM((2, nz, 8, ny), F32),
        ],
        compiler_params=params,
        name="joined",
    )(modes, weights, bottom, top, folded, high, low_above, final, side_east, tables, east_table, east_values)

    ends = lax.all_to_all(ends, "gz", split_axis=0, concat_axis=0, tiled=True)
    own, own_more = pl.pallas_call(
        functools.partial(ends_kernel, nz),
        in_specs=[kept] * 6,
        out_specs=[kept] * 2,
        out_shape=[array(total, 2 * width), array(total + nz * ny // (2 * width), 2 * width)],
        scratch_shapes=[pltpu.VMEM((total * 8, 2 * width), F32)],
        compiler_params=params,
        name="ends",
    )(ends, final, pairs, part, sums, sines)
    found = [own]
    for shift in range(1, groups):
        sent = own_more if shift == groups - 1 else own
        found.append(lax.ppermute(sent, "xy", [((i + shift) % groups, i) for i in range(groups)]))
    f_below, found[0] = lax.optimization_barrier((f_below, found[0]))
    solved = pl.pallas_call(
        functools.partial(correct_kernel, nz, groups),
        in_specs=[kept] * (groups + 4),
        out_specs=kept,
        out_shape=ends_shape,
        scratch_shapes=[pltpu.VMEM((total, 2 * width), F32)],
        compiler_params=params,
        name="correct",
    )(ends, *found, pairs, part, sines)
    solved = lax.all_to_all(solved, "gz", split_axis=0, concat_axis=0, tiled=True)

    outs = pl.pallas_call(
        functools.partial(backward_kernel, nz, slabs, BACK_ROWS),
        in_specs=[kept] * 17,
        out_specs=[far] * 5,
        out_shape=[array(nx * nz, ny)] * 5,
        scratch_shapes=[
            pltpu.VMEM((5, nx * nz, ny), F32),
            pltpu.SemaphoreType.DMA((5,)),
            pltpu.VMEM((nz, nx, ny), F32),
            pltpu.VMEM((nx, ny), F32),
            pltpu.VMEM((nx, ny), F32),
            pltpu.VMEM((2, nz, ny), F32),
            pltpu.VMEM((lanes, (nx + BACK_ROWS + 1) * nz, 128), F32),
            pltpu.VMEM(((BACK_ROWS + 1) * nz, ny), F32),
            pltpu.VMEM((BACK_ROWS * nz, ny), F32),
            pltpu.VMEM((nx, ny), F32),
            pltpu.VMEM((nx, ny), F32),
            pltpu.VMEM((nx, ny), F32),
        ],
        compiler_params=pltpu.CompilerParams(vmem_limit_bytes=BACK_LIMIT),
        name="backward",
    )(modes, weights, crown, solved, fluid, up, east, north, found[-1], side_east, f_below, high, low,
      low_above, tables, east_table, east_values)
    return tuple(o.reshape(nx, nz, ny) for o in outs)


def solution(mesh):
    placed = P("xy", "gz", None)
    return jax.shard_map(
        functools.partial(local, mesh.shape["xy"], mesh.shape["gz"]),
        mesh=mesh,
        in_specs=(placed,) * 4,
        out_specs=(placed,) * 5,
        check_vma=False,
    )
```
